32 devices in a mesh: dp: 16 (over z, y, core), tensor: 2 (over x).
Axes of the slice: x: 2, y: 2, z: 4, core: 2. Of those that a mesh axis runs over, the one named last changes fastest.
Arguments:
- tokens: bfloat16 [32, 1024, 1024], P('dp'), may hold values from -6 to 6
- d_output: bfloat16 [32, 1024, 1024], P('dp'), may hold values from -6 to 6
- lengths: int32 [32], P('dp'), may hold values from 256 to 1024, as said below
- ln1_gain: bfloat16 [1024], replicated, may hold values from 0.5 to 1.5
- ln1_bias: bfloat16 [1024], replicated, may hold values from -4 to 4
- w_qkv: bfloat16 [1024, 3, 1024], P(None, None, 'tensor'), may hold values from -0.1875 to 0.1875
- qv_bias: bfloat16 [2, 1024], P(None, 'tensor'), may hold values from -4 to 4
- w_out: bfloat16 [1024, 1024], P('tensor'), may hold values from -0.75 to 0.75
- bias_out: bfloat16 [1024], replicated, may hold values from -4 to 4
- ln2_gain: bfloat16 [1024], replicated, may hold values from 0.5 to 1.5
- ln2_bias: bfloat16 [1024], replicated, may hold values from -4 to 4
- w_up: bfloat16 [1024, 4096], P(None, 'tensor'), may hold values from -0.1875 to 0.1875
- b_up: bfloat16 [4096], P('tensor'), may hold values from -6 to 6
- w_down: bfloat16 [4096, 1024], P('tensor'), may hold values from -0.09375 to 0.09375
- b_down: bfloat16 [1024], replicated, may hold values from -4 to 4
Outputs:
- output: bfloat16 [32, 1024, 1024], P('dp', 'tensor')
- grad_tokens: bfloat16 [32, 1024, 1024], P('dp', 'tensor')
- grad_ln1_gain: float32 [1024], replicated
- grad_ln1_bias: float32 [1024], replicated
- grad_w_qkv: float32 [1024, 3, 1024], P(None, None, 'tensor')
- grad_qv_bias: float32 [2, 1024], P(None, 'tensor')
- grad_w_out: float32 [1024, 1024], P('tensor')
- grad_bias_out: float32 [1024], replicated
- grad_ln2_gain: float32 [1024], replicated
- grad_ln2_bias: float32 [1024], replicated
- grad_w_up: float32 [1024, 4096], P(None, 'tensor')
- grad_b_up: float32 [4096], P('tensor')
- grad_w_down: float32 [4096, 1024], P('tensor')
- grad_b_down: float32 [1024], replicated
The draws below stay inside these ranges and needn't reach their ends.
Inputs may be any that keep to these rules, and one draw needn't show every extreme that they name: A sequence's valid slots are its first lengths[b]; at least one sequence has all 1024 slots valid.
All inputs are finite; a program needn't handle non-finite values.
Results may differ from the reference program's by a relative error of at most 0.02.
Values may be sent and summed in bfloat16 or wider, within the bound.
A program may use at most 384 MiB of HBM per device.

```python
import math
import jax
import jax.numpy as jnp
from jax import lax

D = 1024
HEADS = 16
HEAD_DIM = 64
FF = 4096
SEQ = 1024
SEQS = 32


def draw_lengths(key, part):
    drawn = jax.random.randint(key, (SEQS,), SEQ // 4, SEQ + 1)
    chosen = jax.random.randint(jax.random.fold_in(key, 7), (), 0, SEQS)
    return jnp.where(jnp.arange(SEQS) == chosen, SEQ, drawn).astype(jnp.int32)


def level_of(own_key, dims, cuts, least, largest):
    factor_of = 1.0
    for position, parts in cuts:
        draws = jax.random.uniform(jax.random.fold_in(jax.random.fold_in(own_key, 6), position), (parts,), jnp.float32, least / len(cuts), largest / len(cuts))
        factor_of = factor_of * jnp.repeat(jnp.exp(draws), dims[position] // parts).reshape((-1,) + (1,) * (len(dims) - 1 - position))
    return factor_of


def centred(stream_key, dims, spread, bound, cuts=(), held_as=jnp.bfloat16):
    values = spread * jax.random.normal(stream_key, dims, jnp.float32)
    if cuts:
        values = values * level_of(stream_key, dims, cuts, -0.22, 0.18)
    return jnp.clip(values, -bound, bound).astype(held_as)


def setup_inputs(seed: int = 0) -> dict:
    key_list = jax.random.split(jax.random.key(seed), 16)
    tokens = centred(key_list[0], (SEQS, SEQ, D), 1.0, 6.0, ((0, 16),))
    d_output = centred(key_list[1], (SEQS, SEQ, D), 1.0, 6.0, ((0, 16),))
    lengths = draw_lengths(jax.random.fold_in(key_list[15], 71), 0)
    ln1_gain = jnp.clip(1.0 + 0.1 * jax.random.normal(key_list[3], (D,), jnp.float32), 0.5, 1.5).astype(jnp.bfloat16)
    ln1_bias = centred(key_list[4], (D,), 0.3, 4.0)
    w_qkv = centred(key_list[5], (D, 3, D), D ** -0.5, 0.1875, ((2, 2),))
    qv_bias = centred(key_list[6], (2, D), 0.3, 4.0, ((1, 2),))
    w_out = centred(key_list[7], (D, D), (D // 16) ** -0.5, 0.75, ((0, 2),))
    bias_out = centred(key_list[8], (D,), 0.3, 4.0)
    ln2_gain = jnp.clip(1.0 + 0.1 * jax.random.normal(key_list[9], (D,), jnp.float32), 0.5, 1.5).astype(jnp.bfloat16)
    ln2_bias = centred(key_list[10], (D,), 0.3, 4.0)
    w_up = centred(key_list[11], (D, FF), D ** -0.5, 0.1875, ((1, 2),))
    b_up = centred(key_list[12], (FF,), 0.5, 6.0, ((0, 2),))
    w_down = centred(key_list[13], (FF, D), FF ** -0.5, 0.09375, ((0, 2),))
    b_down = centred(key_list[14], (D,), 0.3, 4.0)
    return {"tokens": tokens, "d_output": d_output, "lengths": lengths, "ln1_gain": ln1_gain, "ln1_bias": ln1_bias, "w_qkv": w_qkv, "qv_bias": qv_bias, "w_out": w_out, "bias_out": bias_out, "ln2_gain": ln2_gain, "ln2_bias": ln2_bias, "w_up": w_up, "b_up": b_up, "w_down": w_down, "b_down": b_down}


@jax.custom_vjp
def low(v):
    return lax.optimization_barrier(v.astype(jnp.bfloat16)).astype(jnp.float32)

@jax.custom_vjp
def low_back(v):
    return v

def low_keep(v):
    return (low(v), None)

def low_pass(kept, grad):
    return (grad,)

def back_keep(v):
    return (v, None)

def back_low(kept, grad):
    return (low(grad),)
low.defvjp(low_keep, low_pass)
low_back.defvjp(back_keep, back_low)

def layer_norm(values, gain, shift):
    centre = lax.optimization_barrier(jnp.mean(values, -1, keepdims=True))
    shifted = values - centre
    variance = lax.optimization_barrier(jnp.mean(shifted * shifted, -1, keepdims=True))
    return shifted * lax.rsqrt(variance + 1e-05) * gain + shift

def split_heads(values):
    return values.reshape(SEQ, HEADS, HEAD_DIM).transpose(1, 0, 2)

def sequence_forward(params, tokens_f, length):
    ln1_gain, ln1_bias, w_qkv, qv_bias, w_out, bias_out, ln2_gain, ln2_bias, w_up, b_up, w_down, b_down = params
    precise = lax.Precision.HIGHEST
    normed1 = low(layer_norm(tokens_f, ln1_gain, ln1_bias))
    query = low_back(low(jnp.dot(normed1, w_qkv[:, 0, :], precision=precise) + qv_bias[0]))
    keys = low_back(low(jnp.dot(normed1, w_qkv[:, 1, :], precision=precise)))
    values = low_back(low(jnp.dot(normed1, w_qkv[:, 2, :], precision=precise) + qv_bias[1]))
    positions = jnp.arange(SEQ, dtype=jnp.int32)
    distance = positions[:, None] - positions[None, :]
    slopes = jnp.exp2(-8.0 * (jnp.arange(HEADS, dtype=jnp.int32).astype(jnp.float32) + 1.0) / HEADS)
    scale = 1.0 / math.sqrt(HEAD_DIM)
    products = jnp.einsum('hid,hjd->hij', split_heads(query), split_heads(keys), precision=precise)
    scores = low_back(products * scale - slopes[:, None, None] * distance.astype(jnp.float32)[None])
    allowed = (distance >= 0) & (positions[None, :] < length)
    probs = jax.nn.softmax(jnp.where(allowed[None], scores, -1e+30), axis=-1)
    mixed = jnp.einsum('hij,hjd->hid', low(probs), split_heads(values), precision=precise)
    attn = low_back(low(mixed.transpose(1, 0, 2).reshape(SEQ, D)))
    branch_one = low_back(jnp.dot(attn, w_out, precision=precise) + bias_out)
    hidden_state = tokens_f + branch_one
    normed2 = low(layer_norm(hidden_state, ln2_gain, ln2_bias))
    pre = low_back(jnp.dot(normed2, w_up, precision=precise) + b_up)
    act = low(jax.nn.gelu(pre, approximate=True))
    branch_two = low_back(jnp.dot(act, w_down, precision=precise) + b_down)
    return hidden_state + branch_two

def reference(tokens, d_output, lengths, ln1_gain, ln1_bias, w_qkv, qv_bias, w_out, bias_out, ln2_gain, ln2_bias, w_up, b_up, w_down, b_down):
    params = tuple((item.astype(jnp.float32) for item in (ln1_gain, ln1_bias, w_qkv, qv_bias, w_out, bias_out, ln2_gain, ln2_bias, w_up, b_up, w_down, b_down)))
    group = 2 if SEQS % 2 == 0 else 1
    steps_count = SEQS // group
    tokens_f = tokens.astype(jnp.float32).reshape(steps_count, group, SEQ, D)
    grads_f = d_output.astype(jnp.float32).reshape(steps_count, group, SEQ, D)
    lengths_g = lengths.reshape(steps_count, group)
    positions = jnp.arange(SEQ, dtype=jnp.int32)

    def step(totals, batch):
        tokens_b, grads_b, lengths_b = batch

        def forward(params_in, tokens_in):
            return jax.vmap(sequence_forward, in_axes=(None, 0, 0))(params_in, tokens_in, lengths_b)
        result, pull = jax.vjp(forward, params, tokens_b)
        valid = (positions[None, :] < lengths_b[:, None]).astype(jnp.float32)
        grad_params, grad_input = pull(grads_b * valid[:, :, None])
        totals = jax.tree.map(jnp.add, totals, grad_params)
        return (totals, (result.astype(jnp.bfloat16), grad_input.astype(jnp.bfloat16)))
    initial = jax.tree.map(jnp.zeros_like, params)
    totals, (outputs, grad_inputs) = lax.scan(step, initial, (tokens_f, grads_f, lengths_g))
    return (outputs.reshape(SEQS, SEQ, D), grad_inputs.reshape(SEQS, SEQ, D), totals[0], totals[1], totals[2], totals[3], totals[4], totals[5], totals[6], totals[7], totals[8], totals[9], totals[10], totals[11])
```

```python
import math

import jax
import jax.numpy as jnp
import numpy as np
from jax import lax
from jax.experimental import pallas as pl
from jax.experimental.pallas import tpu as pltpu
from jax.sharding import PartitionSpec as P

HEADS = 16
HEAD_DIM = 64


epsilon = 1e-05
root_two_pi = math.sqrt(2.0 / math.pi)
masked_score = -1e30


def matmul(left, right):
    return jnp.dot(left, right, preferred_element_type=jnp.float32)


def contract_rows(left, right):
    return lax.dot_general(
        left, right, (((0,), (0,)), ((), ())), preferred_element_type=jnp.float32
    )


def contract_cols(left, right):
    return lax.dot_general(
        left, right, (((1,), (1,)), ((), ())), preferred_element_type=jnp.float32
    )


def norm_parts(values):
    centre = jnp.mean(values, -1, keepdims=True)
    shifted = values - centre
    inverse = lax.rsqrt(jnp.mean(shifted * shifted, -1, keepdims=True) + epsilon)
    return (shifted * inverse, inverse)


def norm_backward(grad_normed, normal, inverse, gain):
    scaled = grad_normed * gain
    return inverse * (
        scaled
        - jnp.mean(scaled, -1, keepdims=True)
        - normal * jnp.mean(scaled * normal, -1, keepdims=True)
    )


def gelu_parts(pre):
    tangent = jnp.tanh(root_two_pi * (pre + 0.044715 * pre * pre * pre))
    value = 0.5 * pre * (1.0 + tangent)
    slope = 0.5 * (1.0 + tangent) + 0.5 * pre * (1.0 - tangent * tangent) * root_two_pi * (
        1.0 + 3.0 * 0.044715 * pre * pre
    )
    return (value, slope)


def block_probs(query_rows, key_rows, start, length, slopes, scale):
    rows = query_rows.shape[0]
    cols = key_rows.shape[0]
    products = jnp.einsum("ihd,jhd->hij", query_rows, key_rows, preferred_element_type=jnp.float32)
    key_place = jnp.arange(cols, dtype=jnp.int32)
    distance = (start + jnp.arange(rows, dtype=jnp.int32))[:, None] - key_place[None, :]
    scores = products * scale - slopes[:, None, None] * distance.astype(jnp.float32)[None]
    allowed = (distance >= 0) & (key_place[None, :] < length)
    masked = jnp.where(allowed[None], scores, masked_score)
    highest = jnp.max(masked, -1, keepdims=True)
    exponent = jnp.exp(masked - highest)
    return exponent / jnp.sum(exponent, -1, keepdims=True)


def attention_forward(query, keys, values, length, slopes, scale):
    slots = query.shape[0]
    block = min(512, slots)
    outputs = []
    for number in range(slots // block):
        start = number * block
        probs = block_probs(query[start : start + block], keys, start, length, slopes, scale)
        mixed = jnp.einsum(
            "hij,jhd->ihd", probs.astype(jnp.bfloat16), values, preferred_element_type=jnp.float32
        )
        outputs.append(mixed.reshape(block, -1).astype(jnp.bfloat16))
    return jnp.concatenate(outputs, 0)


def attention_backward(query, keys, values, grad_attn, length, slopes, scale):
    slots, heads_local, head_width = query.shape
    block = min(512, slots)
    grad_keys = jnp.zeros((slots, heads_local, head_width), jnp.float32)
    grad_values = jnp.zeros((slots, heads_local, head_width), jnp.float32)
    query_parts = []
    for number in range(slots // block):
        start = number * block
        query_rows = query[start : start + block]
        grad_rows = grad_attn[start : start + block]
        probs = block_probs(query_rows, keys, start, length, slopes, scale)
        grad_probs = jnp.einsum(
            "ihd,jhd->hij", grad_rows, values, preferred_element_type=jnp.float32
        )
        delta = jnp.sum(probs * grad_probs, -1, keepdims=True)
        grad_scores = (probs * (grad_probs - delta)).astype(jnp.bfloat16)
        part_query = (
            jnp.einsum("hij,jhd->ihd", grad_scores, keys, preferred_element_type=jnp.float32)
            * scale
        )
        part_keys = (
            jnp.einsum("hij,ihd->jhd", grad_scores, query_rows, preferred_element_type=jnp.float32)
            * scale
        )
        part_values = jnp.einsum(
            "hij,ihd->jhd",
            probs.astype(jnp.bfloat16),
            grad_rows,
            preferred_element_type=jnp.float32,
        )
        part_query, part_keys, part_values = (part_query, part_keys, part_values)
        query_parts.append(part_query)
        grad_keys = grad_keys.at[:slots].add(part_keys)
        grad_values = grad_values.at[:slots].add(part_values)
    grad_query = jnp.concatenate(query_parts, 0).reshape(slots, -1).astype(jnp.bfloat16)
    return (
        grad_query,
        grad_keys.reshape(slots, -1).astype(jnp.bfloat16),
        grad_values.reshape(slots, -1).astype(jnp.bfloat16),
    )


QUERY_BLOCK = 256
PAIR = 128
NT = (((1,), (1,)), ((), ()))
TN = (((0,), (0,)), ((), ()))


def mm(left, right, dims=(((1,), (0,)), ((), ()))):
    return lax.dot_general(left, right, dims, preferred_element_type=jnp.float32)


def low_lanes(rows):
    return lax.broadcasted_iota(jnp.int32, (rows, PAIR), 1) < HEAD_DIM


def slope_rows():
    table = np.zeros((HEADS // 2, 8, PAIR), np.float64)
    for head in range(HEADS):
        rest = np.float64(np.float32(2.0 ** (-8.0 * (head + 1) / HEADS)))
        base = HEAD_DIM * (1 - head % 2)
        for part in range(3):
            piece = np.float64(np.asarray(rest).astype(jnp.bfloat16))
            rest = rest - piece
            table[head // 2, head % 2, base + part] = 32.0 * piece
            table[head // 2, head % 2, base + 3 + part] = piece
        table[head // 2, head % 2, base + 6] = 1.0
    return table.astype(jnp.bfloat16)


def key_lanes(slots, length):
    place = jnp.arange(slots, dtype=jnp.int32)[:, None]
    lane = jnp.arange(PAIR, dtype=jnp.int32)[None, :] % HEAD_DIM
    high = (place // 32).astype(jnp.float32)
    low = (place % 32).astype(jnp.float32)
    mask = jnp.where(place < length, 0.0, masked_score)
    return jnp.where(
        lane < 3, high, jnp.where(lane < 6, low, jnp.where(lane == 6, mask, 0.0))
    ).astype(jnp.bfloat16)


def forward_kernel(q_ref, k_ref, v_ref, lanes_ref, rows_ref, o_ref, key0, key1, val0, val1):
    slots = q_ref.shape[0]
    block = QUERY_BLOCK
    low = low_lanes(slots)
    zero = jnp.zeros((slots, PAIR), jnp.bfloat16)
    one = jnp.ones((slots, PAIR), jnp.bfloat16)
    key0[...] = jnp.where(low, k_ref[...], lanes_ref[...])
    key1[...] = jnp.where(low, lanes_ref[...], k_ref[...])
    val0[:, :PAIR] = jnp.where(low, v_ref[...], zero)
    val0[:, PAIR:] = jnp.where(low, one, zero)
    val1[:, :PAIR] = jnp.where(low, zero, v_ref[...])
    val1[:, PAIR:] = jnp.where(low, zero, one)
    low_block = low_lanes(block)
    causal = lax.broadcasted_iota(jnp.int32, (block, block), 1) <= lax.broadcasted_iota(
        jnp.int32, (block, block), 0
    )
    for number in range(slots // block):
        start = number * block
        rows = q_ref[start : start + block, :] * jnp.bfloat16(0.125)
        total = None
        for head, (key, val) in enumerate(((key0, val0), (key1, val1))):
            extra = jnp.broadcast_to(rows_ref[0, head : head + 1, :], (block, PAIR))
            query = jnp.where(low_block, rows, extra) if head == 0 else jnp.where(
                low_block, extra, rows
            )
            own = jnp.where(causal, mm(query, key[start : start + block, :], NT), masked_score)
            highest = jnp.max(own, 1, keepdims=True)
            if start:
                past = mm(query, key[:start, :], NT)
                highest = jnp.maximum(highest, jnp.max(past, 1, keepdims=True))
                part = mm(jnp.exp(past - highest).astype(jnp.bfloat16), val[:start, :])
                total = part if total is None else total + part
            part = mm(jnp.exp(own - highest).astype(jnp.bfloat16), val[start : start + block, :])
            total = part if total is None else total + part
        o_ref[start : start + block, :] = (total[:, :PAIR] / total[:, PAIR:]).astype(jnp.bfloat16)


def backward_kernel(
    q_ref, k_ref, v_ref, g_ref, lanes_ref, rows_ref, dq_ref, dk_ref, dv_ref,
    key0, key1, val0, val1, bare0, bare1, total_k, total_v,
):
    slots = q_ref.shape[0]
    block = QUERY_BLOCK
    low = low_lanes(slots)
    zero = jnp.zeros((slots, PAIR), jnp.bfloat16)
    key0[...] = jnp.where(low, k_ref[...], lanes_ref[...])
    key1[...] = jnp.where(low, lanes_ref[...], k_ref[...])
    bare0[...] = jnp.where(low, k_ref[...], zero)
    bare1[...] = jnp.where(low, zero, k_ref[...])
    val0[...] = jnp.where(low, v_ref[...], zero)
    val1[...] = jnp.where(low, zero, v_ref[...])
    low_block = low_lanes(block)
    nil = jnp.zeros((block, PAIR), jnp.bfloat16)
    causal = lax.broadcasted_iota(jnp.int32, (block, block), 0) <= lax.broadcasted_iota(
        jnp.int32, (block, block), 1
    )
    for number in reversed(range(slots // block)):
        start = number * block
        stop = start + block
        rows = q_ref[start:stop, :] * jnp.bfloat16(0.125)
        grad = g_ref[start:stop, :]
        probs, scores = [], []
        grad_query = None
        for head, (key, val, bare) in enumerate(((key0, val0, bare0), (key1, val1, bare1))):
            extra = jnp.broadcast_to(rows_ref[0, head : head + 1, :], (block, PAIR))
            query = jnp.where(low_block, rows, extra) if head == 0 else jnp.where(
                low_block, extra, rows
            )
            score = mm(key[:stop, :], query, NT)
            own = jnp.where(causal, score[start:], masked_score)
            score = jnp.concatenate([score[:start], own], 0) if start else own
            highest = jnp.max(score, 0, keepdims=True)
            raised = jnp.exp(score - highest)
            prob = raised * (1.0 / jnp.sum(raised, 0, keepdims=True))
            grad_prob = mm(val[:stop, :], grad, NT)
            delta = jnp.sum(prob * grad_prob, 0, keepdims=True)
            grad_score = (prob * (grad_prob - delta)).astype(jnp.bfloat16)
            probs.append(prob.astype(jnp.bfloat16))
            scores.append(grad_score)
            part = mm(grad_score, bare[:stop, :], TN)
            grad_query = part if grad_query is None else grad_query + part
        dq_ref[start:stop, :] = (grad_query * 0.125).astype(jnp.bfloat16)
        part_v = mm(
            jnp.concatenate(probs, 1),
            jnp.concatenate([jnp.where(low_block, grad, nil), jnp.where(low_block, nil, grad)], 0),
        )
        part_k = mm(
            jnp.concatenate(scores, 1),
            jnp.concatenate([jnp.where(low_block, rows, nil), jnp.where(low_block, nil, rows)], 0),
        )
        if stop == slots:
            total_v[...] = part_v
            total_k[...] = part_k
        else:
            total_v[:stop, :] += part_v
            total_k[:stop, :] += part_k
    dk_ref[...] = total_k[...].astype(jnp.bfloat16)
    dv_ref[...] = total_v[...].astype(jnp.bfloat16)


def pair_specs(slots):
    part = pl.BlockSpec((slots, PAIR), lambda pair: (0, pair))
    lanes = pl.BlockSpec((slots, PAIR), lambda pair: (0, 0))
    rows = pl.BlockSpec((1, 8, PAIR), lambda pair: (pair, 0, 0))
    return part, lanes, rows


def attention_out(query, keys, values, lanes, rows):
    slots, columns = query.shape
    part, lane_spec, row_spec = pair_specs(slots)
    pairs = columns // PAIR
    half = slots * slots * PAIR * pairs
    return pl.pallas_call(
        forward_kernel,
        grid=(pairs,),
        out_shape=jax.ShapeDtypeStruct((slots, columns), jnp.bfloat16),
        in_specs=[part, part, part, lane_spec, row_spec],
        out_specs=part,
        scratch_shapes=[pltpu.VMEM((slots, PAIR), jnp.bfloat16)] * 2
        + [pltpu.VMEM((slots, 2 * PAIR), jnp.bfloat16)] * 2,
        cost_estimate=pl.CostEstimate(
            flops=8 * half, bytes_accessed=8 * slots * columns, transcendentals=slots * slots * pairs
        ),
        name="attention_out",
    )(query, keys, values, lanes, rows)


def attention_grads(query, keys, values, grad, lanes, rows):
    slots, columns = query.shape
    part, lane_spec, row_spec = pair_specs(slots)
    pairs = columns // PAIR
    half = slots * slots * PAIR * pairs
    shape = jax.ShapeDtypeStruct((slots, columns), jnp.bfloat16)
    return pl.pallas_call(
        backward_kernel,
        grid=(pairs,),
        out_shape=(shape, shape, shape),
        in_specs=[part, part, part, part, lane_spec, row_spec],
        out_specs=(part, part, part),
        scratch_shapes=[pltpu.VMEM((slots, PAIR), jnp.bfloat16)] * 6
        + [pltpu.VMEM((slots, PAIR), jnp.float32)] * 2,
        cost_estimate=pl.CostEstimate(
            flops=20 * half,
            bytes_accessed=14 * slots * columns,
            transcendentals=slots * slots * pairs,
        ),
        name="attention_grads",
    )(query, keys, values, grad, lanes, rows)


RING = ((0, 0), (1, 0), (2, 0), (3, 0), (3, 1), (2, 1), (1, 1), (0, 1))


def device_of(z, y, core):
    return (z * 2 + y) * 2 + core


def ring_pairs(direction):
    return [
        (device_of(*RING[i], core), device_of(*RING[(i + direction) % len(RING)], core))
        for i in range(len(RING))
        for core in range(2)
    ]


def to_tensor(value):
    return lax.ppermute(value, "tensor", [(0, 1), (1, 0)])


def to_core(value):
    return lax.ppermute(value, "dp", [(i, i ^ 1) for i in range(2 * len(RING))])


def to_y(value):
    return lax.ppermute(value, "dp", [(i, i ^ 2) for i in range(2 * len(RING))])


def to_z(value, bit):
    return lax.ppermute(value, "dp", [(i, i ^ bit) for i in range(2 * len(RING))])


def rows_at(value, start, size):
    return lax.dynamic_slice_in_dim(value, start, size, value.ndim - 2)


def put_rows(whole, value, start):
    return lax.dynamic_update_slice_in_dim(whole, value, start, whole.ndim - 2)


def other_half(weight, y, core):
    quarter = weight.shape[-2] // 4
    mine = to_tensor(rows_at(weight, (2 * y + core) * quarter, quarter))
    beside = to_y(mine)
    whole = jnp.zeros(weight.shape, weight.dtype)
    whole = put_rows(whole, mine, (2 * y + core) * quarter)
    whole = put_rows(whole, beside, (2 * (1 - y) + core) * quarter)
    whole = put_rows(whole, to_core(mine), (2 * y + 1 - core) * quarter)
    return put_rows(whole, to_core(beside), (2 * (1 - y) + 1 - core) * quarter)


def ring_sum(value, place, direction):
    count = len(RING)
    pairs = ring_pairs(direction)

    def block(offset):
        return lax.rem(place - direction * offset + 2 * count, count)

    def take(offset):
        return lax.dynamic_index_in_dim(value, block(offset), 0, keepdims=False)

    held = take(0)
    for step in range(1, count):
        arrived = lax.ppermute(held, "dp", pairs)
        held = (arrived.astype(jnp.float32) + take(step).astype(jnp.float32)).astype(jnp.bfloat16)
    result = jnp.zeros(value.shape, jnp.bfloat16)
    result = lax.dynamic_update_index_in_dim(result, held, block(count - 1), 0)
    for step in range(count, 2 * count - 1):
        held = lax.ppermute(held, "dp", pairs)
        result = lax.dynamic_update_index_in_dim(result, held, block(step), 0)
    return result


def plane_sum(value, place):
    rows, columns = value.shape
    parts = value.reshape(2, len(RING), rows // (2 * len(RING)), columns)
    both = [ring_sum(parts[0], place, 1), ring_sum(parts[1], place, -1)]
    return jnp.stack(both, 0).reshape(rows, columns)


def core_half(left, rights, core):
    half = left.shape[1] // 2
    sent_left = lax.dynamic_slice_in_dim(left, (1 - core) * half, half, 1)
    kept_left = lax.dynamic_slice_in_dim(left, core * half, half, 1)
    arrived = [to_core(contract_rows(sent_left, right).astype(jnp.bfloat16)) for right in rights]
    return [
        contract_rows(kept_left, right) + part.astype(jnp.float32)
        for right, part in zip(rights, arrived)
    ]


def total_grad(local, other, core, place):
    passed = [to_tensor(part.astype(jnp.bfloat16)) for part in core_half(*other, core)]
    kept = core_half(*local, core)
    mine = [
        (part + more.astype(jnp.float32)).astype(jnp.bfloat16) for part, more in zip(kept, passed)
    ]
    rows = mine[0].shape[0]
    summed = plane_sum(jnp.concatenate(mine, 0), place)
    beside = to_core(summed)
    first = jnp.where(core == 0, summed, beside).astype(jnp.float32)
    second = jnp.where(core == 0, beside, summed).astype(jnp.float32)
    count = len(mine)
    first = first.reshape(count, rows, -1)
    second = second.reshape(count, rows, -1)
    return jnp.concatenate([first, second], 1)


def everywhere(value):
    value = value + to_core(value)
    value = value + to_tensor(value)
    for bit in (2, 4, 8):
        value = value + to_z(value, bit)
    return value


def trade_rows(value, place, own):
    share = value.shape[0] // 2
    arrived = to_tensor(lax.dynamic_slice_in_dim(value, (1 - own) * share, share, 0))
    kept = lax.dynamic_slice_in_dim(value, own * share, share, 0)
    return jnp.stack(
        [jnp.where(own == 0, kept, arrived), jnp.where(own == 0, arrived, kept)], 0
    )


def whole_sequence(
    tokens,
    d_output,
    lengths,
    ln1_gain,
    ln1_bias,
    w_qkv,
    qv_bias,
    w_out,
    bias_out,
    ln2_gain,
    ln2_bias,
    w_up,
    b_up,
    w_down,
    b_down,
):
    own = lax.axis_index("tensor")
    device = lax.axis_index("dp")
    core, y, z = device % 2, (device // 2) % 2, device // 4
    place = jnp.where(y == 0, z, len(RING) - 1 - z)
    slots, width = tokens.shape[1:]
    local_width = w_qkv.shape[2]
    hidden_local = w_up.shape[1]
    table = jnp.asarray(slope_rows())
    pairs = local_width // PAIR
    f32 = jnp.float32

    weight_qkv = w_qkv.transpose(1, 0, 2)
    biases = jnp.concatenate([qv_bias.reshape(-1), b_up])
    other_biases = to_tensor(biases)
    qkv = (weight_qkv, other_half(weight_qkv, y, core))
    out = (w_out, other_half(w_out, y, core))
    up = (w_up, other_half(w_up, y, core))
    down = (w_down, other_half(w_down, y, core))
    qv = [b[: 2 * local_width].reshape(2, local_width).astype(f32) for b in (biases, other_biases)]
    ups = [b[2 * local_width :].astype(f32) for b in (biases, other_biases)]
    rows = [lax.dynamic_slice_in_dim(table, index * pairs, pairs, 0) for index in (own, 1 - own)]
    gain_one, shift_one = ln1_gain.astype(f32), ln1_bias.astype(f32)
    gain_two, shift_two = ln2_gain.astype(f32), ln2_bias.astype(f32)

    def pick(value):
        return lax.dynamic_index_in_dim(value, own, 0, keepdims=False)

    tokens_f = pick(tokens).astype(f32)
    length = pick(lengths)
    lanes = key_lanes(slots, length)
    normal_one, inverse_one = norm_parts(tokens_f)
    normed_one = (normal_one * gain_one + shift_one).astype(jnp.bfloat16)
    heads = []
    mixed = []
    for half in range(2):
        query = (matmul(normed_one, qkv[half][0]) + qv[half][0]).astype(jnp.bfloat16)
        keys = matmul(normed_one, qkv[half][1]).astype(jnp.bfloat16)
        values = (matmul(normed_one, qkv[half][2]) + qv[half][1]).astype(jnp.bfloat16)
        heads.append((query, keys, values))
        mixed.append(attention_out(query, keys, values, lanes, rows[half]))
    hidden = tokens_f + bias_out.astype(f32) + matmul(mixed[0], out[0]) + matmul(mixed[1], out[1])
    normal_two, inverse_two = norm_parts(hidden)
    normed_two = (normal_two * gain_two + shift_two).astype(jnp.bfloat16)
    acts = []
    for half in range(2):
        value, slope = gelu_parts(matmul(normed_two, up[half]) + ups[half])
        acts.append(
            lax.optimization_barrier((value.astype(jnp.bfloat16), slope.astype(jnp.bfloat16)))
        )
    result = hidden + b_down.astype(f32) + matmul(acts[0][0], down[0]) + matmul(acts[1][0], down[1])
    output = trade_rows(result.astype(jnp.bfloat16), place, own)

    valid = (jnp.arange(slots, dtype=jnp.int32) < length).astype(f32)[:, None]
    grad_out = pick(d_output).astype(f32) * valid
    grad_two = grad_out.astype(jnp.bfloat16)
    grad_wdown = total_grad((acts[0][0], [grad_two]), (acts[1][0], [grad_two]), core, place)
    grad_pre = [
        (contract_cols(grad_two, down[half]) * acts[half][1].astype(f32)).astype(jnp.bfloat16)
        for half in range(2)
    ]
    grad_wup = total_grad((normed_two, [grad_pre[0]]), (normed_two, [grad_pre[1]]), core, place)
    grad_norm_two = contract_cols(grad_pre[0], up[0]) + contract_cols(grad_pre[1], up[1])
    grad_hidden = grad_out + norm_backward(grad_norm_two, normal_two, inverse_two, gain_two)
    grad_one = grad_hidden.astype(jnp.bfloat16)
    grad_wout = total_grad((mixed[0], [grad_one]), (mixed[1], [grad_one]), core, place)
    grads = [None, None]
    for half in (1, 0):
        grad_attn = contract_cols(grad_one, out[half]).astype(jnp.bfloat16)
        grads[half] = attention_grads(*heads[half], grad_attn, lanes, rows[half])
    grad_wqkv = total_grad(
        (normed_one, list(grads[0])), (normed_one, list(grads[1])), core, place
    )
    grad_norm_one = sum(
        contract_cols(grads[half][part], qkv[half][part]) for half in range(2) for part in range(3)
    )
    grad_tokens = grad_hidden + norm_backward(grad_norm_one, normal_one, inverse_one, gain_one)
    grad_tokens = trade_rows(grad_tokens.astype(jnp.bfloat16), place, own)

    def column_sum(value):
        return jnp.sum(value.astype(f32), 0)

    def in_place(parts):
        first = jnp.where(own == 0, parts[0], parts[1])
        second = jnp.where(own == 0, parts[1], parts[0])
        return jnp.concatenate([first, second], 0)

    small = [
        jnp.sum(grad_norm_one * normal_one, 0),
        jnp.sum(grad_norm_one, 0),
        jnp.sum(grad_norm_two * normal_two, 0),
        jnp.sum(grad_norm_two, 0),
        column_sum(grad_one),
        column_sum(grad_two),
        in_place([column_sum(grads[half][0]) for half in range(2)]),
        in_place([column_sum(grads[half][2]) for half in range(2)]),
        in_place([column_sum(grad_pre[half]) for half in range(2)]),
    ]
    small = everywhere(jnp.concatenate(small).reshape(-1, width))
    wide = [lax.dynamic_slice_in_dim(small[i], own * local_width, local_width, 0) for i in (6, 7)]
    grad_bup = lax.dynamic_slice_in_dim(
        small[8:].reshape(-1), own * hidden_local, hidden_local, 0
    )
    return (
        output,
        grad_tokens,
        small[0],
        small[1],
        grad_wqkv.transpose(1, 0, 2),
        jnp.stack(wide, 0),
        grad_wout[0],
        small[4],
        small[2],
        small[3],
        grad_wup[0],
        grad_bup,
        grad_wdown[0],
        small[5],
    )


def on_device(
    tokens,
    d_output,
    lengths,
    ln1_gain,
    ln1_bias,
    w_qkv,
    qv_bias,
    w_out,
    bias_out,
    ln2_gain,
    ln2_bias,
    w_up,
    b_up,
    w_down,
    b_down,
):
    parts = lax.axis_size("tensor")
    place = lax.axis_index("tensor")
    batches, slots, width = tokens.shape
    share = slots // parts
    row_start = place * share
    local_width = w_qkv.shape[2]
    hidden_local = w_up.shape[1]
    heads_local = local_width // HEAD_DIM
    scale = 1.0 / math.sqrt(HEAD_DIM)
    first_head = place * heads_local
    slopes = jnp.exp2(
        -8.0
        * ((first_head + jnp.arange(heads_local, dtype=jnp.int32)).astype(jnp.float32) + 1.0)
        / HEADS
    )
    weight_qkv = w_qkv.reshape(width, 3 * local_width)
    qkv_shift = jnp.concatenate(
        [
            qv_bias[0].astype(jnp.float32),
            jnp.zeros((local_width,), jnp.float32),
            qv_bias[1].astype(jnp.float32),
        ]
    )
    gain_one = ln1_gain.astype(jnp.float32)
    shift_one = ln1_bias.astype(jnp.float32)
    gain_two = ln2_gain.astype(jnp.float32)
    shift_two = ln2_bias.astype(jnp.float32)
    out_shift = bias_out.astype(jnp.float32)
    up_shift = b_up.astype(jnp.float32)
    down_shift = b_down.astype(jnp.float32)
    grad_qkv = jnp.zeros((width, 3 * local_width), jnp.float32)
    grad_qvb = jnp.zeros((2, local_width), jnp.float32)
    grad_wout = jnp.zeros((local_width, width), jnp.float32)
    grad_wup = jnp.zeros((width, hidden_local), jnp.float32)
    grad_bup = jnp.zeros((hidden_local,), jnp.float32)
    grad_wdown = jnp.zeros((hidden_local, width), jnp.float32)
    grad_gain_one = jnp.zeros((width,), jnp.float32)
    grad_shift_one = jnp.zeros((width,), jnp.float32)
    grad_gain_two = jnp.zeros((width,), jnp.float32)
    grad_shift_two = jnp.zeros((width,), jnp.float32)
    grad_out_shift = jnp.zeros((width,), jnp.float32)
    grad_down_shift = jnp.zeros((width,), jnp.float32)
    output_rows = []
    input_rows = []
    for index in range(batches):
        tokens_f = tokens[index].astype(jnp.float32)
        length = lengths[index]
        normal_one, inverse_one = norm_parts(tokens_f)
        normed_one = (normal_one * gain_one + shift_one).astype(jnp.bfloat16)
        projected = (matmul(normed_one, weight_qkv) + qkv_shift).astype(jnp.bfloat16)
        query = projected[:, :local_width].reshape(slots, heads_local, HEAD_DIM)
        keys = projected[:, local_width : 2 * local_width].reshape(slots, heads_local, HEAD_DIM)
        values = projected[:, 2 * local_width :].reshape(slots, heads_local, HEAD_DIM)
        attn = attention_forward(query, keys, values, length, slopes, scale)
        partial_value = matmul(attn, w_out)
        summed = lax.psum(partial_value.astype(jnp.bfloat16), "tensor").astype(jnp.float32)
        hidden_full = tokens_f + summed + out_shift
        normal_full, inverse_full = norm_parts(hidden_full)
        normed_two = (normal_full * gain_two + shift_two).astype(jnp.bfloat16)
        hidden_rows = lax.dynamic_slice_in_dim(hidden_full, row_start, share, 0)
        normal_two = lax.dynamic_slice_in_dim(normal_full, row_start, share, 0)
        inverse_two = lax.dynamic_slice_in_dim(inverse_full, row_start, share, 0)
        pre = matmul(normed_two, w_up) + up_shift
        act_value, act_slope = gelu_parts(pre)
        act = act_value.astype(jnp.bfloat16)
        mlp_part = lax.psum_scatter(
            matmul(act, w_down).astype(jnp.bfloat16), "tensor", scatter_dimension=0, tiled=True
        ).astype(jnp.float32)
        output_rows.append((hidden_rows + mlp_part + down_shift).astype(jnp.bfloat16))
        valid = (jnp.arange(slots, dtype=jnp.int32) < length).astype(jnp.float32)[:, None]
        grad_out = d_output[index].astype(jnp.float32) * valid
        grad_two = grad_out.astype(jnp.bfloat16)
        grad_wdown = grad_wdown + contract_rows(act, grad_two)
        grad_pre = (contract_cols(grad_two, w_down) * act_slope).astype(jnp.bfloat16)
        grad_wup = grad_wup + contract_rows(normed_two, grad_pre)
        grad_bup = grad_bup + jnp.sum(grad_pre.astype(jnp.float32), 0)
        grad_norm_two = lax.psum_scatter(
            contract_cols(grad_pre, w_up).astype(jnp.bfloat16),
            "tensor",
            scatter_dimension=0,
            tiled=True,
        ).astype(jnp.float32)
        grad_gain_two = grad_gain_two + jnp.sum(grad_norm_two * normal_two, 0)
        grad_shift_two = grad_shift_two + jnp.sum(grad_norm_two, 0)
        grad_out_rows = lax.dynamic_slice_in_dim(grad_out, row_start, share, 0)
        grad_hidden_rows = grad_out_rows + norm_backward(
            grad_norm_two, normal_two, inverse_two, gain_two
        )
        grad_one_rows = grad_hidden_rows.astype(jnp.bfloat16)
        grad_down_shift = grad_down_shift + jnp.sum(
            lax.dynamic_slice_in_dim(grad_two, row_start, share, 0).astype(jnp.float32), 0
        )
        grad_out_shift = grad_out_shift + jnp.sum(grad_one_rows.astype(jnp.float32), 0)
        grad_one = lax.all_gather(grad_one_rows, "tensor", axis=0, tiled=True)
        grad_wout = grad_wout + contract_rows(attn, grad_one)
        grad_attn = (
            contract_cols(grad_one, w_out)
            .astype(jnp.bfloat16)
            .reshape(slots, heads_local, HEAD_DIM)
        )
        grad_query, grad_keys, grad_values = attention_backward(
            query, keys, values, grad_attn, length, slopes, scale
        )
        grad_proj = jnp.concatenate([grad_query, grad_keys, grad_values], 1)
        grad_qkv = grad_qkv + contract_rows(normed_one, grad_proj)
        grad_qvb = grad_qvb + jnp.stack(
            [
                jnp.sum(grad_query.astype(jnp.float32), 0),
                jnp.sum(grad_values.astype(jnp.float32), 0),
            ],
            0,
        )
        grad_norm_one = lax.psum_scatter(
            contract_cols(grad_proj, weight_qkv).astype(jnp.bfloat16),
            "tensor",
            scatter_dimension=0,
            tiled=True,
        ).astype(jnp.float32)
        normal_one_rows = lax.dynamic_slice_in_dim(normal_one, row_start, share, 0)
        inverse_one_rows = lax.dynamic_slice_in_dim(inverse_one, row_start, share, 0)
        grad_gain_one = grad_gain_one + jnp.sum(grad_norm_one * normal_one_rows, 0)
        grad_shift_one = grad_shift_one + jnp.sum(grad_norm_one, 0)
        input_rows.append(
            (
                grad_hidden_rows
                + norm_backward(grad_norm_one, normal_one_rows, inverse_one_rows, gain_one)
            ).astype(jnp.bfloat16)
        )
    grad_qkv, grad_qvb, grad_wout, grad_wup, grad_bup, grad_wdown = (
        lax.psum(grad_qkv.astype(jnp.bfloat16), "dp").astype(jnp.float32),
        lax.psum(grad_qvb.astype(jnp.bfloat16), "dp").astype(jnp.float32),
        lax.psum(grad_wout.astype(jnp.bfloat16), "dp").astype(jnp.float32),
        lax.psum(grad_wup.astype(jnp.bfloat16), "dp").astype(jnp.float32),
        lax.psum(grad_bup.astype(jnp.bfloat16), "dp").astype(jnp.float32),
        lax.psum(grad_wdown.astype(jnp.bfloat16), "dp").astype(jnp.float32),
    )
    (
        grad_gain_one,
        grad_shift_one,
        grad_gain_two,
        grad_shift_two,
        grad_out_shift,
        grad_down_shift,
    ) = lax.psum(
        (
            grad_gain_one,
            grad_shift_one,
            grad_gain_two,
            grad_shift_two,
            grad_out_shift,
            grad_down_shift,
        ),
        ("dp", "tensor"),
    )
    return (
        jnp.stack(output_rows, 0),
        jnp.stack(input_rows, 0),
        grad_gain_one,
        grad_shift_one,
        grad_qkv.reshape(width, 3, local_width),
        grad_qvb,
        grad_wout,
        grad_out_shift,
        grad_gain_two,
        grad_shift_two,
        grad_wup,
        grad_bup,
        grad_wdown,
        grad_down_shift,
    )


def solution(mesh):
    whole = mesh.shape["tensor"] == 2 and mesh.shape["dp"] == 2 * len(RING)
    return jax.shard_map(
        whole_sequence if whole else on_device,
        mesh=mesh,
        in_specs=(
            P("dp", None, None),
            P("dp", None, None),
            P("dp"),
            P(),
            P(),
            P(None, None, "tensor"),
            P(None, "tensor"),
            P("tensor", None),
            P(),
            P(),
            P(),
            P(None, "tensor"),
            P("tensor"),
            P("tensor", None),
            P(),
        ),
        out_specs=(
            P("dp", "tensor", None),
            P("dp", "tensor", None),
            P(),
            P(),
            P(None, None, "tensor"),
            P(None, "tensor"),
            P("tensor", None),
            P(),
            P(),
            P(),
            P(None, "tensor"),
            P("tensor"),
            P("tensor", None),
            P(),
        ),
        check_vma=False,
    )
```

```python
import functools
import math

import jax
import jax.numpy as jnp
import numpy as np
from jax import lax
from jax.experimental import pallas as pl
from jax.experimental.pallas import tpu as pltpu
from jax.sharding import PartitionSpec as P

HEADS = 16
HEAD_DIM = 64


epsilon = 1e-05
root_two_pi = math.sqrt(2.0 / math.pi)
masked_score = -1e30


def matmul(left, right):
    return jnp.dot(left, right, preferred_element_type=jnp.float32)


def contract_rows(left, right):
    return lax.dot_general(
        left, right, (((0,), (0,)), ((), ())), preferred_element_type=jnp.float32
    )


def contract_cols(left, right):
    return lax.dot_general(
        left, right, (((1,), (1,)), ((), ())), preferred_element_type=jnp.float32
    )


def norm_parts(values):
    centre = jnp.mean(values, -1, keepdims=True)
    shifted = values - centre
    inverse = lax.rsqrt(jnp.mean(shifted * shifted, -1, keepdims=True) + epsilon)
    return (shifted * inverse, inverse)


def norm_backward(grad_normed, normal, inverse, gain):
    scaled = grad_normed * gain
    return inverse * (
        scaled
        - jnp.mean(scaled, -1, keepdims=True)
        - normal * jnp.mean(scaled * normal, -1, keepdims=True)
    )


def gelu_parts(pre):
    tangent = jnp.tanh(root_two_pi * (pre + 0.044715 * pre * pre * pre))
    value = 0.5 * pre * (1.0 + tangent)
    slope = 0.5 * (1.0 + tangent) + 0.5 * pre * (1.0 - tangent * tangent) * root_two_pi * (
        1.0 + 3.0 * 0.044715 * pre * pre
    )
    return (value, slope)


def block_probs(query_rows, key_rows, start, length, slopes, scale):
    rows = query_rows.shape[0]
    cols = key_rows.shape[0]
    products = jnp.einsum("ihd,jhd->hij", query_rows, key_rows, preferred_element_type=jnp.float32)
    key_place = jnp.arange(cols, dtype=jnp.int32)
    distance = (start + jnp.arange(rows, dtype=jnp.int32))[:, None] - key_place[None, :]
    scores = products * scale - slopes[:, None, None] * distance.astype(jnp.float32)[None]
    allowed = (distance >= 0) & (key_place[None, :] < length)
    masked = jnp.where(allowed[None], scores, masked_score)
    highest = jnp.max(masked, -1, keepdims=True)
    exponent = jnp.exp(masked - highest)
    return exponent / jnp.sum(exponent, -1, keepdims=True)


def attention_forward(query, keys, values, length, slopes, scale):
    slots = query.shape[0]
    block = min(512, slots)
    outputs = []
    for number in range(slots // block):
        start = number * block
        probs = block_probs(query[start : start + block], keys, start, length, slopes, scale)
        mixed = jnp.einsum(
            "hij,jhd->ihd", probs.astype(jnp.bfloat16), values, preferred_element_type=jnp.float32
        )
        outputs.append(mixed.reshape(block, -1).astype(jnp.bfloat16))
    return jnp.concatenate(outputs, 0)


def attention_backward(query, keys, values, grad_attn, length, slopes, scale):
    slots, heads_local, head_width = query.shape
    block = min(512, slots)
    grad_keys = jnp.zeros((slots, heads_local, head_width), jnp.float32)
    grad_values = jnp.zeros((slots, heads_local, head_width), jnp.float32)
    query_parts = []
    for number in range(slots // block):
        start = number * block
        query_rows = query[start : start + block]
        grad_rows = grad_attn[start : start + block]
        probs = block_probs(query_rows, keys, start, length, slopes, scale)
        grad_probs = jnp.einsum(
            "ihd,jhd->hij", grad_rows, values, preferred_element_type=jnp.float32
        )
        delta = jnp.sum(probs * grad_probs, -1, keepdims=True)
        grad_scores = (probs * (grad_probs - delta)).astype(jnp.bfloat16)
        part_query = (
            jnp.einsum("hij,jhd->ihd", grad_scores, keys, preferred_element_type=jnp.float32)
            * scale
        )
        part_keys = (
            jnp.einsum("hij,ihd->jhd", grad_scores, query_rows, preferred_element_type=jnp.float32)
            * scale
        )
        part_values = jnp.einsum(
            "hij,ihd->jhd",
            probs.astype(jnp.bfloat16),
            grad_rows,
            preferred_element_type=jnp.float32,
        )
        part_query, part_keys, part_values = (part_query, part_keys, part_values)
        query_parts.append(part_query)
        grad_keys = grad_keys.at[:slots].add(part_keys)
        grad_values = grad_values.at[:slots].add(part_values)
    grad_query = jnp.concatenate(query_parts, 0).reshape(slots, -1).astype(jnp.bfloat16)
    return (
        grad_query,
        grad_keys.reshape(slots, -1).astype(jnp.bfloat16),
        grad_values.reshape(slots, -1).astype(jnp.bfloat16),
    )


QUERY_BLOCK = 256
PAIR = 128
NT = (((1,), (1,)), ((), ()))
TN = (((0,), (0,)), ((), ()))


def mm(left, right, dims=(((1,), (0,)), ((), ()))):
    return lax.dot_general(left, right, dims, preferred_element_type=jnp.float32)


def low_lanes(rows):
    return lax.broadcasted_iota(jnp.int32, (rows, PAIR), 1) < HEAD_DIM


def slope_rows():
    table = np.zeros((HEADS // 2, 8, PAIR), np.float64)
    for head in range(HEADS):
        rest = np.float64(np.float32(2.0 ** (-8.0 * (head + 1) / HEADS)))
        base = HEAD_DIM * (1 - head % 2)
        for part in range(3):
            piece = np.float64(np.asarray(rest).astype(jnp.bfloat16))
            rest = rest - piece
            table[head // 2, head % 2, base + part] = 32.0 * piece
            table[head // 2, head % 2, base + 3 + part] = piece
        table[head // 2, head % 2, base + 6] = 1.0
    return table.astype(jnp.bfloat16)


def key_lanes(slots, length):
    place = jnp.arange(slots, dtype=jnp.int32)[:, None]
    lane = jnp.arange(PAIR, dtype=jnp.int32)[None, :] % HEAD_DIM
    high = (place // 32).astype(jnp.float32)
    low = (place % 32).astype(jnp.float32)
    mask = jnp.where(place < length, 0.0, masked_score)
    return jnp.where(
        lane < 3, high, jnp.where(lane < 6, low, jnp.where(lane == 6, mask, 0.0))
    ).astype(jnp.bfloat16)


def forward_kernel(q_ref, k_ref, v_ref, lanes_ref, rows_ref, o_ref, key0, key1, val0, val1):
    slots = q_ref.shape[0]
    block = QUERY_BLOCK
    low = low_lanes(slots)
    zero = jnp.zeros((slots, PAIR), jnp.bfloat16)
    one = jnp.ones((slots, PAIR), jnp.bfloat16)
    key0[...] = jnp.where(low, k_ref[...], lanes_ref[...])
    key1[...] = jnp.where(low, lanes_ref[...], k_ref[...])
    val0[:, :PAIR] = jnp.where(low, v_ref[...], zero)
    val0[:, PAIR:] = jnp.where(low, one, zero)
    val1[:, :PAIR] = jnp.where(low, zero, v_ref[...])
    val1[:, PAIR:] = jnp.where(low, zero, one)
    low_block = low_lanes(block)
    causal = lax.broadcasted_iota(jnp.int32, (block, block), 1) <= lax.broadcasted_iota(
        jnp.int32, (block, block), 0
    )
    for number in range(slots // block):
        start = number * block
        rows = q_ref[start : start + block, :] * jnp.bfloat16(0.125)
        total = None
        for head, (key, val) in enumerate(((key0, val0), (key1, val1))):
            extra = jnp.broadcast_to(rows_ref[0, head : head + 1, :], (block, PAIR))
            query = jnp.where(low_block, rows, extra) if head == 0 else jnp.where(
                low_block, extra, rows
            )
            own = jnp.where(causal, mm(query, key[start : start + block, :], NT), masked_score)
            highest = jnp.max(own, 1, keepdims=True)
            if start:
                past = mm(query, key[:start, :], NT)
                highest = jnp.maximum(highest, jnp.max(past, 1, keepdims=True))
                part = mm(jnp.exp(past - highest).astype(jnp.bfloat16), val[:start, :])
                total = part if total is None else total + part
            part = mm(jnp.exp(own - highest).astype(jnp.bfloat16), val[start : start + block, :])
            total = part if total is None else total + part
        o_ref[start : start + block, :] = (total[:, :PAIR] / total[:, PAIR:]).astype(jnp.bfloat16)


def backward_kernel(
    q_ref, k_ref, v_ref, g_ref, lanes_ref, rows_ref, dq_ref, dk_ref, dv_ref,
    key0, key1, val0, val1, bare0, bare1, total_k, total_v,
):
    slots = q_ref.shape[0]
    block = QUERY_BLOCK
    low = low_lanes(slots)
    zero = jnp.zeros((slots, PAIR), jnp.bfloat16)
    key0[...] = jnp.where(low, k_ref[...], lanes_ref[...])
    key1[...] = jnp.where(low, lanes_ref[...], k_ref[...])
    bare0[...] = jnp.where(low, k_ref[...], zero)
    bare1[...] = jnp.where(low, zero, k_ref[...])
    val0[...] = jnp.where(low, v_ref[...], zero)
    val1[...] = jnp.where(low, zero, v_ref[...])
    low_block = low_lanes(block)
    nil = jnp.zeros((block, PAIR), jnp.bfloat16)
    causal = lax.broadcasted_iota(jnp.int32, (block, block), 0) <= lax.broadcasted_iota(
        jnp.int32, (block, block), 1
    )
    for number in reversed(range(slots // block)):
        start = number * block
        stop = start + block
        rows = q_ref[start:stop, :] * jnp.bfloat16(0.125)
        grad = g_ref[start:stop, :]
        probs, scores = [], []
        grad_query = None
        for head, (key, val, bare) in enumerate(((key0, val0, bare0), (key1, val1, bare1))):
            extra = jnp.broadcast_to(rows_ref[0, head : head + 1, :], (block, PAIR))
            query = jnp.where(low_block, rows, extra) if head == 0 else jnp.where(
                low_block, extra, rows
            )
            score = mm(key[:stop, :], query, NT)
            own = jnp.where(causal, score[start:], masked_score)
            score = jnp.concatenate([score[:start], own], 0) if start else own
            highest = jnp.max(score, 0, keepdims=True)
            raised = jnp.exp(score - highest)
            prob = raised * (1.0 / jnp.sum(raised, 0, keepdims=True))
            grad_prob = mm(val[:stop, :], grad, NT)
            delta = jnp.sum(prob * grad_prob, 0, keepdims=True)
            grad_score = (prob * (grad_prob - delta)).astype(jnp.bfloat16)
            probs.append(prob.astype(jnp.bfloat16))
            scores.append(grad_score)
            part = mm(grad_score, bare[:stop, :], TN)
            grad_query = part if grad_query is None else grad_query + part
        dq_ref[start:stop, :] = (grad_query * 0.125).astype(jnp.bfloat16)
        part_v = mm(
            jnp.concatenate(probs, 1),
            jnp.concatenate([jnp.where(low_block, grad, nil), jnp.where(low_block, nil, grad)], 0),
        )
        part_k = mm(
            jnp.concatenate(scores, 1),
            jnp.concatenate([jnp.where(low_block, rows, nil), jnp.where(low_block, nil, rows)], 0),
        )
        if stop == slots:
            total_v[...] = part_v
            total_k[...] = part_k
        else:
            total_v[:stop, :] += part_v
            total_k[:stop, :] += part_k
    dk_ref[...] = total_k[...].astype(jnp.bfloat16)
    dv_ref[...] = total_v[...].astype(jnp.bfloat16)


def pair_specs(slots):
    part = pl.BlockSpec((slots, PAIR), lambda pair: (0, pair))
    lanes = pl.BlockSpec((slots, PAIR), lambda pair: (0, 0))
    rows = pl.BlockSpec((1, 8, PAIR), lambda pair: (pair, 0, 0))
    return part, lanes, rows


def attention_out(query, keys, values, lanes, rows):
    slots, columns = query.shape
    part, lane_spec, row_spec = pair_specs(slots)
    pairs = columns // PAIR
    half = slots * slots * PAIR * pairs
    return pl.pallas_call(
        forward_kernel,
        grid=(pairs,),
        out_shape=jax.ShapeDtypeStruct((slots, columns), jnp.bfloat16),
        in_specs=[part, part, part, lane_spec, row_spec],
        out_specs=part,
        scratch_shapes=[pltpu.VMEM((slots, PAIR), jnp.bfloat16)] * 2
        + [pltpu.VMEM((slots, 2 * PAIR), jnp.bfloat16)] * 2,
        cost_estimate=pl.CostEstimate(
            flops=8 * half, bytes_accessed=8 * slots * columns, transcendentals=slots * slots * pairs
        ),
        name="attention_out",
    )(query, keys, values, lanes, rows)


def attention_grads(query, keys, values, grad, lanes, rows):
    slots, columns = query.shape
    part, lane_spec, row_spec = pair_specs(slots)
    pairs = columns // PAIR
    half = slots * slots * PAIR * pairs
    shape = jax.ShapeDtypeStruct((slots, columns), jnp.bfloat16)
    return pl.pallas_call(
        backward_kernel,
        grid=(pairs,),
        out_shape=(shape, shape, shape),
        in_specs=[part, part, part, part, lane_spec, row_spec],
        out_specs=(part, part, part),
        scratch_shapes=[pltpu.VMEM((slots, PAIR), jnp.bfloat16)] * 6
        + [pltpu.VMEM((slots, PAIR), jnp.float32)] * 2,
        cost_estimate=pl.CostEstimate(
            flops=20 * half,
            bytes_accessed=14 * slots * columns,
            transcendentals=slots * slots * pairs,
        ),
        name="attention_grads",
    )(query, keys, values, grad, lanes, rows)


RING = ((0, 0), (1, 0), (2, 0), (3, 0), (3, 1), (2, 1), (1, 1), (0, 1))


def device_of(z, y, core):
    return (z * 2 + y) * 2 + core


def to_tensor(value):
    return lax.ppermute(value, "tensor", [(0, 1), (1, 0)])


def to_core(value):
    return lax.ppermute(value, "dp", [(i, i ^ 1) for i in range(2 * len(RING))])


def to_y(value):
    return lax.ppermute(value, "dp", [(i, i ^ 2) for i in range(2 * len(RING))])


def to_z(value, bit):
    return lax.ppermute(value, "dp", [(i, i ^ bit) for i in range(2 * len(RING))])


def rows_at(value, start, size):
    return lax.dynamic_slice_in_dim(value, start, size, value.ndim - 2)


def put_rows(whole, value, start):
    return lax.dynamic_update_slice_in_dim(whole, value, start, whole.ndim - 2)


def after(value, *earlier):
    return lax.optimization_barrier((value, *earlier))[0]


def quarter_over_x(weight, y, core, *earlier):
    quarter = weight.shape[-2] // 4
    return to_tensor(after(rows_at(weight, (2 * y + core) * quarter, quarter), *earlier))


def other_half(mine, y, core):
    quarter = mine.shape[-2]
    beside = to_y(mine)
    whole = jnp.zeros((*mine.shape[:-2], 4 * quarter, mine.shape[-1]), mine.dtype)
    whole = put_rows(whole, mine, (2 * y + core) * quarter)
    whole = put_rows(whole, to_core(mine), (2 * y + 1 - core) * quarter)
    whole = put_rows(whole, beside, (2 * (1 - y) + core) * quarter)
    return put_rows(whole, to_core(beside), (2 * (1 - y) + 1 - core) * quarter)


def ring_kernel(blocks, *refs):
    count = len(RING)
    values, refs = refs[:blocks], refs[blocks:]
    results, refs = refs[:blocks], refs[blocks:]
    slots, refs = refs[:blocks], refs[blocks:]
    sums, refs = refs[:blocks], refs[blocks:]
    send_sems, recv_sems, swap_send_sems, swap_recv_sems = refs
    device = lax.axis_index("dp")
    core, y, z = lax.rem(device, 2), lax.rem(device // 2, 2), device // 4
    place = z * (1 - y) + (count - 1 - z) * y

    def at_place(where):
        side = where // 4
        return {"dp": device_of(where * (1 - side) + (count - 1 - where) * side, side, core)}

    nexts = (at_place(lax.rem(place + 1, count)), at_place(lax.rem(place + count - 1, count)))
    partner = {"dp": device + 1 - 2 * core}
    barrier = pltpu.get_barrier_semaphore()
    for target in (*nexts, partner):
        pl.semaphore_signal(barrier, inc=1, device_id=target, device_id_type=pl.DeviceIdType.MESH)
    pl.semaphore_wait(barrier, 3)

    streams = [(array, way) for array in range(blocks) for way in range(2)]

    def block(way, offset):
        return lax.rem(place - (1, -1)[way] * offset + 2 * count, count)

    def send(array, way, step, source, target):
        index = 2 * array + way
        copy = pltpu.make_async_remote_copy(
            src_ref=source,
            dst_ref=target,
            send_sem=send_sems.at[index, step],
            recv_sem=recv_sems.at[index, step],
            device_id=nexts[way],
            device_id_type=pl.DeviceIdType.MESH,
        )
        copy.start()
        return copy

    def swap(array, way, step, offset):
        index = 2 * array + way
        done = results[array].at[core, way, block(way, offset)]
        copy = pltpu.make_async_remote_copy(
            src_ref=done,
            dst_ref=done,
            send_sem=swap_send_sems.at[index, step],
            recv_sem=swap_recv_sems.at[index, step],
            device_id=partner,
            device_id_type=pl.DeviceIdType.MESH,
        )
        copy.start()
        return copy

    flying, swaps, started = {}, [], []
    for array, way in streams:
        copy = send(array, way, 0, values[array].at[way, block(way, 0)], slots[array].at[way, 0])
        flying[array, way] = copy
        started.append(copy)
    for step in range(1, 2 * count - 2):
        for array, way in streams:
            flying[array, way].wait_recv()
            if step < count:
                total = values[array][way, block(way, step)].astype(jnp.float32) + slots[array][
                    way, step - 1
                ].astype(jnp.float32)
                total = total.astype(jnp.bfloat16)
            if step < count - 1:
                sums[array][way, step - 1] = total
                source, target = sums[array].at[way, step - 1], slots[array].at[way, step]
            else:
                if step == count - 1:
                    results[array][core, way, block(way, step)] = total
                source = target = results[array].at[core, way, block(way, step)]
            copy = send(array, way, step, source, target)
            flying[array, way] = copy
            started.append(copy)
            if step >= count - 1:
                swaps.append(swap(array, way, step - count + 1, step))
    for array, way in streams:
        flying[array, way].wait_recv()
        swaps.append(swap(array, way, count - 1, 2 * count - 2))
    for copy in started:
        copy.wait_send()
    for copy in swaps:
        copy.wait()


def plane_sums(values, identity):
    count = len(RING)
    blocks = len(values)
    shaped = [
        value.reshape(2, count, value.shape[0] // (2 * count), value.shape[1]) for value in values
    ]
    size = sum(value.size for value in values)
    results = pl.pallas_call(
        functools.partial(ring_kernel, blocks),
        out_shape=[jax.ShapeDtypeStruct((2, *value.shape), value.dtype) for value in shaped],
        in_specs=[pl.BlockSpec(memory_space=pltpu.VMEM)] * blocks,
        out_specs=[pl.BlockSpec(memory_space=pltpu.VMEM)] * blocks,
        scratch_shapes=[
            pltpu.VMEM((2, count - 1, *value.shape[2:]), value.dtype) for value in shaped
        ]
        + [pltpu.VMEM((2, count - 2, *value.shape[2:]), value.dtype) for value in shaped]
        + [
            pltpu.SemaphoreType.DMA((2 * blocks, 2 * count - 2)),
            pltpu.SemaphoreType.DMA((2 * blocks, 2 * count - 2)),
            pltpu.SemaphoreType.DMA((2 * blocks, count)),
            pltpu.SemaphoreType.DMA((2 * blocks, count)),
        ],
        compiler_params=pltpu.CompilerParams(collective_id=identity, has_side_effects=True),
        cost_estimate=pl.CostEstimate(flops=size, bytes_accessed=6 * size, transcendentals=0),
        name="plane_sums",
    )(*shaped)
    return [
        result.reshape(2 * value.shape[0], value.shape[1]) for result, value in zip(results, values)
    ]


def core_send(left, rights, core):
    half = left.shape[1] // 2
    sent = lax.dynamic_slice_in_dim(left, (1 - core) * half, half, 1)
    return [to_core(contract_rows(sent, right).astype(jnp.bfloat16)) for right in rights]


def core_sum(left, rights, arrived, core):
    half = left.shape[1] // 2
    kept = lax.dynamic_slice_in_dim(left, core * half, half, 1)
    return [
        contract_rows(kept, right) + part.astype(jnp.float32)
        for right, part in zip(rights, arrived)
    ]


def start_grad(left, rights, core):
    other = core_send(left[1], rights[1], core)
    local = core_send(left[0], rights[0], core)
    summed = [
        part.astype(jnp.bfloat16) for part in core_sum(left[1], rights[1], other, core)
    ]
    return local, summed, [to_tensor(part) for part in summed]


def pair_grad(left, rights, local, passed, core):
    mine = [
        (part + more.astype(jnp.float32)).astype(jnp.bfloat16)
        for part, more in zip(core_sum(left, rights, local, core), passed)
    ]
    return jnp.concatenate(mine, 0)


def everywhere(value):
    value = value + to_core(value)
    value = value + to_tensor(value)
    for bit in (2, 4, 8):
        value = value + to_z(value, bit)
    return value


def trade_rows(value, own):
    share = value.shape[0] // 2
    arrived = to_tensor(lax.dynamic_slice_in_dim(value, (1 - own) * share, share, 0))
    kept = lax.dynamic_slice_in_dim(value, own * share, share, 0)
    return jnp.stack(
        [jnp.where(own == 0, kept, arrived), jnp.where(own == 0, arrived, kept)], 0
    )


def whole_sequence(
    tokens,
    d_output,
    lengths,
    ln1_gain,
    ln1_bias,
    w_qkv,
    qv_bias,
    w_out,
    bias_out,
    ln2_gain,
    ln2_bias,
    w_up,
    b_up,
    w_down,
    b_down,
):
    own = lax.axis_index("tensor")
    device = lax.axis_index("dp")
    core, y = device % 2, (device // 2) % 2
    slots, width = tokens.shape[1:]
    local_width = w_qkv.shape[2]
    hidden_local = w_up.shape[1]
    table = jnp.asarray(slope_rows())
    pairs = local_width // PAIR
    f32 = jnp.float32

    weight_qkv = w_qkv.transpose(1, 0, 2)
    biases = jnp.concatenate([qv_bias.reshape(-1), b_up])
    other_biases = to_tensor(biases)
    far_qkv = quarter_over_x(weight_qkv, y, core)
    qv = [b[: 2 * local_width].reshape(2, local_width).astype(f32) for b in (biases, other_biases)]
    ups = [b[2 * local_width :].astype(f32) for b in (biases, other_biases)]
    rows = [lax.dynamic_slice_in_dim(table, index * pairs, pairs, 0) for index in (own, 1 - own)]
    gain_one, shift_one = ln1_gain.astype(f32), ln1_bias.astype(f32)
    gain_two, shift_two = ln2_gain.astype(f32), ln2_bias.astype(f32)

    def pick(value):
        return lax.dynamic_index_in_dim(value, own, 0, keepdims=False)

    tokens_f = pick(tokens).astype(f32)
    length = pick(lengths)
    lanes = key_lanes(slots, length)
    normal_one, inverse_one = norm_parts(tokens_f)
    normed_one = (normal_one * gain_one + shift_one).astype(jnp.bfloat16)
    heads = []
    mixed = []

    def project(weights, half):
        query = (matmul(normed_one, weights[0]) + qv[half][0]).astype(jnp.bfloat16)
        keys = matmul(normed_one, weights[1]).astype(jnp.bfloat16)
        values = (matmul(normed_one, weights[2]) + qv[half][1]).astype(jnp.bfloat16)
        heads.append((query, keys, values))
        mixed.append(attention_out(query, keys, values, lanes, rows[half]))

    project(weight_qkv, 0)
    far_out = quarter_over_x(w_out, y, core, heads[0][0])
    far_up = quarter_over_x(w_up, y, core, heads[0][0])
    far_down = quarter_over_x(w_down, y, core, mixed[0])
    qkv = (weight_qkv, other_half(far_qkv, y, core))
    project(qkv[1], 1)
    out = (w_out, other_half(far_out, y, core))
    up = (w_up, other_half(far_up, y, core))
    down = (w_down, other_half(far_down, y, core))
    hidden = tokens_f + bias_out.astype(f32) + matmul(mixed[0], out[0]) + matmul(mixed[1], out[1])
    normal_two, inverse_two = norm_parts(hidden)
    normed_two = (normal_two * gain_two + shift_two).astype(jnp.bfloat16)
    acts = []
    for half in range(2):
        value, slope = gelu_parts(matmul(normed_two, up[half]) + ups[half])
        acts.append(
            lax.optimization_barrier((value.astype(jnp.bfloat16), slope.astype(jnp.bfloat16)))
        )

    valid = (jnp.arange(slots, dtype=jnp.int32) < length).astype(f32)[:, None]
    grad_out = pick(d_output).astype(f32) * valid
    grad_two = grad_out.astype(jnp.bfloat16)
    left_down, right_down = (acts[0][0], acts[1][0]), ([grad_two], [grad_two])
    local_down, sent_down, passed_down = start_grad(left_down, right_down, core)
    late_two = after(grad_two, *sent_down, *local_down)
    grad_pre = [
        (contract_cols(late_two, down[half]) * acts[half][1].astype(f32)).astype(jnp.bfloat16)
        for half in range(2)
    ]
    left_up, right_up = (normed_two, normed_two), ([grad_pre[0]], [grad_pre[1]])
    local_up, sent_up, passed_up = start_grad(left_up, right_up, core)
    late_pre = lax.optimization_barrier((*grad_pre, *sent_up, *local_up))
    grad_norm_two = contract_cols(late_pre[0], up[0]) + contract_cols(late_pre[1], up[1])
    grad_hidden = grad_out + norm_backward(grad_norm_two, normal_two, inverse_two, gain_two)
    grad_one = grad_hidden.astype(jnp.bfloat16)
    left_out, right_out = (mixed[0], mixed[1]), ([grad_one], [grad_one])
    local_out, sent_out, passed_out = start_grad(left_out, right_out, core)
    late_one = after(grad_one, *sent_out, *local_out)
    grads = [None, None]
    grad_attn = contract_cols(late_one, out[1]).astype(jnp.bfloat16)
    grads[1] = attention_grads(*heads[1], grad_attn, lanes, rows[1])
    other_qkv = core_send(normed_one, grads[1], core)
    sent_qkv = [
        part.astype(jnp.bfloat16) for part in core_sum(normed_one, grads[1], other_qkv, core)
    ]
    passed_qkv = [to_tensor(part) for part in sent_qkv]
    later_one = after(late_one, *sent_qkv)
    grad_attn = contract_cols(later_one, out[0]).astype(jnp.bfloat16)
    grads[0] = attention_grads(*heads[0], grad_attn, lanes, rows[0])
    local_qkv = core_send(normed_one, grads[0], core)
    grad_norm_one = sum(
        contract_cols(grads[half][part], qkv[half][part]) for half in range(2) for part in range(3)
    )
    grad_tokens = grad_hidden + norm_backward(grad_norm_one, normal_one, inverse_one, gain_one)
    grad_tokens = trade_rows(grad_tokens.astype(jnp.bfloat16), own)
    result = hidden + b_down.astype(f32) + matmul(acts[0][0], down[0]) + matmul(acts[1][0], down[1])
    output = trade_rows(result.astype(jnp.bfloat16), own)
    grad_wdown, grad_wup = plane_sums(
        [
            pair_grad(left_down[0], right_down[0], local_down, passed_down, core),
            pair_grad(left_up[0], right_up[0], local_up, passed_up, core),
        ],
        1,
    )
    mine_out = pair_grad(left_out[0], right_out[0], local_out, passed_out, core)
    mine_qkv = pair_grad(normed_one, grads[0], local_qkv, passed_qkv, core)
    grad_wout, grad_wqkv = plane_sums([mine_out, after(mine_qkv, grad_wdown)], 2)
    grad_wqkv = grad_wqkv.astype(f32).reshape(2, 3, width // 2, local_width)
    grad_wqkv = grad_wqkv.transpose(1, 0, 2, 3).reshape(3, width, local_width)

    def column_sum(value):
        return jnp.sum(value.astype(f32), 0)

    def in_place(parts):
        first = jnp.where(own == 0, parts[0], parts[1])
        second = jnp.where(own == 0, parts[1], parts[0])
        return jnp.concatenate([first, second], 0)

    small = [
        jnp.sum(grad_norm_one * normal_one, 0),
        jnp.sum(grad_norm_one, 0),
        jnp.sum(grad_norm_two * normal_two, 0),
        jnp.sum(grad_norm_two, 0),
        column_sum(grad_one),
        column_sum(grad_two),
        in_place([column_sum(grads[half][0]) for half in range(2)]),
        in_place([column_sum(grads[half][2]) for half in range(2)]),
        in_place([column_sum(grad_pre[half]) for half in range(2)]),
    ]
    small = everywhere(jnp.concatenate(small).reshape(-1, width))
    wide = [lax.dynamic_slice_in_dim(small[i], own * local_width, local_width, 0) for i in (6, 7)]
    grad_bup = lax.dynamic_slice_in_dim(
        small[8:].reshape(-1), own * hidden_local, hidden_local, 0
    )
    return (
        output,
        grad_tokens,
        small[0],
        small[1],
        grad_wqkv.transpose(1, 0, 2),
        jnp.stack(wide, 0),
        grad_wout.astype(f32),
        small[4],
        small[2],
        small[3],
        grad_wup.astype(f32),
        grad_bup,
        grad_wdown.astype(f32),
        small[5],
    )


def on_device(
    tokens,
    d_output,
    lengths,
    ln1_gain,
    ln1_bias,
    w_qkv,
    qv_bias,
    w_out,
    bias_out,
    ln2_gain,
    ln2_bias,
    w_up,
    b_up,
    w_down,
    b_down,
):
    parts = lax.axis_size("tensor")
    place = lax.axis_index("tensor")
    batches, slots, width = tokens.shape
    share = slots // parts
    row_start = place * share
    local_width = w_qkv.shape[2]
    hidden_local = w_up.shape[1]
    heads_local = local_width // HEAD_DIM
    scale = 1.0 / math.sqrt(HEAD_DIM)
    first_head = place * heads_local
    slopes = jnp.exp2(
        -8.0
        * ((first_head + jnp.arange(heads_local, dtype=jnp.int32)).astype(jnp.float32) + 1.0)
        / HEADS
    )
    weight_qkv = w_qkv.reshape(width, 3 * local_width)
    qkv_shift = jnp.concatenate(
        [
            qv_bias[0].astype(jnp.float32),
            jnp.zeros((local_width,), jnp.float32),
            qv_bias[1].astype(jnp.float32),
        ]
    )
    gain_one = ln1_gain.astype(jnp.float32)
    shift_one = ln1_bias.astype(jnp.float32)
    gain_two = ln2_gain.astype(jnp.float32)
    shift_two = ln2_bias.astype(jnp.float32)
    out_shift = bias_out.astype(jnp.float32)
    up_shift = b_up.astype(jnp.float32)
    down_shift = b_down.astype(jnp.float32)
    grad_qkv = jnp.zeros((width, 3 * local_width), jnp.float32)
    grad_qvb = jnp.zeros((2, local_width), jnp.float32)
    grad_wout = jnp.zeros((local_width, width), jnp.float32)
    grad_wup = jnp.zeros((width, hidden_local), jnp.float32)
    grad_bup = jnp.zeros((hidden_local,), jnp.float32)
    grad_wdown = jnp.zeros((hidden_local, width), jnp.float32)
    grad_gain_one = jnp.zeros((width,), jnp.float32)
    grad_shift_one = jnp.zeros((width,), jnp.float32)
    grad_gain_two = jnp.zeros((width,), jnp.float32)
    grad_shift_two = jnp.zeros((width,), jnp.float32)
    grad_out_shift = jnp.zeros((width,), jnp.float32)
    grad_down_shift = jnp.zeros((width,), jnp.float32)
    output_rows = []
    input_rows = []
    for index in range(batches):
        tokens_f = tokens[index].astype(jnp.float32)
        length = lengths[index]
        normal_one, inverse_one = norm_parts(tokens_f)
        normed_one = (normal_one * gain_one + shift_one).astype(jnp.bfloat16)
        projected = (matmul(normed_one, weight_qkv) + qkv_shift).astype(jnp.bfloat16)
        query = projected[:, :local_width].reshape(slots, heads_local, HEAD_DIM)
        keys = projected[:, local_width : 2 * local_width].reshape(slots, heads_local, HEAD_DIM)
        values = projected[:, 2 * local_width :].reshape(slots, heads_local, HEAD_DIM)
        attn = attention_forward(query, keys, values, length, slopes, scale)
        partial_value = matmul(attn, w_out)
        summed = lax.psum(partial_value.astype(jnp.bfloat16), "tensor").astype(jnp.float32)
        hidden_full = tokens_f + summed + out_shift
        normal_full, inverse_full = norm_parts(hidden_full)
        normed_two = (normal_full * gain_two + shift_two).astype(jnp.bfloat16)
        hidden_rows = lax.dynamic_slice_in_dim(hidden_full, row_start, share, 0)
        normal_two = lax.dynamic_slice_in_dim(normal_full, row_start, share, 0)
        inverse_two = lax.dynamic_slice_in_dim(inverse_full, row_start, share, 0)
        pre = matmul(normed_two, w_up) + up_shift
        act_value, act_slope = gelu_parts(pre)
        act = act_value.astype(jnp.bfloat16)
        mlp_part = lax.psum_scatter(
            matmul(act, w_down).astype(jnp.bfloat16), "tensor", scatter_dimension=0, tiled=True
        ).astype(jnp.float32)
        output_rows.append((hidden_rows + mlp_part + down_shift).astype(jnp.bfloat16))
        valid = (jnp.arange(slots, dtype=jnp.int32) < length).astype(jnp.float32)[:, None]
        grad_out = d_output[index].astype(jnp.float32) * valid
        grad_two = grad_out.astype(jnp.bfloat16)
        grad_wdown = grad_wdown + contract_rows(act, grad_two)
        grad_pre = (contract_cols(grad_two, w_down) * act_slope).astype(jnp.bfloat16)
        grad_wup = grad_wup + contract_rows(normed_two, grad_pre)
        grad_bup = grad_bup + jnp.sum(grad_pre.astype(jnp.float32), 0)
        grad_norm_two = lax.psum_scatter(
            contract_cols(grad_pre, w_up).astype(jnp.bfloat16),
            "tensor",
            scatter_dimension=0,
            tiled=True,
        ).astype(jnp.float32)
        grad_gain_two = grad_gain_two + jnp.sum(grad_norm_two * normal_two, 0)
        grad_shift_two = grad_shift_two + jnp.sum(grad_norm_two, 0)
        grad_out_rows = lax.dynamic_slice_in_dim(grad_out, row_start, share, 0)
        grad_hidden_rows = grad_out_rows + norm_backward(
            grad_norm_two, normal_two, inverse_two, gain_two
        )
        grad_one_rows = grad_hidden_rows.astype(jnp.bfloat16)
        grad_down_shift = grad_down_shift + jnp.sum(
            lax.dynamic_slice_in_dim(grad_two, row_start, share, 0).astype(jnp.float32), 0
        )
        grad_out_shift = grad_out_shift + jnp.sum(grad_one_rows.astype(jnp.float32), 0)
        grad_one = lax.all_gather(grad_one_rows, "tensor", axis=0, tiled=True)
        grad_wout = grad_wout + contract_rows(attn, grad_one)
        grad_attn = (
            contract_cols(grad_one, w_out)
            .astype(jnp.bfloat16)
            .reshape(slots, heads_local, HEAD_DIM)
        )
        grad_query, grad_keys, grad_values = attention_backward(
            query, keys, values, grad_attn, length, slopes, scale
        )
        grad_proj = jnp.concatenate([grad_query, grad_keys, grad_values], 1)
        grad_qkv = grad_qkv + contract_rows(normed_one, grad_proj)
        grad_qvb = grad_qvb + jnp.stack(
            [
                jnp.sum(grad_query.astype(jnp.float32), 0),
                jnp.sum(grad_values.astype(jnp.float32), 0),
            ],
            0,
        )
        grad_norm_one = lax.psum_scatter(
            contract_cols(grad_proj, weight_qkv).astype(jnp.bfloat16),
            "tensor",
            scatter_dimension=0,
            tiled=True,
        ).astype(jnp.float32)
        normal_one_rows = lax.dynamic_slice_in_dim(normal_one, row_start, share, 0)
        inverse_one_rows = lax.dynamic_slice_in_dim(inverse_one, row_start, share, 0)
        grad_gain_one = grad_gain_one + jnp.sum(grad_norm_one * normal_one_rows, 0)
        grad_shift_one = grad_shift_one + jnp.sum(grad_norm_one, 0)
        input_rows.append(
            (
                grad_hidden_rows
                + norm_backward(grad_norm_one, normal_one_rows, inverse_one_rows, gain_one)
            ).astype(jnp.bfloat16)
        )
    grad_qkv, grad_qvb, grad_wout, grad_wup, grad_bup, grad_wdown = (
        lax.psum(grad_qkv.astype(jnp.bfloat16), "dp").astype(jnp.float32),
        lax.psum(grad_qvb.astype(jnp.bfloat16), "dp").astype(jnp.float32),
        lax.psum(grad_wout.astype(jnp.bfloat16), "dp").astype(jnp.float32),
        lax.psum(grad_wup.astype(jnp.bfloat16), "dp").astype(jnp.float32),
        lax.psum(grad_bup.astype(jnp.bfloat16), "dp").astype(jnp.float32),
        lax.psum(grad_wdown.astype(jnp.bfloat16), "dp").astype(jnp.float32),
    )
    (
        grad_gain_one,
        grad_shift_one,
        grad_gain_two,
        grad_shift_two,
        grad_out_shift,
        grad_down_shift,
    ) = lax.psum(
        (
            grad_gain_one,
            grad_shift_one,
            grad_gain_two,
            grad_shift_two,
            grad_out_shift,
            grad_down_shift,
        ),
        ("dp", "tensor"),
    )
    return (
        jnp.stack(output_rows, 0),
        jnp.stack(input_rows, 0),
        grad_gain_one,
        grad_shift_one,
        grad_qkv.reshape(width, 3, local_width),
        grad_qvb,
        grad_wout,
        grad_out_shift,
        grad_gain_two,
        grad_shift_two,
        grad_wup,
        grad_bup,
        grad_wdown,
        grad_down_shift,
    )


def solution(mesh):
    whole = mesh.shape["tensor"] == 2 and mesh.shape["dp"] == 2 * len(RING)
    return jax.shard_map(
        whole_sequence if whole else on_device,
        mesh=mesh,
        in_specs=(
            P("dp", None, None),
            P("dp", None, None),
            P("dp"),
            P(),
            P(),
            P(None, None, "tensor"),
            P(None, "tensor"),
            P("tensor", None),
            P(),
            P(),
            P(),
            P(None, "tensor"),
            P("tensor"),
            P("tensor", None),
            P(),
        ),
        out_specs=(
            P("dp", "tensor", None),
            P("dp", "tensor", None),
            P(),
            P(),
            P(None, None, "tensor"),
            P(None, "tensor"),
            P("tensor", None),
            P(),
            P(),
            P(),
            P(None, "tensor"),
            P("tensor"),
            P("tensor", None),
            P(),
        ),
        check_vma=False,
    )
```

```python
import functools
import math

import jax
import jax.numpy as jnp
import numpy as np
from jax import lax
from jax.experimental import pallas as pl
from jax.experimental.pallas import tpu as pltpu
from jax.sharding import PartitionSpec as P

HEADS = 16
HEAD_DIM = 64


epsilon = 1e-05
root_two_pi = math.sqrt(2.0 / math.pi)
masked_score = -1e30


def matmul(left, right):
    return jnp.dot(left, right, preferred_element_type=jnp.float32)


def contract_rows(left, right):
    return lax.dot_general(
        left, right, (((0,), (0,)), ((), ())), preferred_element_type=jnp.float32
    )


def contract_cols(left, right):
    return lax.dot_general(
        left, right, (((1,), (1,)), ((), ())), preferred_element_type=jnp.float32
    )


def norm_parts(values):
    centre = jnp.mean(values, -1, keepdims=True)
    shifted = values - centre
    inverse = lax.rsqrt(jnp.mean(shifted * shifted, -1, keepdims=True) + epsilon)
    return (shifted * inverse, inverse)


def norm_backward(grad_normed, normal, inverse, gain):
    scaled = grad_normed * gain
    return inverse * (
        scaled
        - jnp.mean(scaled, -1, keepdims=True)
        - normal * jnp.mean(scaled * normal, -1, keepdims=True)
    )


def gelu_parts(pre):
    tangent = jnp.tanh(root_two_pi * (pre + 0.044715 * pre * pre * pre))
    value = 0.5 * pre * (1.0 + tangent)
    slope = 0.5 * (1.0 + tangent) + 0.5 * pre * (1.0 - tangent * tangent) * root_two_pi * (
        1.0 + 3.0 * 0.044715 * pre * pre
    )
    return (value, slope)


def block_probs(query_rows, key_rows, start, length, slopes, scale):
    rows = query_rows.shape[0]
    cols = key_rows.shape[0]
    products = jnp.einsum("ihd,jhd->hij", query_rows, key_rows, preferred_element_type=jnp.float32)
    key_place = jnp.arange(cols, dtype=jnp.int32)
    distance = (start + jnp.arange(rows, dtype=jnp.int32))[:, None] - key_place[None, :]
    scores = products * scale - slopes[:, None, None] * distance.astype(jnp.float32)[None]
    allowed = (distance >= 0) & (key_place[None, :] < length)
    masked = jnp.where(allowed[None], scores, masked_score)
    highest = jnp.max(masked, -1, keepdims=True)
    exponent = jnp.exp(masked - highest)
    return exponent / jnp.sum(exponent, -1, keepdims=True)


def attention_forward(query, keys, values, length, slopes, scale):
    slots = query.shape[0]
    block = min(512, slots)
    outputs = []
    for number in range(slots // block):
        start = number * block
        probs = block_probs(query[start : start + block], keys, start, length, slopes, scale)
        mixed = jnp.einsum(
            "hij,jhd->ihd", probs.astype(jnp.bfloat16), values, preferred_element_type=jnp.float32
        )
        outputs.append(mixed.reshape(block, -1).astype(jnp.bfloat16))
    return jnp.concatenate(outputs, 0)


def attention_backward(query, keys, values, grad_attn, length, slopes, scale):
    slots, heads_local, head_width = query.shape
    block = min(512, slots)
    grad_keys = jnp.zeros((slots, heads_local, head_width), jnp.float32)
    grad_values = jnp.zeros((slots, heads_local, head_width), jnp.float32)
    query_parts = []
    for number in range(slots // block):
        start = number * block
        query_rows = query[start : start + block]
        grad_rows = grad_attn[start : start + block]
        probs = block_probs(query_rows, keys, start, length, slopes, scale)
        grad_probs = jnp.einsum(
            "ihd,jhd->hij", grad_rows, values, preferred_element_type=jnp.float32
        )
        delta = jnp.sum(probs * grad_probs, -1, keepdims=True)
        grad_scores = (probs * (grad_probs - delta)).astype(jnp.bfloat16)
        part_query = (
            jnp.einsum("hij,jhd->ihd", grad_scores, keys, preferred_element_type=jnp.float32)
            * scale
        )
        part_keys = (
            jnp.einsum("hij,ihd->jhd", grad_scores, query_rows, preferred_element_type=jnp.float32)
            * scale
        )
        part_values = jnp.einsum(
            "hij,ihd->jhd",
            probs.astype(jnp.bfloat16),
            grad_rows,
            preferred_element_type=jnp.float32,
        )
        part_query, part_keys, part_values = (part_query, part_keys, part_values)
        query_parts.append(part_query)
        grad_keys = grad_keys.at[:slots].add(part_keys)
        grad_values = grad_values.at[:slots].add(part_values)
    grad_query = jnp.concatenate(query_parts, 0).reshape(slots, -1).astype(jnp.bfloat16)
    return (
        grad_query,
        grad_keys.reshape(slots, -1).astype(jnp.bfloat16),
        grad_values.reshape(slots, -1).astype(jnp.bfloat16),
    )


QUERY_BLOCK = 256
KEY_BLOCK = 1024
PAIR = 128
NT = (((1,), (1,)), ((), ()))
TN = (((0,), (0,)), ((), ()))


def mm(left, right, dims=(((1,), (0,)), ((), ()))):
    return lax.dot_general(left, right, dims, preferred_element_type=jnp.float32)


def low_lanes(rows):
    return lax.broadcasted_iota(jnp.int32, (rows, PAIR), 1) < HEAD_DIM


def slope_rows():
    table = np.zeros((HEADS // 2, 8, PAIR), np.float64)
    for head in range(HEADS):
        rest = np.float64(np.float32(2.0 ** (-8.0 * (head + 1) / HEADS)))
        base = HEAD_DIM * (1 - head % 2)
        for part in range(3):
            piece = np.float64(np.asarray(rest).astype(jnp.bfloat16))
            rest = rest - piece
            table[head // 2, head % 2, base + part] = 32.0 * piece
            table[head // 2, head % 2, base + 3 + part] = piece
        table[head // 2, head % 2, base + 6] = 1.0
    return table.astype(jnp.bfloat16)


def key_lanes(slots, length):
    place = jnp.arange(slots, dtype=jnp.int32)[:, None]
    lane = jnp.arange(PAIR, dtype=jnp.int32)[None, :] % HEAD_DIM
    high = (place // 32).astype(jnp.float32)
    low = (place % 32).astype(jnp.float32)
    mask = jnp.where(place < length, 0.0, masked_score)
    return jnp.where(
        lane < 3, high, jnp.where(lane < 6, low, jnp.where(lane == 6, mask, 0.0))
    ).astype(jnp.bfloat16)


def forward_kernel(
    q_ref, k_ref, v_ref, lanes_ref, rows_ref, o_ref, level_ref, key0, key1, val0, val1
):
    slots = q_ref.shape[0]
    block = QUERY_BLOCK
    low = low_lanes(slots)
    zero = jnp.zeros((slots, PAIR), jnp.bfloat16)
    one = jnp.ones((slots, PAIR), jnp.bfloat16)
    key0[...] = jnp.where(low, k_ref[...], lanes_ref[...])
    key1[...] = jnp.where(low, lanes_ref[...], k_ref[...])
    val0[:, :PAIR] = jnp.where(low, v_ref[...], zero)
    val0[:, PAIR:] = jnp.where(low, one, zero)
    val1[:, :PAIR] = jnp.where(low, zero, v_ref[...])
    val1[:, PAIR:] = jnp.where(low, zero, one)
    low_block = low_lanes(block)
    causal = lax.broadcasted_iota(jnp.int32, (block, block), 1) <= lax.broadcasted_iota(
        jnp.int32, (block, block), 0
    )
    for number in range(slots // block):
        start = number * block
        rows = q_ref[start : start + block, :] * jnp.bfloat16(0.125)
        total = None
        tops = []
        for head, (key, val) in enumerate(((key0, val0), (key1, val1))):
            extra = jnp.broadcast_to(rows_ref[0, head : head + 1, :], (block, PAIR))
            query = jnp.where(low_block, rows, extra) if head == 0 else jnp.where(
                low_block, extra, rows
            )
            own = jnp.where(causal, mm(query, key[start : start + block, :], NT), masked_score)
            highest = jnp.max(own, 1, keepdims=True)
            if start:
                past = mm(query, key[:start, :], NT)
                highest = jnp.maximum(highest, jnp.max(past, 1, keepdims=True))
                part = mm(jnp.exp(past - highest).astype(jnp.bfloat16), val[:start, :])
                total = part if total is None else total + part
            part = mm(jnp.exp(own - highest).astype(jnp.bfloat16), val[start : start + block, :])
            total = part if total is None else total + part
            tops.append(highest)
        o_ref[start : start + block, :] = (total[:, :PAIR] / total[:, PAIR:]).astype(jnp.bfloat16)
        level = (jnp.where(low_block, tops[0], tops[1]) + jnp.log(total[:, PAIR:])).T
        level_ref[0, 0:1, start : start + block] = level[0:1, :]
        level_ref[0, 1:2, start : start + block] = level[HEAD_DIM : HEAD_DIM + 1, :]


def backward_kernel(
    q_ref, k_ref, v_ref, o_ref, g_ref, level_ref, lanes_ref, rows_ref, dq_ref, dk_ref, dv_ref,
    key0, key1, val0, val1, bare0, bare1, total_k, total_v,
):
    slots = q_ref.shape[0]
    block = QUERY_BLOCK
    piece = KEY_BLOCK
    low = low_lanes(slots)
    zero = jnp.zeros((slots, PAIR), jnp.bfloat16)
    key0[...] = jnp.where(low, k_ref[...], lanes_ref[...])
    key1[...] = jnp.where(low, lanes_ref[...], k_ref[...])
    bare0[...] = jnp.where(low, k_ref[...], zero)
    bare1[...] = jnp.where(low, zero, k_ref[...])
    val0[...] = jnp.where(low, v_ref[...], zero)
    val1[...] = jnp.where(low, zero, v_ref[...])
    low_block = low_lanes(block)
    nil = jnp.zeros((block, PAIR), jnp.bfloat16)
    causal = lax.broadcasted_iota(jnp.int32, (block, block), 0) <= lax.broadcasted_iota(
        jnp.int32, (block, block), 1
    )
    for number in reversed(range(slots // block)):
        start = number * block
        stop = start + block
        rows = q_ref[start:stop, :] * jnp.bfloat16(0.125)
        grad = g_ref[start:stop, :]
        shares = (grad.astype(jnp.float32) * o_ref[start:stop, :].astype(jnp.float32)).T
        deltas = [
            jnp.sum(shares[head * HEAD_DIM : (head + 1) * HEAD_DIM, :], 0, keepdims=True)
            for head in range(2)
        ]
        levels = [level_ref[0, head : head + 1, start:stop] for head in range(2)]
        extras = [jnp.broadcast_to(rows_ref[0, h : h + 1, :], (block, PAIR)) for h in range(2)]
        queries = (
            jnp.where(low_block, rows, extras[0]),
            jnp.where(low_block, extras[1], rows),
        )
        grads = jnp.concatenate(
            [jnp.where(low_block, grad, nil), jnp.where(low_block, nil, grad)], 0
        )
        both = jnp.concatenate(
            [jnp.where(low_block, rows, nil), jnp.where(low_block, nil, rows)], 0
        )
        grad_query = None
        for begin in range(0, stop, min(piece, stop)):
            end = min(begin + piece, stop)
            probs, scores = [], []
            for head, (key, val, bare) in enumerate(((key0, val0, bare0), (key1, val1, bare1))):
                score = mm(key[begin:end, :], queries[head], NT)
                if end > start:
                    own = jnp.where(causal, score[start - begin :], masked_score)
                    score = jnp.concatenate([score[: start - begin], own], 0) if start > begin else own
                prob = jnp.exp(score - levels[head])
                grad_prob = mm(val[begin:end, :], grad, NT)
                grad_score = (prob * (grad_prob - deltas[head])).astype(jnp.bfloat16)
                probs.append(prob.astype(jnp.bfloat16))
                scores.append(grad_score)
                part = mm(grad_score, bare[begin:end, :], TN)
                grad_query = part if grad_query is None else grad_query + part
            part_v = mm(jnp.concatenate(probs, 1), grads)
            part_k = mm(jnp.concatenate(scores, 1), both)
            if stop == slots:
                total_v[begin:end, :] = part_v
                total_k[begin:end, :] = part_k
            else:
                total_v[begin:end, :] += part_v
                total_k[begin:end, :] += part_k
        dq_ref[start:stop, :] = (grad_query * 0.125).astype(jnp.bfloat16)
    dk_ref[...] = total_k[...].astype(jnp.bfloat16)
    dv_ref[...] = total_v[...].astype(jnp.bfloat16)


def pair_specs(slots):
    part = pl.BlockSpec((slots, PAIR), lambda pair: (0, pair))
    lanes = pl.BlockSpec((slots, PAIR), lambda pair: (0, 0))
    rows = pl.BlockSpec((1, 8, PAIR), lambda pair: (pair, 0, 0))
    levels = pl.BlockSpec((1, 8, slots), lambda pair: (pair, 0, 0))
    return part, lanes, rows, levels


def attention_out(query, keys, values, lanes, rows):
    slots, columns = query.shape
    part, lane_spec, row_spec, level_spec = pair_specs(slots)
    pairs = columns // PAIR
    half = slots * slots * PAIR * pairs
    return pl.pallas_call(
        forward_kernel,
        grid=(pairs,),
        out_shape=(
            jax.ShapeDtypeStruct((slots, columns), jnp.bfloat16),
            jax.ShapeDtypeStruct((pairs, 8, slots), jnp.float32),
        ),
        in_specs=[part, part, part, lane_spec, row_spec],
        out_specs=(part, level_spec),
        scratch_shapes=[pltpu.VMEM((slots, PAIR), jnp.bfloat16)] * 2
        + [pltpu.VMEM((slots, 2 * PAIR), jnp.bfloat16)] * 2,
        cost_estimate=pl.CostEstimate(
            flops=8 * half, bytes_accessed=8 * slots * columns, transcendentals=slots * slots * pairs
        ),
        name="attention_out",
    )(query, keys, values, lanes, rows)


def attention_grads(query, keys, values, mixed, levels, grad, lanes, rows):
    slots, columns = query.shape
    part, lane_spec, row_spec, level_spec = pair_specs(slots)
    pairs = columns // PAIR
    half = slots * slots * PAIR * pairs
    shape = jax.ShapeDtypeStruct((slots, columns), jnp.bfloat16)
    return pl.pallas_call(
        backward_kernel,
        grid=(pairs,),
        out_shape=(shape, shape, shape),
        in_specs=[part, part, part, part, part, level_spec, lane_spec, row_spec],
        out_specs=(part, part, part),
        scratch_shapes=[pltpu.VMEM((slots, PAIR), jnp.bfloat16)] * 6
        + [pltpu.VMEM((slots, PAIR), jnp.float32)] * 2,
        cost_estimate=pl.CostEstimate(
            flops=20 * half,
            bytes_accessed=14 * slots * columns,
            transcendentals=slots * slots * pairs,
        ),
        name="attention_grads",
    )(query, keys, values, mixed, grad, levels, lanes, rows)


RING = ((0, 0), (1, 0), (2, 0), (3, 0), (3, 1), (2, 1), (1, 1), (0, 1))


def device_of(z, y, core):
    return (z * 2 + y) * 2 + core


def to_tensor(value):
    return lax.ppermute(value, "tensor", [(0, 1), (1, 0)])


def to_core(value):
    return lax.ppermute(value, "dp", [(i, i ^ 1) for i in range(2 * len(RING))])


def rows_at(value, start, size):
    return lax.dynamic_slice_in_dim(value, start, size, value.ndim - 2)


def after(value, *earlier):
    return lax.optimization_barrier((value, *earlier))[0]


def piece_over_x(weight, index, pieces, *earlier):
    size = weight.shape[-2] // pieces
    return to_tensor(after(rows_at(weight, index * size, size), *earlier))


def both_cores(value, core, axis):
    beside = to_core(value)
    first = jnp.where(core == 0, value, beside)
    second = jnp.where(core == 0, beside, value)
    return jnp.concatenate([first, second], axis)


def ring_kernel(blocks, has_small, has_tie, *refs):
    count = len(RING)
    values, refs = refs[:blocks], refs[blocks:]
    if has_small:
        small_ref, refs = refs[0], refs[1:]
    refs = refs[has_tie:]
    results, refs = refs[:blocks], refs[blocks:]
    if has_small:
        small_out, refs = refs[0], refs[1:]
    slots, refs = refs[:blocks], refs[blocks:]
    sums, refs = refs[:blocks], refs[blocks:]
    send_sems, recv_sems, swap_send_sems, swap_recv_sems = refs[:4]
    if has_small:
        small_slots, small_sums, small_send_sems, small_recv_sems = refs[4:]
    device = lax.axis_index("dp")
    core, y, z = lax.rem(device, 2), lax.rem(device // 2, 2), device // 4
    place = z * (1 - y) + (count - 1 - z) * y

    def at_place(where):
        side = where // 4
        return {"dp": device_of(where * (1 - side) + (count - 1 - where) * side, side, core)}

    nexts = (at_place(lax.rem(place + 1, count)), at_place(lax.rem(place + count - 1, count)))
    partner = {"dp": device + 1 - 2 * core}
    barrier = pltpu.get_barrier_semaphore()
    greeted = [*nexts, partner]
    if has_small:
        low_z = lax.rem(z, 2)
        small_targets = [
            partner,
            {"tensor": 1 - lax.axis_index("tensor")},
            {"dp": device + 2 - 4 * y},
            {"dp": device + 4 - 8 * low_z},
            {"dp": device + 8 - 16 * (z // 2)},
        ]
        greeted += small_targets[1:]
    for target in greeted:
        pl.semaphore_signal(barrier, inc=1, device_id=target, device_id_type=pl.DeviceIdType.MESH)
    pl.semaphore_wait(barrier, len(greeted))

    streams = [(array, way) for array in range(blocks) for way in range(2)]

    def block(way, offset):
        return lax.rem(place - (1, -1)[way] * offset + 2 * count, count)

    def send(array, way, step, source, target):
        index = 2 * array + way
        copy = pltpu.make_async_remote_copy(
            src_ref=source,
            dst_ref=target,
            send_sem=send_sems.at[index, step],
            recv_sem=recv_sems.at[index, step],
            device_id=nexts[way],
            device_id_type=pl.DeviceIdType.MESH,
        )
        copy.start()
        return copy

    def swap(array, way, step, offset):
        index = 2 * array + way
        done = results[array].at[core, way, block(way, offset)]
        copy = pltpu.make_async_remote_copy(
            src_ref=done,
            dst_ref=done,
            send_sem=swap_send_sems.at[index, step],
            recv_sem=swap_recv_sems.at[index, step],
            device_id=partner,
            device_id_type=pl.DeviceIdType.MESH,
        )
        copy.start()
        return copy

    def exchange(turn):
        copy = pltpu.make_async_remote_copy(
            src_ref=small_ref if turn == 0 else small_sums.at[turn - 1],
            dst_ref=small_slots.at[turn],
            send_sem=small_send_sems.at[turn],
            recv_sem=small_recv_sems.at[turn],
            device_id=small_targets[turn],
            device_id_type=pl.DeviceIdType.MESH,
        )
        copy.start()
        return copy

    def take_exchange(turn):
        exchanges[turn].wait_recv()
        total = (small_ref[...] if turn == 0 else small_sums[turn - 1]) + small_slots[turn]
        if turn == len(small_targets) - 1:
            small_out[...] = total
        else:
            small_sums[turn] = total
            exchanges.append(exchange(turn + 1))

    flying, swaps, started = {}, [], []
    exchanges = [exchange(0)] if has_small else []
    for array, way in streams:
        copy = send(array, way, 0, values[array].at[way, block(way, 0)], slots[array].at[way, 0])
        flying[array, way] = copy
        started.append(copy)
    for step in range(1, 2 * count - 2):
        if has_small and step % 2 == 0 and step // 2 <= len(small_targets):
            take_exchange(step // 2 - 1)
        for array, way in streams:
            flying[array, way].wait_recv()
            if step < count:
                total = values[array][way, block(way, step)].astype(jnp.float32) + slots[array][
                    way, step - 1
                ].astype(jnp.float32)
                total = total.astype(jnp.bfloat16)
            if step < count - 1:
                sums[array][way, step - 1] = total
                source, target = sums[array].at[way, step - 1], slots[array].at[way, step]
            else:
                if step == count - 1:
                    results[array][core, way, block(way, step)] = total
                source = target = results[array].at[core, way, block(way, step)]
            copy = send(array, way, step, source, target)
            flying[array, way] = copy
            started.append(copy)
            if step >= count - 1:
                swaps.append(swap(array, way, step - count + 1, step))
    for array, way in streams:
        flying[array, way].wait_recv()
        swaps.append(swap(array, way, count - 1, 2 * count - 2))
    for copy in started + exchanges:
        copy.wait_send()
    for copy in swaps:
        copy.wait()


def plane_sums(values, identity, small=None, tie=None):
    count = len(RING)
    blocks = len(values)
    shaped = [
        value.reshape(2, count, value.shape[0] // (2 * count), value.shape[1]) for value in values
    ]
    size = sum(value.size for value in values)
    vmem = pl.BlockSpec(memory_space=pltpu.VMEM)
    inputs, in_specs = list(shaped), [vmem] * blocks
    shapes = [jax.ShapeDtypeStruct((2, *value.shape), value.dtype) for value in shaped]
    scratch = [pltpu.VMEM((2, count - 1, *value.shape[2:]), value.dtype) for value in shaped]
    scratch += [pltpu.VMEM((2, count - 2, *value.shape[2:]), value.dtype) for value in shaped]
    scratch += [pltpu.SemaphoreType.DMA((2 * blocks, 2 * count - 2))] * 2
    scratch += [pltpu.SemaphoreType.DMA((2 * blocks, count))] * 2
    if small is not None:
        inputs.append(small)
        in_specs.append(vmem)
        shapes.append(jax.ShapeDtypeStruct(small.shape, small.dtype))
        scratch += [pltpu.VMEM((5, *small.shape), small.dtype)] * 2
        scratch += [pltpu.SemaphoreType.DMA((5,))] * 2
    if tie is not None:
        inputs.append(tie)
        in_specs.append(pl.BlockSpec(memory_space=pl.ANY))
    results = pl.pallas_call(
        functools.partial(ring_kernel, blocks, small is not None, int(tie is not None)),
        out_shape=shapes,
        in_specs=in_specs,
        out_specs=[vmem] * len(shapes),
        scratch_shapes=scratch,
        compiler_params=pltpu.CompilerParams(collective_id=identity, has_side_effects=True),
        cost_estimate=pl.CostEstimate(flops=size, bytes_accessed=6 * size, transcendentals=0),
        name="plane_sums",
    )(*inputs)
    sums = [
        result.reshape(2 * value.shape[0], value.shape[1]) for result, value in zip(results, values)
    ]
    return sums if small is None else (sums, results[-1])


def core_send(left, rights, core):
    half = left.shape[1] // 2
    sent = lax.dynamic_slice_in_dim(left, (1 - core) * half, half, 1)
    return [to_core(contract_rows(sent, right).astype(jnp.bfloat16)) for right in rights]


def core_sum(left, rights, arrived, core):
    half = left.shape[1] // 2
    kept = lax.dynamic_slice_in_dim(left, core * half, half, 1)
    return [
        contract_rows(kept, right) + part.astype(jnp.float32)
        for right, part in zip(rights, arrived)
    ]


def start_grad(left, rights, core):
    other = core_send(left[1], rights[1], core)
    local = core_send(left[0], rights[0], core)
    summed = [
        part.astype(jnp.bfloat16) for part in core_sum(left[1], rights[1], other, core)
    ]
    return local, summed, [to_tensor(part) for part in summed]


def pair_grad(left, rights, local, passed, core):
    mine = [
        (part + more.astype(jnp.float32)).astype(jnp.bfloat16)
        for part, more in zip(core_sum(left, rights, local, core), passed)
    ]
    return mine


def trade_rows(value, own):
    share = value.shape[0] // 2
    arrived = to_tensor(lax.dynamic_slice_in_dim(value, (1 - own) * share, share, 0))
    kept = lax.dynamic_slice_in_dim(value, own * share, share, 0)
    return jnp.stack(
        [jnp.where(own == 0, kept, arrived), jnp.where(own == 0, arrived, kept)], 0
    )


def whole_sequence(
    tokens,
    d_output,
    lengths,
    ln1_gain,
    ln1_bias,
    w_qkv,
    qv_bias,
    w_out,
    bias_out,
    ln2_gain,
    ln2_bias,
    w_up,
    b_up,
    w_down,
    b_down,
):
    own = lax.axis_index("tensor")
    device = lax.axis_index("dp")
    core = device % 2
    slots, width = tokens.shape[1:]
    local_width = w_qkv.shape[2]
    hidden_local = w_up.shape[1]
    table = jnp.asarray(slope_rows())
    pairs = local_width // PAIR
    f32 = jnp.float32

    weight_qkv = w_qkv.transpose(1, 0, 2)
    biases = jnp.concatenate([qv_bias.reshape(-1), b_up])
    other_biases = to_tensor(biases)
    far_up = piece_over_x(w_up, device, 2 * len(RING))
    far_qkv = piece_over_x(weight_qkv, core, 2)
    qv = [b[: 2 * local_width].reshape(2, local_width).astype(f32) for b in (biases, other_biases)]
    ups = [b[2 * local_width :].astype(f32) for b in (biases, other_biases)]
    rows = [lax.dynamic_slice_in_dim(table, index * pairs, pairs, 0) for index in (own, 1 - own)]
    gain_one, shift_one = ln1_gain.astype(f32), ln1_bias.astype(f32)
    gain_two, shift_two = ln2_gain.astype(f32), ln2_bias.astype(f32)

    def pick(value):
        return lax.dynamic_index_in_dim(value, own, 0, keepdims=False)

    tokens_f = pick(tokens).astype(f32)
    length = pick(lengths)
    lanes = key_lanes(slots, length)
    normal_one, inverse_one = norm_parts(tokens_f)
    normed_one = (normal_one * gain_one + shift_one).astype(jnp.bfloat16)
    heads = []
    mixed = []
    levels = []

    def project(weights, half):
        query = (matmul(normed_one, weights[0]) + qv[half][0]).astype(jnp.bfloat16)
        keys = matmul(normed_one, weights[1]).astype(jnp.bfloat16)
        values = (matmul(normed_one, weights[2]) + qv[half][1]).astype(jnp.bfloat16)
        heads.append((query, keys, values))
        attn, level = attention_out(query, keys, values, lanes, rows[half])
        mixed.append(attn)
        levels.append(level)

    project(weight_qkv, 0)
    far_down = piece_over_x(w_down, device, 2 * len(RING), heads[0][0])
    far_out = piece_over_x(w_out, core, 2, heads[0][0])
    up = (w_up, lax.all_gather(far_up, "dp", axis=0, tiled=True))
    down = (w_down, lax.all_gather(far_down, "dp", axis=0, tiled=True))
    qkv = (weight_qkv, both_cores(far_qkv, core, 1))
    project(qkv[1], 1)
    out = (w_out, both_cores(far_out, core, 0))
    hidden = tokens_f + bias_out.astype(f32) + matmul(mixed[0], out[0]) + matmul(mixed[1], out[1])
    normal_two, inverse_two = norm_parts(hidden)
    normed_two = (normal_two * gain_two + shift_two).astype(jnp.bfloat16)
    acts = []
    for half in range(2):
        value, slope = gelu_parts(matmul(normed_two, up[half]) + ups[half])
        acts.append(
            lax.optimization_barrier((value.astype(jnp.bfloat16), slope.astype(jnp.bfloat16)))
        )

    valid = (jnp.arange(slots, dtype=jnp.int32) < length).astype(f32)[:, None]
    grad_out = pick(d_output).astype(f32) * valid
    grad_two = grad_out.astype(jnp.bfloat16)
    left_down, right_down = (acts[0][0], acts[1][0]), ([grad_two], [grad_two])
    local_down, sent_down, passed_down = start_grad(left_down, right_down, core)
    late_two = after(grad_two, *sent_down, *local_down)
    grad_pre = [
        (contract_cols(late_two, down[half]) * acts[half][1].astype(f32)).astype(jnp.bfloat16)
        for half in range(2)
    ]
    left_up, right_up = (normed_two, normed_two), ([grad_pre[0]], [grad_pre[1]])
    local_up, sent_up, passed_up = start_grad(left_up, right_up, core)
    late_pre = lax.optimization_barrier((*grad_pre, *sent_up, *local_up))
    grad_norm_two = contract_cols(late_pre[0], up[0]) + contract_cols(late_pre[1], up[1])
    grad_hidden = grad_out + norm_backward(grad_norm_two, normal_two, inverse_two, gain_two)
    grad_one = grad_hidden.astype(jnp.bfloat16)
    left_out, right_out = (mixed[0], mixed[1]), ([grad_one], [grad_one])
    local_out, sent_out, passed_out = start_grad(left_out, right_out, core)
    late_one = after(grad_one, *sent_out, *local_out)
    grads = [None, None]
    grad_attn = contract_cols(late_one, out[1]).astype(jnp.bfloat16)
    grads[1] = attention_grads(
        *heads[1], mixed[1], levels[1], grad_attn, lanes, rows[1]
    )
    other_qkv = core_send(normed_one, grads[1], core)
    sent_qkv = [
        part.astype(jnp.bfloat16) for part in core_sum(normed_one, grads[1], other_qkv, core)
    ]
    passed_qkv = [to_tensor(part) for part in sent_qkv]
    later_one = after(late_one, *sent_qkv)
    grad_attn = contract_cols(later_one, out[0]).astype(jnp.bfloat16)
    grads[0] = attention_grads(
        *heads[0], mixed[0], levels[0], grad_attn, lanes, rows[0]
    )
    local_qkv = core_send(normed_one, grads[0], core)
    grad_norm_one = sum(
        contract_cols(grads[half][part], qkv[half][part]) for half in range(2) for part in range(3)
    )
    grad_tokens = grad_hidden + norm_backward(grad_norm_one, normal_one, inverse_one, gain_one)
    grad_tokens = trade_rows(grad_tokens.astype(jnp.bfloat16), own)
    result = hidden + b_down.astype(f32) + matmul(acts[0][0], down[0]) + matmul(acts[1][0], down[1])
    output = trade_rows(result.astype(jnp.bfloat16), own)
    def column_sum(value):
        return jnp.sum(value.astype(f32), 0)

    def in_place(parts):
        first = jnp.where(own == 0, parts[0], parts[1])
        second = jnp.where(own == 0, parts[1], parts[0])
        return jnp.concatenate([first, second], 0)

    small = [
        jnp.sum(grad_norm_one * normal_one, 0),
        jnp.sum(grad_norm_one, 0),
        jnp.sum(grad_norm_two * normal_two, 0),
        jnp.sum(grad_norm_two, 0),
        column_sum(grad_one),
        column_sum(grad_two),
        in_place([column_sum(grads[half][0]) for half in range(2)]),
        in_place([column_sum(grads[half][2]) for half in range(2)]),
        in_place([column_sum(grad_pre[half]) for half in range(2)]),
    ]
    small = jnp.concatenate(small).reshape(-1, width)
    small = jnp.pad(small, ((0, 16 - small.shape[0]), (0, 0)))
    mine_down = pair_grad(left_down[0], right_down[0], local_down, passed_down, core)
    mine_up = pair_grad(left_up[0], right_up[0], local_up, passed_up, core)
    grad_wdown, grad_wup = plane_sums(mine_down + mine_up, 1)
    mine_out = pair_grad(left_out[0], right_out[0], local_out, passed_out, core)
    mine_qkv = pair_grad(normed_one, grads[0], local_qkv, passed_qkv, core)
    (grad_wout, *grad_wqkv), small = plane_sums(mine_out + mine_qkv, 2, small, grad_wdown)
    grad_wqkv = jnp.stack(grad_wqkv, 0).astype(f32)
    wide = [lax.dynamic_slice_in_dim(small[i], own * local_width, local_width, 0) for i in (6, 7)]
    grad_bup = lax.dynamic_slice_in_dim(
        small[8:12].reshape(-1), own * hidden_local, hidden_local, 0
    )
    return (
        output,
        grad_tokens,
        small[0],
        small[1],
        grad_wqkv.transpose(1, 0, 2),
        jnp.stack(wide, 0),
        grad_wout.astype(f32),
        small[4],
        small[2],
        small[3],
        grad_wup.astype(f32),
        grad_bup,
        grad_wdown.astype(f32),
        small[5],
    )


def on_device(
    tokens,
    d_output,
    lengths,
    ln1_gain,
    ln1_bias,
    w_qkv,
    qv_bias,
    w_out,
    bias_out,
    ln2_gain,
    ln2_bias,
    w_up,
    b_up,
    w_down,
    b_down,
):
    parts = lax.axis_size("tensor")
    place = lax.axis_index("tensor")
    batches, slots, width = tokens.shape
    share = slots // parts
    row_start = place * share
    local_width = w_qkv.shape[2]
    hidden_local = w_up.shape[1]
    heads_local = local_width // HEAD_DIM
    scale = 1.0 / math.sqrt(HEAD_DIM)
    first_head = place * heads_local
    slopes = jnp.exp2(
        -8.0
        * ((first_head + jnp.arange(heads_local, dtype=jnp.int32)).astype(jnp.float32) + 1.0)
        / HEADS
    )
    weight_qkv = w_qkv.reshape(width, 3 * local_width)
    qkv_shift = jnp.concatenate(
        [
            qv_bias[0].astype(jnp.float32),
            jnp.zeros((local_width,), jnp.float32),
            qv_bias[1].astype(jnp.float32),
        ]
    )
    gain_one = ln1_gain.astype(jnp.float32)
    shift_one = ln1_bias.astype(jnp.float32)
    gain_two = ln2_gain.astype(jnp.float32)
    shift_two = ln2_bias.astype(jnp.float32)
    out_shift = bias_out.astype(jnp.float32)
    up_shift = b_up.astype(jnp.float32)
    down_shift = b_down.astype(jnp.float32)
    grad_qkv = jnp.zeros((width, 3 * local_width), jnp.float32)
    grad_qvb = jnp.zeros((2, local_width), jnp.float32)
    grad_wout = jnp.zeros((local_width, width), jnp.float32)
    grad_wup = jnp.zeros((width, hidden_local), jnp.float32)
    grad_bup = jnp.zeros((hidden_local,), jnp.float32)
    grad_wdown = jnp.zeros((hidden_local, width), jnp.float32)
    grad_gain_one = jnp.zeros((width,), jnp.float32)
    grad_shift_one = jnp.zeros((width,), jnp.float32)
    grad_gain_two = jnp.zeros((width,), jnp.float32)
    grad_shift_two = jnp.zeros((width,), jnp.float32)
    grad_out_shift = jnp.zeros((width,), jnp.float32)
    grad_down_shift = jnp.zeros((width,), jnp.float32)
    output_rows = []
    input_rows = []
    for index in range(batches):
        tokens_f = tokens[index].astype(jnp.float32)
        length = lengths[index]
        normal_one, inverse_one = norm_parts(tokens_f)
        normed_one = (normal_one * gain_one + shift_one).astype(jnp.bfloat16)
        projected = (matmul(normed_one, weight_qkv) + qkv_shift).astype(jnp.bfloat16)
        query = projected[:, :local_width].reshape(slots, heads_local, HEAD_DIM)
        keys = projected[:, local_width : 2 * local_width].reshape(slots, heads_local, HEAD_DIM)
        values = projected[:, 2 * local_width :].reshape(slots, heads_local, HEAD_DIM)
        attn = attention_forward(query, keys, values, length, slopes, scale)
        partial_value = matmul(attn, w_out)
        summed = lax.psum(partial_value.astype(jnp.bfloat16), "tensor").astype(jnp.float32)
        hidden_full = tokens_f + summed + out_shift
        normal_full, inverse_full = norm_parts(hidden_full)
        normed_two = (normal_full * gain_two + shift_two).astype(jnp.bfloat16)
        hidden_rows = lax.dynamic_slice_in_dim(hidden_full, row_start, share, 0)
        normal_two = lax.dynamic_slice_in_dim(normal_full, row_start, share, 0)
        inverse_two = lax.dynamic_slice_in_dim(inverse_full, row_start, share, 0)
        pre = matmul(normed_two, w_up) + up_shift
        act_value, act_slope = gelu_parts(pre)
        act = act_value.astype(jnp.bfloat16)
        mlp_part = lax.psum_scatter(
            matmul(act, w_down).astype(jnp.bfloat16), "tensor", scatter_dimension=0, tiled=True
        ).astype(jnp.float32)
        output_rows.append((hidden_rows + mlp_part + down_shift).astype(jnp.bfloat16))
        valid = (jnp.arange(slots, dtype=jnp.int32) < length).astype(jnp.float32)[:, None]
        grad_out = d_output[index].astype(jnp.float32) * valid
        grad_two = grad_out.astype(jnp.bfloat16)
        grad_wdown = grad_wdown + contract_rows(act, grad_two)
        grad_pre = (contract_cols(grad_two, w_down) * act_slope).astype(jnp.bfloat16)
        grad_wup = grad_wup + contract_rows(normed_two, grad_pre)
        grad_bup = grad_bup + jnp.sum(grad_pre.astype(jnp.float32), 0)
        grad_norm_two = lax.psum_scatter(
            contract_cols(grad_pre, w_up).astype(jnp.bfloat16),
            "tensor",
            scatter_dimension=0,
            tiled=True,
        ).astype(jnp.float32)
        grad_gain_two = grad_gain_two + jnp.sum(grad_norm_two * normal_two, 0)
        grad_shift_two = grad_shift_two + jnp.sum(grad_norm_two, 0)
        grad_out_rows = lax.dynamic_slice_in_dim(grad_out, row_start, share, 0)
        grad_hidden_rows = grad_out_rows + norm_backward(
            grad_norm_two, normal_two, inverse_two, gain_two
        )
        grad_one_rows = grad_hidden_rows.astype(jnp.bfloat16)
        grad_down_shift = grad_down_shift + jnp.sum(
            lax.dynamic_slice_in_dim(grad_two, row_start, share, 0).astype(jnp.float32), 0
        )
        grad_out_shift = grad_out_shift + jnp.sum(grad_one_rows.astype(jnp.float32), 0)
        grad_one = lax.all_gather(grad_one_rows, "tensor", axis=0, tiled=True)
        grad_wout = grad_wout + contract_rows(attn, grad_one)
        grad_attn = (
            contract_cols(grad_one, w_out)
            .astype(jnp.bfloat16)
            .reshape(slots, heads_local, HEAD_DIM)
        )
        grad_query, grad_keys, grad_values = attention_backward(
            query, keys, values, grad_attn, length, slopes, scale
        )
        grad_proj = jnp.concatenate([grad_query, grad_keys, grad_values], 1)
        grad_qkv = grad_qkv + contract_rows(normed_one, grad_proj)
        grad_qvb = grad_qvb + jnp.stack(
            [
                jnp.sum(grad_query.astype(jnp.float32), 0),
                jnp.sum(grad_values.astype(jnp.float32), 0),
            ],
            0,
        )
        grad_norm_one = lax.psum_scatter(
            contract_cols(grad_proj, weight_qkv).astype(jnp.bfloat16),
            "tensor",
            scatter_dimension=0,
            tiled=True,
        ).astype(jnp.float32)
        normal_one_rows = lax.dynamic_slice_in_dim(normal_one, row_start, share, 0)
        inverse_one_rows = lax.dynamic_slice_in_dim(inverse_one, row_start, share, 0)
        grad_gain_one = grad_gain_one + jnp.sum(grad_norm_one * normal_one_rows, 0)
        grad_shift_one = grad_shift_one + jnp.sum(grad_norm_one, 0)
        input_rows.append(
            (
                grad_hidden_rows
                + norm_backward(grad_norm_one, normal_one_rows, inverse_one_rows, gain_one)
            ).astype(jnp.bfloat16)
        )
    grad_qkv, grad_qvb, grad_wout, grad_wup, grad_bup, grad_wdown = (
        lax.psum(grad_qkv.astype(jnp.bfloat16), "dp").astype(jnp.float32),
        lax.psum(grad_qvb.astype(jnp.bfloat16), "dp").astype(jnp.float32),
        lax.psum(grad_wout.astype(jnp.bfloat16), "dp").astype(jnp.float32),
        lax.psum(grad_wup.astype(jnp.bfloat16), "dp").astype(jnp.float32),
        lax.psum(grad_bup.astype(jnp.bfloat16), "dp").astype(jnp.float32),
        lax.psum(grad_wdown.astype(jnp.bfloat16), "dp").astype(jnp.float32),
    )
    (
        grad_gain_one,
        grad_shift_one,
        grad_gain_two,
        grad_shift_two,
        grad_out_shift,
        grad_down_shift,
    ) = lax.psum(
        (
            grad_gain_one,
            grad_shift_one,
            grad_gain_two,
            grad_shift_two,
            grad_out_shift,
            grad_down_shift,
        ),
        ("dp", "tensor"),
    )
    return (
        jnp.stack(output_rows, 0),
        jnp.stack(input_rows, 0),
        grad_gain_one,
        grad_shift_one,
        grad_qkv.reshape(width, 3, local_width),
        grad_qvb,
        grad_wout,
        grad_out_shift,
        grad_gain_two,
        grad_shift_two,
        grad_wup,
        grad_bup,
        grad_wdown,
        grad_down_shift,
    )


def solution(mesh):
    whole = mesh.shape["tensor"] == 2 and mesh.shape["dp"] == 2 * len(RING)
    return jax.shard_map(
        whole_sequence if whole else on_device,
        mesh=mesh,
        in_specs=(
            P("dp", None, None),
            P("dp", None, None),
            P("dp"),
            P(),
            P(),
            P(None, None, "tensor"),
            P(None, "tensor"),
            P("tensor", None),
            P(),
            P(),
            P(),
            P(None, "tensor"),
            P("tensor"),
            P("tensor", None),
            P(),
        ),
        out_specs=(
            P("dp", "tensor", None),
            P("dp", "tensor", None),
            P(),
            P(),
            P(None, None, "tensor"),
            P(None, "tensor"),
            P("tensor", None),
            P(),
            P(),
            P(),
            P(None, "tensor"),
            P("tensor"),
            P("tensor", None),
            P(),
        ),
        check_vma=False,
    )
```

```python
import functools
import math

import jax
import jax.numpy as jnp
import numpy as np
from jax import lax
from jax.experimental import pallas as pl
from jax.experimental.pallas import tpu as pltpu
from jax.sharding import PartitionSpec as P

HEADS = 16
HEAD_DIM = 64


epsilon = 1e-05
root_two_pi = math.sqrt(2.0 / math.pi)
masked_score = -1e30


def matmul(left, right):
    return jnp.dot(left, right, preferred_element_type=jnp.float32)


def contract_rows(left, right):
    return lax.dot_general(
        left, right, (((0,), (0,)), ((), ())), preferred_element_type=jnp.float32
    )


def contract_cols(left, right):
    return lax.dot_general(
        left, right, (((1,), (1,)), ((), ())), preferred_element_type=jnp.float32
    )


def norm_parts(values):
    centre = jnp.mean(values, -1, keepdims=True)
    shifted = values - centre
    inverse = lax.rsqrt(jnp.mean(shifted * shifted, -1, keepdims=True) + epsilon)
    return (shifted * inverse, inverse)


def norm_backward(grad_normed, normal, inverse, gain):
    scaled = grad_normed * gain
    return inverse * (
        scaled
        - jnp.mean(scaled, -1, keepdims=True)
        - normal * jnp.mean(scaled * normal, -1, keepdims=True)
    )


def gelu_parts(pre):
    tangent = jnp.tanh(root_two_pi * (pre + 0.044715 * pre * pre * pre))
    value = 0.5 * pre * (1.0 + tangent)
    slope = 0.5 * (1.0 + tangent) + 0.5 * pre * (1.0 - tangent * tangent) * root_two_pi * (
        1.0 + 3.0 * 0.044715 * pre * pre
    )
    return (value, slope)


def block_probs(query_rows, key_rows, start, length, slopes, scale):
    rows = query_rows.shape[0]
    cols = key_rows.shape[0]
    products = jnp.einsum("ihd,jhd->hij", query_rows, key_rows, preferred_element_type=jnp.float32)
    key_place = jnp.arange(cols, dtype=jnp.int32)
    distance = (start + jnp.arange(rows, dtype=jnp.int32))[:, None] - key_place[None, :]
    scores = products * scale - slopes[:, None, None] * distance.astype(jnp.float32)[None]
    allowed = (distance >= 0) & (key_place[None, :] < length)
    masked = jnp.where(allowed[None], scores, masked_score)
    highest = jnp.max(masked, -1, keepdims=True)
    exponent = jnp.exp(masked - highest)
    return exponent / jnp.sum(exponent, -1, keepdims=True)


def attention_forward(query, keys, values, length, slopes, scale):
    slots = query.shape[0]
    block = min(512, slots)
    outputs = []
    for number in range(slots // block):
        start = number * block
        probs = block_probs(query[start : start + block], keys, start, length, slopes, scale)
        mixed = jnp.einsum(
            "hij,jhd->ihd", probs.astype(jnp.bfloat16), values, preferred_element_type=jnp.float32
        )
        outputs.append(mixed.reshape(block, -1).astype(jnp.bfloat16))
    return jnp.concatenate(outputs, 0)


def attention_backward(query, keys, values, grad_attn, length, slopes, scale):
    slots, heads_local, head_width = query.shape
    block = min(512, slots)
    grad_keys = jnp.zeros((slots, heads_local, head_width), jnp.float32)
    grad_values = jnp.zeros((slots, heads_local, head_width), jnp.float32)
    query_parts = []
    for number in range(slots // block):
        start = number * block
        query_rows = query[start : start + block]
        grad_rows = grad_attn[start : start + block]
        probs = block_probs(query_rows, keys, start, length, slopes, scale)
        grad_probs = jnp.einsum(
            "ihd,jhd->hij", grad_rows, values, preferred_element_type=jnp.float32
        )
        delta = jnp.sum(probs * grad_probs, -1, keepdims=True)
        grad_scores = (probs * (grad_probs - delta)).astype(jnp.bfloat16)
        part_query = (
            jnp.einsum("hij,jhd->ihd", grad_scores, keys, preferred_element_type=jnp.float32)
            * scale
        )
        part_keys = (
            jnp.einsum("hij,ihd->jhd", grad_scores, query_rows, preferred_element_type=jnp.float32)
            * scale
        )
        part_values = jnp.einsum(
            "hij,ihd->jhd",
            probs.astype(jnp.bfloat16),
            grad_rows,
            preferred_element_type=jnp.float32,
        )
        part_query, part_keys, part_values = (part_query, part_keys, part_values)
        query_parts.append(part_query)
        grad_keys = grad_keys.at[:slots].add(part_keys)
        grad_values = grad_values.at[:slots].add(part_values)
    grad_query = jnp.concatenate(query_parts, 0).reshape(slots, -1).astype(jnp.bfloat16)
    return (
        grad_query,
        grad_keys.reshape(slots, -1).astype(jnp.bfloat16),
        grad_values.reshape(slots, -1).astype(jnp.bfloat16),
    )


QUERY_BLOCK = 256
KEY_BLOCK = 1024
PAIR = 128
NT = (((1,), (1,)), ((), ()))
TN = (((0,), (0,)), ((), ()))


def mm(left, right, dims=(((1,), (0,)), ((), ()))):
    return lax.dot_general(left, right, dims, preferred_element_type=jnp.float32)


def low_lanes(rows):
    return lax.broadcasted_iota(jnp.int32, (rows, PAIR), 1) < HEAD_DIM


def slope_rows():
    table = np.zeros((HEADS // 2, 8, PAIR), np.float64)
    for head in range(HEADS):
        rest = np.float64(np.float32(2.0 ** (-8.0 * (head + 1) / HEADS)))
        base = HEAD_DIM * (1 - head % 2)
        for part in range(3):
            piece = np.float64(np.asarray(rest).astype(jnp.bfloat16))
            rest = rest - piece
            table[head // 2, head % 2, base + part] = 32.0 * piece
            table[head // 2, head % 2, base + 3 + part] = piece
        table[head // 2, head % 2, base + 6] = 1.0
    return table.astype(jnp.bfloat16)


def key_lanes(slots, length):
    place = jnp.arange(slots, dtype=jnp.int32)[:, None]
    lane = jnp.arange(PAIR, dtype=jnp.int32)[None, :] % HEAD_DIM
    high = (place // 32).astype(jnp.float32)
    low = (place % 32).astype(jnp.float32)
    mask = jnp.where(place < length, 0.0, masked_score)
    return jnp.where(
        lane < 3, high, jnp.where(lane < 6, low, jnp.where(lane == 6, mask, 0.0))
    ).astype(jnp.bfloat16)


def forward_kernel(
    q_ref, k_ref, v_ref, lanes_ref, rows_ref, o_ref, level_ref, key0, key1, val0, val1
):
    slots = q_ref.shape[0]
    block = QUERY_BLOCK
    low = low_lanes(slots)
    zero = jnp.zeros((slots, PAIR), jnp.bfloat16)
    one = jnp.ones((slots, PAIR), jnp.bfloat16)
    key0[...] = jnp.where(low, k_ref[...], lanes_ref[...])
    key1[...] = jnp.where(low, lanes_ref[...], k_ref[...])
    val0[:, :PAIR] = jnp.where(low, v_ref[...], zero)
    val0[:, PAIR:] = jnp.where(low, one, zero)
    val1[:, :PAIR] = jnp.where(low, zero, v_ref[...])
    val1[:, PAIR:] = jnp.where(low, zero, one)
    low_block = low_lanes(block)
    causal = lax.broadcasted_iota(jnp.int32, (block, block), 1) <= lax.broadcasted_iota(
        jnp.int32, (block, block), 0
    )
    for number in range(slots // block):
        start = number * block
        rows = q_ref[start : start + block, :] * jnp.bfloat16(0.125)
        total = None
        tops = []
        for head, (key, val) in enumerate(((key0, val0), (key1, val1))):
            extra = jnp.broadcast_to(rows_ref[0, head : head + 1, :], (block, PAIR))
            query = jnp.where(low_block, rows, extra) if head == 0 else jnp.where(
                low_block, extra, rows
            )
            own = jnp.where(causal, mm(query, key[start : start + block, :], NT), masked_score)
            highest = jnp.max(own, 1, keepdims=True)
            if start:
                past = mm(query, key[:start, :], NT)
                highest = jnp.maximum(highest, jnp.max(past, 1, keepdims=True))
                part = mm(jnp.exp(past - highest).astype(jnp.bfloat16), val[:start, :])
                total = part if total is None else total + part
            part = mm(jnp.exp(own - highest).astype(jnp.bfloat16), val[start : start + block, :])
            total = part if total is None else total + part
            tops.append(highest)
        o_ref[start : start + block, :] = (total[:, :PAIR] / total[:, PAIR:]).astype(jnp.bfloat16)
        level = (jnp.where(low_block, tops[0], tops[1]) + jnp.log(total[:, PAIR:])).T
        level_ref[0, 0:1, start : start + block] = level[0:1, :]
        level_ref[0, 1:2, start : start + block] = level[HEAD_DIM : HEAD_DIM + 1, :]


def backward_kernel(
    q_ref, k_ref, v_ref, o_ref, g_ref, level_ref, lanes_ref, rows_ref, dq_ref, dk_ref, dv_ref,
    key0, key1, val0, val1, bare0, bare1, total_k, total_v,
):
    slots = q_ref.shape[0]
    block = QUERY_BLOCK
    piece = KEY_BLOCK
    low = low_lanes(slots)
    zero = jnp.zeros((slots, PAIR), jnp.bfloat16)
    key0[...] = jnp.where(low, k_ref[...], lanes_ref[...])
    key1[...] = jnp.where(low, lanes_ref[...], k_ref[...])
    bare0[...] = jnp.where(low, k_ref[...], zero)
    bare1[...] = jnp.where(low, zero, k_ref[...])
    val0[...] = jnp.where(low, v_ref[...], zero)
    val1[...] = jnp.where(low, zero, v_ref[...])
    low_block = low_lanes(block)
    nil = jnp.zeros((block, PAIR), jnp.bfloat16)
    causal = lax.broadcasted_iota(jnp.int32, (block, block), 0) <= lax.broadcasted_iota(
        jnp.int32, (block, block), 1
    )
    for number in reversed(range(slots // block)):
        start = number * block
        stop = start + block
        rows = q_ref[start:stop, :] * jnp.bfloat16(0.125)
        grad = g_ref[start:stop, :]
        shares = (grad.astype(jnp.float32) * o_ref[start:stop, :].astype(jnp.float32)).T
        deltas = [
            jnp.sum(shares[head * HEAD_DIM : (head + 1) * HEAD_DIM, :], 0, keepdims=True)
            for head in range(2)
        ]
        levels = [level_ref[0, head : head + 1, start:stop] for head in range(2)]
        extras = [jnp.broadcast_to(rows_ref[0, h : h + 1, :], (block, PAIR)) for h in range(2)]
        queries = (
            jnp.where(low_block, rows, extras[0]),
            jnp.where(low_block, extras[1], rows),
        )
        grads = jnp.concatenate(
            [jnp.where(low_block, grad, nil), jnp.where(low_block, nil, grad)], 0
        )
        both = jnp.concatenate(
            [jnp.where(low_block, rows, nil), jnp.where(low_block, nil, rows)], 0
        )
        grad_query = None
        for begin in range(0, stop, min(piece, stop)):
            end = min(begin + piece, stop)
            probs, scores = [], []
            for head, (key, val, bare) in enumerate(((key0, val0, bare0), (key1, val1, bare1))):
                score = mm(key[begin:end, :], queries[head], NT)
                if end > start:
                    own = jnp.where(causal, score[start - begin :], masked_score)
                    score = jnp.concatenate([score[: start - begin], own], 0) if start > begin else own
                prob = jnp.exp(score - levels[head])
                grad_prob = mm(val[begin:end, :], grad, NT)
                grad_score = (prob * (grad_prob - deltas[head])).astype(jnp.bfloat16)
                probs.append(prob.astype(jnp.bfloat16))
                scores.append(grad_score)
                part = mm(grad_score, bare[begin:end, :], TN)
                grad_query = part if grad_query is None else grad_query + part
            part_v = mm(jnp.concatenate(probs, 1), grads)
            part_k = mm(jnp.concatenate(scores, 1), both)
            if stop == slots:
                total_v[begin:end, :] = part_v
                total_k[begin:end, :] = part_k
            else:
                total_v[begin:end, :] += part_v
                total_k[begin:end, :] += part_k
        dq_ref[start:stop, :] = (grad_query * 0.125).astype(jnp.bfloat16)
    dk_ref[...] = total_k[...].astype(jnp.bfloat16)
    dv_ref[...] = total_v[...].astype(jnp.bfloat16)


def pair_specs(slots):
    part = pl.BlockSpec((slots, PAIR), lambda pair: (0, pair))
    lanes = pl.BlockSpec((slots, PAIR), lambda pair: (0, 0))
    rows = pl.BlockSpec((1, 8, PAIR), lambda pair: (pair, 0, 0))
    levels = pl.BlockSpec((1, 8, slots), lambda pair: (pair, 0, 0))
    return part, lanes, rows, levels


def attention_out(query, keys, values, lanes, rows):
    slots, columns = query.shape
    part, lane_spec, row_spec, level_spec = pair_specs(slots)
    pairs = columns // PAIR
    half = slots * slots * PAIR * pairs
    return pl.pallas_call(
        forward_kernel,
        grid=(pairs,),
        out_shape=(
            jax.ShapeDtypeStruct((slots, columns), jnp.bfloat16),
            jax.ShapeDtypeStruct((pairs, 8, slots), jnp.float32),
        ),
        in_specs=[part, part, part, lane_spec, row_spec],
        out_specs=(part, level_spec),
        scratch_shapes=[pltpu.VMEM((slots, PAIR), jnp.bfloat16)] * 2
        + [pltpu.VMEM((slots, 2 * PAIR), jnp.bfloat16)] * 2,
        cost_estimate=pl.CostEstimate(
            flops=8 * half, bytes_accessed=8 * slots * columns, transcendentals=slots * slots * pairs
        ),
        name="attention_out",
    )(query, keys, values, lanes, rows)


def attention_grads(query, keys, values, mixed, levels, grad, lanes, rows):
    slots, columns = query.shape
    part, lane_spec, row_spec, level_spec = pair_specs(slots)
    pairs = columns // PAIR
    half = slots * slots * PAIR * pairs
    shape = jax.ShapeDtypeStruct((slots, columns), jnp.bfloat16)
    return pl.pallas_call(
        backward_kernel,
        grid=(pairs,),
        out_shape=(shape, shape, shape),
        in_specs=[part, part, part, part, part, level_spec, lane_spec, row_spec],
        out_specs=(part, part, part),
        scratch_shapes=[pltpu.VMEM((slots, PAIR), jnp.bfloat16)] * 6
        + [pltpu.VMEM((slots, PAIR), jnp.float32)] * 2,
        cost_estimate=pl.CostEstimate(
            flops=20 * half,
            bytes_accessed=14 * slots * columns,
            transcendentals=slots * slots * pairs,
        ),
        name="attention_grads",
    )(query, keys, values, mixed, grad, levels, lanes, rows)


ROW_BLOCK = 256


def whole_spec(array):
    zeros = (0,) * array.ndim
    return pl.BlockSpec(array.shape, lambda *_: zeros)


def row_spec(columns):
    return pl.BlockSpec((ROW_BLOCK, columns), lambda row, *_: (row, 0))


def own_spec(columns):
    return pl.BlockSpec((1, ROW_BLOCK, columns), lambda row, facts: (facts[0], row, 0))


def over_rows(kernel, name, slots, facts, inputs, outputs, flops):
    arrays, in_specs = zip(*inputs)
    shapes, out_specs = zip(*outputs)
    return pl.pallas_call(
        kernel,
        grid_spec=pltpu.PrefetchScalarGridSpec(
            num_scalar_prefetch=1,
            grid=(slots // ROW_BLOCK,),
            in_specs=list(in_specs),
            out_specs=list(out_specs),
        ),
        out_shape=list(shapes),
        cost_estimate=pl.CostEstimate(
            flops=flops,
            bytes_accessed=sum(array.size * array.dtype.itemsize for array in arrays),
            transcendentals=0,
        ),
        name=name,
    )(facts, *arrays)


def project_kernel(facts, tok_ref, gain_ref, shift_ref, w_ref, bias_ref, norm_ref, q_ref, k_ref, v_ref):
    normal, _ = norm_parts(tok_ref[0].astype(jnp.float32))
    normed = (normal * gain_ref[...] + shift_ref[...]).astype(jnp.bfloat16)
    norm_ref[...] = normed
    q_ref[...] = (mm(normed, w_ref[0]) + bias_ref[0:1, :]).astype(jnp.bfloat16)
    k_ref[...] = mm(normed, w_ref[1]).astype(jnp.bfloat16)
    v_ref[...] = (mm(normed, w_ref[2]) + bias_ref[1:2, :]).astype(jnp.bfloat16)


def hidden_kernel(
    facts, tok_ref, a0_ref, a1_ref, w0_ref, w1_ref, bias_ref, gain_ref, shift_ref, hid_ref, norm_ref
):
    hidden = tok_ref[0].astype(jnp.float32) + bias_ref[...]
    hidden = hidden + mm(a0_ref[...], w0_ref[...]) + mm(a1_ref[...], w1_ref[...])
    hid_ref[...] = hidden
    normal, _ = norm_parts(hidden)
    norm_ref[...] = (normal * gain_ref[...] + shift_ref[...]).astype(jnp.bfloat16)


def act_kernel(norm_ref, w_ref, bias_ref, act_ref, slope_ref):
    def rows(number, carry):
        at = pl.ds(pl.multiple_of(number * ROW_BLOCK, ROW_BLOCK), ROW_BLOCK)
        value, slope = gelu_parts(mm(norm_ref[at, :], w_ref[...]) + bias_ref[...])
        act_ref[at, :] = value.astype(jnp.bfloat16)
        slope_ref[at, :] = slope.astype(jnp.bfloat16)
        return carry

    lax.fori_loop(0, norm_ref.shape[0] // ROW_BLOCK, rows, 0, unroll=True)


def activations(normed, weight, bias):
    slots, width = normed.shape
    hidden = weight.shape[1]
    columns = 512
    out = pl.BlockSpec((slots, columns), lambda col: (0, col))
    shape = jax.ShapeDtypeStruct((slots, hidden), jnp.bfloat16)
    return pl.pallas_call(
        act_kernel,
        grid=(hidden // columns,),
        in_specs=[
            whole_spec(normed),
            pl.BlockSpec((width, columns), lambda col: (0, col)),
            pl.BlockSpec((1, columns), lambda col: (0, col)),
        ],
        out_specs=(out, out),
        out_shape=(shape, shape),
        cost_estimate=pl.CostEstimate(
            flops=2 * slots * width * hidden,
            bytes_accessed=8 * slots * hidden,
            transcendentals=slots * hidden,
        ),
        name="activations",
    )(normed, weight, bias)


def output_kernel(facts, hid_ref, a0_ref, a1_ref, w0_ref, w1_ref, bias_ref, tie_ref, out_ref):
    total = hid_ref[...] + bias_ref[...] + mm(a0_ref[...], w0_ref[...])
    out_ref[...] = (total + mm(a1_ref[...], w1_ref[...])).astype(jnp.bfloat16)


def add_sums(sums_ref, rows):
    @pl.when(pl.program_id(0) == 0)
    def _():
        sums_ref[...] = jnp.zeros_like(sums_ref)

    for index, value in enumerate(rows):
        sums_ref[index : index + 1, :] += jnp.sum(value, 0, keepdims=True)


def hidden_grad_kernel(
    facts, g0_ref, g1_ref, w0_ref, w1_ref, hid_ref, gain_ref, dout_ref, grad_ref, one_ref, sums_ref
):
    grad_norm = mm(g0_ref[...], w0_ref[...], NT) + mm(g1_ref[...], w1_ref[...], NT)
    normal, inverse = norm_parts(hid_ref[...])
    place = lax.broadcasted_iota(jnp.int32, grad_norm.shape, 0) + pl.program_id(0) * ROW_BLOCK
    grad_out = jnp.where(place < facts[1], dout_ref[0].astype(jnp.float32), 0.0)
    grad = grad_out + norm_backward(grad_norm, normal, inverse, gain_ref[...])
    one = grad.astype(jnp.bfloat16)
    grad_ref[...] = grad
    one_ref[...] = one
    add_sums(sums_ref, [grad_norm * normal, grad_norm, one.astype(jnp.float32), grad_out])


def token_grad_kernel(
    facts, q0_ref, k0_ref, v0_ref, q1_ref, k1_ref, v1_ref, w0_ref, w1_ref, tok_ref, grad_ref,
    gain_ref, out_ref, sums_ref, heads_ref,
):
    grad_norm = None
    for refs, weight in (((q0_ref, k0_ref, v0_ref), w0_ref), ((q1_ref, k1_ref, v1_ref), w1_ref)):
        for part, ref in enumerate(refs):
            more = mm(ref[...], weight[part], NT)
            grad_norm = more if grad_norm is None else grad_norm + more
    normal, inverse = norm_parts(tok_ref[0].astype(jnp.float32))
    grad = grad_ref[...] + norm_backward(grad_norm, normal, inverse, gain_ref[...])
    out_ref[...] = grad.astype(jnp.bfloat16)
    add_sums(sums_ref, [grad_norm * normal, grad_norm])
    add_sums(heads_ref, [ref[...].astype(jnp.float32) for ref in (q0_ref, q1_ref, v0_ref, v1_ref)])


RING = ((0, 0), (1, 0), (2, 0), (3, 0), (3, 1), (2, 1), (1, 1), (0, 1))


def device_of(z, y, core):
    return (z * 2 + y) * 2 + core


def to_tensor(value):
    return lax.ppermute(value, "tensor", [(0, 1), (1, 0)])


def to_core(value):
    return lax.ppermute(value, "dp", [(i, i ^ 1) for i in range(2 * len(RING))])


def rows_at(value, start, size):
    return lax.dynamic_slice_in_dim(value, start, size, value.ndim - 2)


def after(value, *earlier):
    return lax.optimization_barrier((value, *earlier))[0]


def piece_over_x(weight, index, pieces, *earlier):
    size = weight.shape[-2] // pieces
    return to_tensor(after(rows_at(weight, index * size, size), *earlier))


def both_cores(value, core, axis):
    beside = to_core(value)
    first = jnp.where(core == 0, value, beside)
    second = jnp.where(core == 0, beside, value)
    return jnp.concatenate([first, second], axis)


def ring_kernel(blocks, has_small, has_tie, *refs):
    count = len(RING)
    values, refs = refs[:blocks], refs[blocks:]
    if has_small:
        small_ref, refs = refs[0], refs[1:]
    refs = refs[has_tie:]
    results, refs = refs[:blocks], refs[blocks:]
    if has_small:
        small_out, refs = refs[0], refs[1:]
    slots, refs = refs[:blocks], refs[blocks:]
    sums, refs = refs[:blocks], refs[blocks:]
    send_sems, recv_sems, swap_send_sems, swap_recv_sems = refs[:4]
    if has_small:
        small_slots, small_sums, small_send_sems, small_recv_sems = refs[4:]
    device = lax.axis_index("dp")
    core, y, z = lax.rem(device, 2), lax.rem(device // 2, 2), device // 4
    place = z * (1 - y) + (count - 1 - z) * y

    def at_place(where):
        side = where // 4
        return {"dp": device_of(where * (1 - side) + (count - 1 - where) * side, side, core)}

    nexts = (at_place(lax.rem(place + 1, count)), at_place(lax.rem(place + count - 1, count)))
    partner = {"dp": device + 1 - 2 * core}
    barrier = pltpu.get_barrier_semaphore()
    greeted = [*nexts, partner]
    if has_small:
        low_z = lax.rem(z, 2)
        small_targets = [
            partner,
            {"tensor": 1 - lax.axis_index("tensor")},
            {"dp": device + 2 - 4 * y},
            {"dp": device + 4 - 8 * low_z},
            {"dp": device + 8 - 16 * (z // 2)},
        ]
        greeted += small_targets[1:]
    for target in greeted:
        pl.semaphore_signal(barrier, inc=1, device_id=target, device_id_type=pl.DeviceIdType.MESH)
    pl.semaphore_wait(barrier, len(greeted))

    streams = [(array, way) for array in range(blocks) for way in range(2)]

    def block(way, offset):
        return lax.rem(place - (1, -1)[way] * offset + 2 * count, count)

    def send(array, way, step, source, target):
        index = 2 * array + way
        copy = pltpu.make_async_remote_copy(
            src_ref=source,
            dst_ref=target,
            send_sem=send_sems.at[index, step],
            recv_sem=recv_sems.at[index, step],
            device_id=nexts[way],
            device_id_type=pl.DeviceIdType.MESH,
        )
        copy.start()
        return copy

    def swap(array, way, step, offset):
        index = 2 * array + way
        done = results[array].at[core, way, block(way, offset)]
        copy = pltpu.make_async_remote_copy(
            src_ref=done,
            dst_ref=done,
            send_sem=swap_send_sems.at[index, step],
            recv_sem=swap_recv_sems.at[index, step],
            device_id=partner,
            device_id_type=pl.DeviceIdType.MESH,
        )
        copy.start()
        return copy

    def exchange(turn):
        copy = pltpu.make_async_remote_copy(
            src_ref=small_ref if turn == 0 else small_sums.at[turn - 1],
            dst_ref=small_slots.at[turn],
            send_sem=small_send_sems.at[turn],
            recv_sem=small_recv_sems.at[turn],
            device_id=small_targets[turn],
            device_id_type=pl.DeviceIdType.MESH,
        )
        copy.start()
        return copy

    def take_exchange(turn):
        exchanges[turn].wait_recv()
        total = (small_ref[...] if turn == 0 else small_sums[turn - 1]) + small_slots[turn]
        if turn == len(small_targets) - 1:
            small_out[...] = total
        else:
            small_sums[turn] = total
            exchanges.append(exchange(turn + 1))

    flying, swaps, started = {}, [], []
    exchanges = [exchange(0)] if has_small else []
    for array, way in streams:
        copy = send(array, way, 0, values[array].at[way, block(way, 0)], slots[array].at[way, 0])
        flying[array, way] = copy
        started.append(copy)
    for step in range(1, 2 * count - 2):
        if has_small and step % 2 == 0 and step // 2 <= len(small_targets):
            take_exchange(step // 2 - 1)
        for array, way in streams:
            flying[array, way].wait_recv()
            if step < count:
                total = values[array][way, block(way, step)].astype(jnp.float32) + slots[array][
                    way, step - 1
                ].astype(jnp.float32)
                total = total.astype(jnp.bfloat16)
            if step < count - 1:
                sums[array][way, step - 1] = total
                source, target = sums[array].at[way, step - 1], slots[array].at[way, step]
            else:
                if step == count - 1:
                    results[array][core, way, block(way, step)] = total
                source = target = results[array].at[core, way, block(way, step)]
            copy = send(array, way, step, source, target)
            flying[array, way] = copy
            started.append(copy)
            if step >= count - 1:
                swaps.append(swap(array, way, step - count + 1, step))
    for array, way in streams:
        flying[array, way].wait_recv()
        swaps.append(swap(array, way, count - 1, 2 * count - 2))
    for copy in started + exchanges:
        copy.wait_send()
    for copy in swaps:
        copy.wait()


def plane_sums(values, identity, small=None, tie=None):
    count = len(RING)
    blocks = len(values)
    shaped = [
        value.reshape(2, count, value.shape[0] // (2 * count), value.shape[1]) for value in values
    ]
    size = sum(value.size for value in values)
    vmem = pl.BlockSpec(memory_space=pltpu.VMEM)
    inputs, in_specs = list(shaped), [vmem] * blocks
    shapes = [jax.ShapeDtypeStruct((2, *value.shape), value.dtype) for value in shaped]
    scratch = [pltpu.VMEM((2, count - 1, *value.shape[2:]), value.dtype) for value in shaped]
    scratch += [pltpu.VMEM((2, count - 2, *value.shape[2:]), value.dtype) for value in shaped]
    scratch += [pltpu.SemaphoreType.DMA((2 * blocks, 2 * count - 2))] * 2
    scratch += [pltpu.SemaphoreType.DMA((2 * blocks, count))] * 2
    if small is not None:
        inputs.append(small)
        in_specs.append(vmem)
        shapes.append(jax.ShapeDtypeStruct(small.shape, small.dtype))
        scratch += [pltpu.VMEM((5, *small.shape), small.dtype)] * 2
        scratch += [pltpu.SemaphoreType.DMA((5,))] * 2
    if tie is not None:
        inputs.append(tie)
        in_specs.append(pl.BlockSpec(memory_space=pl.ANY))
    results = pl.pallas_call(
        functools.partial(ring_kernel, blocks, small is not None, int(tie is not None)),
        out_shape=shapes,
        in_specs=in_specs,
        out_specs=[vmem] * len(shapes),
        scratch_shapes=scratch,
        compiler_params=pltpu.CompilerParams(collective_id=identity, has_side_effects=True),
        cost_estimate=pl.CostEstimate(flops=size, bytes_accessed=6 * size, transcendentals=0),
        name="plane_sums",
    )(*inputs)
    sums = [
        result.reshape(2 * value.shape[0], value.shape[1]) for result, value in zip(results, values)
    ]
    return sums if small is None else (sums, results[-1])


def core_send(left, rights, core):
    half = left.shape[1] // 2
    sent = lax.dynamic_slice_in_dim(left, (1 - core) * half, half, 1)
    return [to_core(contract_rows(sent, right).astype(jnp.bfloat16)) for right in rights]


def core_sum(left, rights, arrived, core):
    half = left.shape[1] // 2
    kept = lax.dynamic_slice_in_dim(left, core * half, half, 1)
    return [
        contract_rows(kept, right) + part.astype(jnp.float32)
        for right, part in zip(rights, arrived)
    ]


def start_grad(left, rights, core):
    other = core_send(left[1], rights[1], core)
    local = core_send(left[0], rights[0], core)
    summed = [
        part.astype(jnp.bfloat16) for part in core_sum(left[1], rights[1], other, core)
    ]
    return local, summed, [to_tensor(part) for part in summed]


def pair_grad(left, rights, local, passed, core):
    mine = [
        (part + more.astype(jnp.float32)).astype(jnp.bfloat16)
        for part, more in zip(core_sum(left, rights, local, core), passed)
    ]
    return mine


def trade_rows(value, own):
    share = value.shape[0] // 2
    arrived = to_tensor(lax.dynamic_slice_in_dim(value, (1 - own) * share, share, 0))
    kept = lax.dynamic_slice_in_dim(value, own * share, share, 0)
    return jnp.stack(
        [jnp.where(own == 0, kept, arrived), jnp.where(own == 0, arrived, kept)], 0
    )


def whole_sequence(
    tokens,
    d_output,
    lengths,
    ln1_gain,
    ln1_bias,
    w_qkv,
    qv_bias,
    w_out,
    bias_out,
    ln2_gain,
    ln2_bias,
    w_up,
    b_up,
    w_down,
    b_down,
):
    own = lax.axis_index("tensor")
    device = lax.axis_index("dp")
    core = device % 2
    slots, width = tokens.shape[1:]
    local_width = w_qkv.shape[2]
    hidden_local = w_up.shape[1]
    table = jnp.asarray(slope_rows())
    pairs = local_width // PAIR
    f32 = jnp.float32

    weight_qkv = w_qkv.transpose(1, 0, 2)
    biases = jnp.concatenate([qv_bias.reshape(-1), b_up])
    other_biases = to_tensor(biases)
    far_up = piece_over_x(w_up, device, 2 * len(RING))
    far_qkv = piece_over_x(weight_qkv, core, 2)
    qv = [b[: 2 * local_width].reshape(2, local_width).astype(f32) for b in (biases, other_biases)]
    ups = [b[2 * local_width :].astype(f32)[None] for b in (biases, other_biases)]
    rows = [lax.dynamic_slice_in_dim(table, index * pairs, pairs, 0) for index in (own, 1 - own)]
    gain_one, shift_one = ln1_gain.astype(f32)[None], ln1_bias.astype(f32)[None]
    gain_two, shift_two = ln2_gain.astype(f32)[None], ln2_bias.astype(f32)[None]

    length = lax.dynamic_index_in_dim(lengths, own, 0, keepdims=False)
    facts = jnp.stack([own.astype(jnp.int32), length])
    lanes = key_lanes(slots, length)
    low = jnp.bfloat16

    def run(kernel, name, inputs, outputs, flops):
        return over_rows(kernel, name, slots, facts, inputs, outputs, flops)

    def fixed(array):
        return array, whole_spec(array)

    def by_row(array):
        return array, row_spec(array.shape[1])

    def rows_out(columns, dtype):
        return jax.ShapeDtypeStruct((slots, columns), dtype), row_spec(columns)

    def sums_out(columns):
        shape = jax.ShapeDtypeStruct((8, columns), f32)
        return shape, whole_spec(shape)

    square = 2 * slots * width
    tokens_in, d_output_in = (tokens, own_spec(width)), (d_output, own_spec(width))
    normed_one, *local_heads = run(
        project_kernel,
        "project",
        [tokens_in, fixed(gain_one), fixed(shift_one), fixed(weight_qkv), fixed(qv[0])],
        [rows_out(width, low)] + [rows_out(local_width, low)] * 3,
        3 * square * local_width,
    )
    attn, level = attention_out(*local_heads, lanes, rows[0])
    heads, mixed, levels = [tuple(local_heads)], [attn], [level]
    far_down = piece_over_x(w_down, device, 2 * len(RING), normed_one)
    far_out = piece_over_x(w_out, core, 2, normed_one)
    up = (w_up, lax.all_gather(far_up, "dp", axis=0, tiled=True))
    down = (w_down, lax.all_gather(far_down, "dp", axis=0, tiled=True))
    qkv = (weight_qkv, both_cores(far_qkv, core, 1))
    query = (matmul(normed_one, qkv[1][0]) + qv[1][0]).astype(low)
    keys = matmul(normed_one, qkv[1][1]).astype(low)
    values = (matmul(normed_one, qkv[1][2]) + qv[1][1]).astype(low)
    heads.append((query, keys, values))
    attn, level = attention_out(query, keys, values, lanes, rows[1])
    mixed.append(attn)
    levels.append(level)
    out = (w_out, both_cores(far_out, core, 0))
    hidden, normed_two = run(
        hidden_kernel,
        "hidden_state",
        [tokens_in, by_row(mixed[0]), by_row(mixed[1]), fixed(out[0]), fixed(out[1])]
        + [fixed(bias_out.astype(f32)[None]), fixed(gain_two), fixed(shift_two)],
        [rows_out(width, f32), rows_out(width, low)],
        2 * square * local_width,
    )
    acts = [activations(normed_two, up[half], ups[half]) for half in range(2)]

    valid = (jnp.arange(slots, dtype=jnp.int32) < length).astype(f32)[:, None]
    grad_out = lax.dynamic_index_in_dim(d_output, own, 0, keepdims=False).astype(f32) * valid
    grad_two = grad_out.astype(low)
    left_down, right_down = (acts[0][0], acts[1][0]), ([grad_two], [grad_two])
    local_down, sent_down, passed_down = start_grad(left_down, right_down, core)
    late_two = after(grad_two, *sent_down, *local_down)
    grad_pre = [
        (contract_cols(late_two, down[half]) * acts[half][1].astype(f32)).astype(low)
        for half in range(2)
    ]
    left_up, right_up = (normed_two, normed_two), ([grad_pre[0]], [grad_pre[1]])
    local_up, sent_up, passed_up = start_grad(left_up, right_up, core)
    late_pre = lax.optimization_barrier((*grad_pre, *sent_up, *local_up))
    grad_hidden, grad_one, sums_two = run(
        hidden_grad_kernel,
        "hidden_grad",
        [by_row(late_pre[0]), by_row(late_pre[1]), fixed(up[0]), fixed(up[1]), by_row(hidden)]
        + [fixed(gain_two), d_output_in],
        [rows_out(width, f32), rows_out(width, low), sums_out(width)],
        2 * square * hidden_local,
    )
    tie = (sent_up[0], pl.BlockSpec(memory_space=pl.ANY))
    (result,) = run(
        output_kernel,
        "layer_output",
        [by_row(hidden), by_row(acts[0][0]), by_row(acts[1][0]), fixed(down[0]), fixed(down[1])]
        + [fixed(b_down.astype(f32)[None]), tie],
        [rows_out(width, low)],
        2 * square * hidden_local,
    )
    output = trade_rows(result, own)
    left_out, right_out = (mixed[0], mixed[1]), ([grad_one], [grad_one])
    local_out, sent_out, passed_out = start_grad(left_out, right_out, core)
    late_one = after(grad_one, *sent_out, *local_out)
    grads = [None, None]
    grad_attn = contract_cols(late_one, out[1]).astype(low)
    grads[1] = attention_grads(*heads[1], mixed[1], levels[1], grad_attn, lanes, rows[1])
    other_qkv = core_send(normed_one, grads[1], core)
    sent_qkv = [part.astype(low) for part in core_sum(normed_one, grads[1], other_qkv, core)]
    passed_qkv = [to_tensor(part) for part in sent_qkv]
    later_one = after(late_one, *sent_qkv)
    grad_attn = contract_cols(later_one, out[0]).astype(low)
    grads[0] = attention_grads(*heads[0], mixed[0], levels[0], grad_attn, lanes, rows[0])
    local_qkv = core_send(normed_one, grads[0], core)
    grad_tokens, sums_one, sums_heads = run(
        token_grad_kernel,
        "token_grad",
        [by_row(part) for part in (*grads[0], *grads[1])]
        + [fixed(qkv[0]), fixed(qkv[1]), tokens_in, by_row(grad_hidden), fixed(gain_one)],
        [rows_out(width, low), sums_out(width), sums_out(local_width)],
        6 * square * local_width,
    )
    grad_tokens = trade_rows(grad_tokens, own)

    def in_place(first, second):
        return jnp.concatenate(
            [jnp.where(own == 0, first, second), jnp.where(own == 0, second, first)], 0
        )

    bias_up = [jnp.sum(grad_pre[half].astype(f32), 0) for half in range(2)]
    small = jnp.concatenate(
        [
            sums_one[:2],
            sums_two[:4],
            in_place(sums_heads[0], sums_heads[1]).reshape(1, width),
            in_place(sums_heads[2], sums_heads[3]).reshape(1, width),
            in_place(*bias_up).reshape(-1, width),
        ],
        0,
    )
    small = jnp.pad(small, ((0, 16 - small.shape[0]), (0, 0)))
    mine_down = pair_grad(left_down[0], right_down[0], local_down, passed_down, core)
    mine_up = pair_grad(left_up[0], right_up[0], local_up, passed_up, core)
    grad_wdown, grad_wup = plane_sums(mine_down + mine_up, 1)
    mine_out = pair_grad(left_out[0], right_out[0], local_out, passed_out, core)
    mine_qkv = pair_grad(normed_one, grads[0], local_qkv, passed_qkv, core)
    (grad_wout, *grad_wqkv), small = plane_sums(mine_out + mine_qkv, 2, small, grad_wdown)
    grad_wqkv = jnp.stack(grad_wqkv, 0).astype(f32)
    wide = [lax.dynamic_slice_in_dim(small[i], own * local_width, local_width, 0) for i in (6, 7)]
    grad_bup = lax.dynamic_slice_in_dim(
        small[8:12].reshape(-1), own * hidden_local, hidden_local, 0
    )
    return (
        output,
        grad_tokens,
        small[0],
        small[1],
        grad_wqkv.transpose(1, 0, 2),
        jnp.stack(wide, 0),
        grad_wout.astype(f32),
        small[4],
        small[2],
        small[3],
        grad_wup.astype(f32),
        grad_bup,
        grad_wdown.astype(f32),
        small[5],
    )


def on_device(
    tokens,
    d_output,
    lengths,
    ln1_gain,
    ln1_bias,
    w_qkv,
    qv_bias,
    w_out,
    bias_out,
    ln2_gain,
    ln2_bias,
    w_up,
    b_up,
    w_down,
    b_down,
):
    parts = lax.axis_size("tensor")
    place = lax.axis_index("tensor")
    batches, slots, width = tokens.shape
    share = slots // parts
    row_start = place * share
    local_width = w_qkv.shape[2]
    hidden_local = w_up.shape[1]
    heads_local = local_width // HEAD_DIM
    scale = 1.0 / math.sqrt(HEAD_DIM)
    first_head = place * heads_local
    slopes = jnp.exp2(
        -8.0
        * ((first_head + jnp.arange(heads_local, dtype=jnp.int32)).astype(jnp.float32) + 1.0)
        / HEADS
    )
    weight_qkv = w_qkv.reshape(width, 3 * local_width)
    qkv_shift = jnp.concatenate(
        [
            qv_bias[0].astype(jnp.float32),
            jnp.zeros((local_width,), jnp.float32),
            qv_bias[1].astype(jnp.float32),
        ]
    )
    gain_one = ln1_gain.astype(jnp.float32)
    shift_one = ln1_bias.astype(jnp.float32)
    gain_two = ln2_gain.astype(jnp.float32)
    shift_two = ln2_bias.astype(jnp.float32)
    out_shift = bias_out.astype(jnp.float32)
    up_shift = b_up.astype(jnp.float32)
    down_shift = b_down.astype(jnp.float32)
    grad_qkv = jnp.zeros((width, 3 * local_width), jnp.float32)
    grad_qvb = jnp.zeros((2, local_width), jnp.float32)
    grad_wout = jnp.zeros((local_width, width), jnp.float32)
    grad_wup = jnp.zeros((width, hidden_local), jnp.float32)
    grad_bup = jnp.zeros((hidden_local,), jnp.float32)
    grad_wdown = jnp.zeros((hidden_local, width), jnp.float32)
    grad_gain_one = jnp.zeros((width,), jnp.float32)
    grad_shift_one = jnp.zeros((width,), jnp.float32)
    grad_gain_two = jnp.zeros((width,), jnp.float32)
    grad_shift_two = jnp.zeros((width,), jnp.float32)
    grad_out_shift = jnp.zeros((width,), jnp.float32)
    grad_down_shift = jnp.zeros((width,), jnp.float32)
    output_rows = []
    input_rows = []
    for index in range(batches):
        tokens_f = tokens[index].astype(jnp.float32)
        length = lengths[index]
        normal_one, inverse_one = norm_parts(tokens_f)
        normed_one = (normal_one * gain_one + shift_one).astype(jnp.bfloat16)
        projected = (matmul(normed_one, weight_qkv) + qkv_shift).astype(jnp.bfloat16)
        query = projected[:, :local_width].reshape(slots, heads_local, HEAD_DIM)
        keys = projected[:, local_width : 2 * local_width].reshape(slots, heads_local, HEAD_DIM)
        values = projected[:, 2 * local_width :].reshape(slots, heads_local, HEAD_DIM)
        attn = attention_forward(query, keys, values, length, slopes, scale)
        partial_value = matmul(attn, w_out)
        summed = lax.psum(partial_value.astype(jnp.bfloat16), "tensor").astype(jnp.float32)
        hidden_full = tokens_f + summed + out_shift
        normal_full, inverse_full = norm_parts(hidden_full)
        normed_two = (normal_full * gain_two + shift_two).astype(jnp.bfloat16)
        hidden_rows = lax.dynamic_slice_in_dim(hidden_full, row_start, share, 0)
        normal_two = lax.dynamic_slice_in_dim(normal_full, row_start, share, 0)
        inverse_two = lax.dynamic_slice_in_dim(inverse_full, row_start, share, 0)
        pre = matmul(normed_two, w_up) + up_shift
        act_value, act_slope = gelu_parts(pre)
        act = act_value.astype(jnp.bfloat16)
        mlp_part = lax.psum_scatter(
            matmul(act, w_down).astype(jnp.bfloat16), "tensor", scatter_dimension=0, tiled=True
        ).astype(jnp.float32)
        output_rows.append((hidden_rows + mlp_part + down_shift).astype(jnp.bfloat16))
        valid = (jnp.arange(slots, dtype=jnp.int32) < length).astype(jnp.float32)[:, None]
        grad_out = d_output[index].astype(jnp.float32) * valid
        grad_two = grad_out.astype(jnp.bfloat16)
        grad_wdown = grad_wdown + contract_rows(act, grad_two)
        grad_pre = (contract_cols(grad_two, w_down) * act_slope).astype(jnp.bfloat16)
        grad_wup = grad_wup + contract_rows(normed_two, grad_pre)
        grad_bup = grad_bup + jnp.sum(grad_pre.astype(jnp.float32), 0)
        grad_norm_two = lax.psum_scatter(
            contract_cols(grad_pre, w_up).astype(jnp.bfloat16),
            "tensor",
            scatter_dimension=0,
            tiled=True,
        ).astype(jnp.float32)
        grad_gain_two = grad_gain_two + jnp.sum(grad_norm_two * normal_two, 0)
        grad_shift_two = grad_shift_two + jnp.sum(grad_norm_two, 0)
        grad_out_rows = lax.dynamic_slice_in_dim(grad_out, row_start, share, 0)
        grad_hidden_rows = grad_out_rows + norm_backward(
            grad_norm_two, normal_two, inverse_two, gain_two
        )
        grad_one_rows = grad_hidden_rows.astype(jnp.bfloat16)
        grad_down_shift = grad_down_shift + jnp.sum(
            lax.dynamic_slice_in_dim(grad_two, row_start, share, 0).astype(jnp.float32), 0
        )
        grad_out_shift = grad_out_shift + jnp.sum(grad_one_rows.astype(jnp.float32), 0)
        grad_one = lax.all_gather(grad_one_rows, "tensor", axis=0, tiled=True)
        grad_wout = grad_wout + contract_rows(attn, grad_one)
        grad_attn = (
            contract_cols(grad_one, w_out)
            .astype(jnp.bfloat16)
            .reshape(slots, heads_local, HEAD_DIM)
        )
        grad_query, grad_keys, grad_values = attention_backward(
            query, keys, values, grad_attn, length, slopes, scale
        )
        grad_proj = jnp.concatenate([grad_query, grad_keys, grad_values], 1)
        grad_qkv = grad_qkv + contract_rows(normed_one, grad_proj)
        grad_qvb = grad_qvb + jnp.stack(
            [
                jnp.sum(grad_query.astype(jnp.float32), 0),
                jnp.sum(grad_values.astype(jnp.float32), 0),
            ],
            0,
        )
        grad_norm_one = lax.psum_scatter(
            contract_cols(grad_proj, weight_qkv).astype(jnp.bfloat16),
            "tensor",
            scatter_dimension=0,
            tiled=True,
        ).astype(jnp.float32)
        normal_one_rows = lax.dynamic_slice_in_dim(normal_one, row_start, share, 0)
        inverse_one_rows = lax.dynamic_slice_in_dim(inverse_one, row_start, share, 0)
        grad_gain_one = grad_gain_one + jnp.sum(grad_norm_one * normal_one_rows, 0)
        grad_shift_one = grad_shift_one + jnp.sum(grad_norm_one, 0)
        input_rows.append(
            (
                grad_hidden_rows
                + norm_backward(grad_norm_one, normal_one_rows, inverse_one_rows, gain_one)
            ).astype(jnp.bfloat16)
        )
    grad_qkv, grad_qvb, grad_wout, grad_wup, grad_bup, grad_wdown = (
        lax.psum(grad_qkv.astype(jnp.bfloat16), "dp").astype(jnp.float32),
        lax.psum(grad_qvb.astype(jnp.bfloat16), "dp").astype(jnp.float32),
        lax.psum(grad_wout.astype(jnp.bfloat16), "dp").astype(jnp.float32),
        lax.psum(grad_wup.astype(jnp.bfloat16), "dp").astype(jnp.float32),
        lax.psum(grad_bup.astype(jnp.bfloat16), "dp").astype(jnp.float32),
        lax.psum(grad_wdown.astype(jnp.bfloat16), "dp").astype(jnp.float32),
    )
    (
        grad_gain_one,
        grad_shift_one,
        grad_gain_two,
        grad_shift_two,
        grad_out_shift,
        grad_down_shift,
    ) = lax.psum(
        (
            grad_gain_one,
            grad_shift_one,
            grad_gain_two,
            grad_shift_two,
            grad_out_shift,
            grad_down_shift,
        ),
        ("dp", "tensor"),
    )
    return (
        jnp.stack(output_rows, 0),
        jnp.stack(input_rows, 0),
        grad_gain_one,
        grad_shift_one,
        grad_qkv.reshape(width, 3, local_width),
        grad_qvb,
        grad_wout,
        grad_out_shift,
        grad_gain_two,
        grad_shift_two,
        grad_wup,
        grad_bup,
        grad_wdown,
        grad_down_shift,
    )


def solution(mesh):
    whole = mesh.shape["tensor"] == 2 and mesh.shape["dp"] == 2 * len(RING)
    return jax.shard_map(
        whole_sequence if whole else on_device,
        mesh=mesh,
        in_specs=(
            P("dp", None, None),
            P("dp", None, None),
            P("dp"),
            P(),
            P(),
            P(None, None, "tensor"),
            P(None, "tensor"),
            P("tensor", None),
            P(),
            P(),
            P(),
            P(None, "tensor"),
            P("tensor"),
            P("tensor", None),
            P(),
        ),
        out_specs=(
            P("dp", "tensor", None),
            P("dp", "tensor", None),
            P(),
            P(),
            P(None, None, "tensor"),
            P(None, "tensor"),
            P("tensor", None),
            P(),
            P(),
            P(),
            P(None, "tensor"),
            P("tensor"),
            P("tensor", None),
            P(),
        ),
        check_vma=False,
    )
```

```python
import functools
import math

import jax
import jax.numpy as jnp
import numpy as np
from jax import lax
from jax.experimental import pallas as pl
from jax.experimental.pallas import tpu as pltpu
from jax.sharding import PartitionSpec as P

HEADS = 16
HEAD_DIM = 64


epsilon = 1e-05
root_two_pi = math.sqrt(2.0 / math.pi)
masked_score = -1e30


def matmul(left, right):
    return jnp.dot(left, right, preferred_element_type=jnp.float32)


def contract_rows(left, right):
    return lax.dot_general(
        left, right, (((0,), (0,)), ((), ())), preferred_element_type=jnp.float32
    )


def contract_cols(left, right):
    return lax.dot_general(
        left, right, (((1,), (1,)), ((), ())), preferred_element_type=jnp.float32
    )


def norm_parts(values):
    centre = jnp.mean(values, -1, keepdims=True)
    shifted = values - centre
    inverse = lax.rsqrt(jnp.mean(shifted * shifted, -1, keepdims=True) + epsilon)
    return (shifted * inverse, inverse)


def norm_backward(grad_normed, normal, inverse, gain):
    scaled = grad_normed * gain
    return inverse * (
        scaled
        - jnp.mean(scaled, -1, keepdims=True)
        - normal * jnp.mean(scaled * normal, -1, keepdims=True)
    )


def gelu_parts(pre):
    tangent = jnp.tanh(root_two_pi * (pre + 0.044715 * pre * pre * pre))
    value = 0.5 * pre * (1.0 + tangent)
    slope = 0.5 * (1.0 + tangent) + 0.5 * pre * (1.0 - tangent * tangent) * root_two_pi * (
        1.0 + 3.0 * 0.044715 * pre * pre
    )
    return (value, slope)


def block_probs(query_rows, key_rows, start, length, slopes, scale):
    rows = query_rows.shape[0]
    cols = key_rows.shape[0]
    products = jnp.einsum("ihd,jhd->hij", query_rows, key_rows, preferred_element_type=jnp.float32)
    key_place = jnp.arange(cols, dtype=jnp.int32)
    distance = (start + jnp.arange(rows, dtype=jnp.int32))[:, None] - key_place[None, :]
    scores = products * scale - slopes[:, None, None] * distance.astype(jnp.float32)[None]
    allowed = (distance >= 0) & (key_place[None, :] < length)
    masked = jnp.where(allowed[None], scores, masked_score)
    highest = jnp.max(masked, -1, keepdims=True)
    exponent = jnp.exp(masked - highest)
    return exponent / jnp.sum(exponent, -1, keepdims=True)


def attention_forward(query, keys, values, length, slopes, scale):
    slots = query.shape[0]
    block = min(512, slots)
    outputs = []
    for number in range(slots // block):
        start = number * block
        probs = block_probs(query[start : start + block], keys, start, length, slopes, scale)
        mixed = jnp.einsum(
            "hij,jhd->ihd", probs.astype(jnp.bfloat16), values, preferred_element_type=jnp.float32
        )
        outputs.append(mixed.reshape(block, -1).astype(jnp.bfloat16))
    return jnp.concatenate(outputs, 0)


def attention_backward(query, keys, values, grad_attn, length, slopes, scale):
    slots, heads_local, head_width = query.shape
    block = min(512, slots)
    grad_keys = jnp.zeros((slots, heads_local, head_width), jnp.float32)
    grad_values = jnp.zeros((slots, heads_local, head_width), jnp.float32)
    query_parts = []
    for number in range(slots // block):
        start = number * block
        query_rows = query[start : start + block]
        grad_rows = grad_attn[start : start + block]
        probs = block_probs(query_rows, keys, start, length, slopes, scale)
        grad_probs = jnp.einsum(
            "ihd,jhd->hij", grad_rows, values, preferred_element_type=jnp.float32
        )
        delta = jnp.sum(probs * grad_probs, -1, keepdims=True)
        grad_scores = (probs * (grad_probs - delta)).astype(jnp.bfloat16)
        part_query = (
            jnp.einsum("hij,jhd->ihd", grad_scores, keys, preferred_element_type=jnp.float32)
            * scale
        )
        part_keys = (
            jnp.einsum("hij,ihd->jhd", grad_scores, query_rows, preferred_element_type=jnp.float32)
            * scale
        )
        part_values = jnp.einsum(
            "hij,ihd->jhd",
            probs.astype(jnp.bfloat16),
            grad_rows,
            preferred_element_type=jnp.float32,
        )
        part_query, part_keys, part_values = (part_query, part_keys, part_values)
        query_parts.append(part_query)
        grad_keys = grad_keys.at[:slots].add(part_keys)
        grad_values = grad_values.at[:slots].add(part_values)
    grad_query = jnp.concatenate(query_parts, 0).reshape(slots, -1).astype(jnp.bfloat16)
    return (
        grad_query,
        grad_keys.reshape(slots, -1).astype(jnp.bfloat16),
        grad_values.reshape(slots, -1).astype(jnp.bfloat16),
    )


QUERY_BLOCK = 256
KEY_BLOCK = 1024
PAIR = 128
NT = (((1,), (1,)), ((), ()))
TN = (((0,), (0,)), ((), ()))


def mm(left, right, dims=(((1,), (0,)), ((), ()))):
    return lax.dot_general(left, right, dims, preferred_element_type=jnp.float32)


def low_lanes(rows):
    return lax.broadcasted_iota(jnp.int32, (rows, PAIR), 1) < HEAD_DIM


def slope_rows():
    table = np.zeros((HEADS // 2, 8, PAIR), np.float64)
    for head in range(HEADS):
        rest = np.float64(np.float32(2.0 ** (-8.0 * (head + 1) / HEADS)))
        base = HEAD_DIM * (1 - head % 2)
        for part in range(3):
            piece = np.float64(np.asarray(rest).astype(jnp.bfloat16))
            rest = rest - piece
            table[head // 2, head % 2, base + part] = 32.0 * piece
            table[head // 2, head % 2, base + 3 + part] = piece
        table[head // 2, head % 2, base + 6] = 1.0
    return table.astype(jnp.bfloat16)


def key_lanes(slots, length):
    place = jnp.arange(slots, dtype=jnp.int32)[:, None]
    lane = jnp.arange(PAIR, dtype=jnp.int32)[None, :] % HEAD_DIM
    high = (place // 32).astype(jnp.float32)
    low = (place % 32).astype(jnp.float32)
    mask = jnp.where(place < length, 0.0, masked_score)
    return jnp.where(
        lane < 3, high, jnp.where(lane < 6, low, jnp.where(lane == 6, mask, 0.0))
    ).astype(jnp.bfloat16)


def forward_kernel(
    q_ref, k_ref, v_ref, lanes_ref, rows_ref, o_ref, level_ref, key0, key1, val0, val1
):
    slots = q_ref.shape[0]
    block = QUERY_BLOCK
    low = low_lanes(slots)
    zero = jnp.zeros((slots, PAIR), jnp.bfloat16)
    one = jnp.ones((slots, PAIR), jnp.bfloat16)
    key0[...] = jnp.where(low, k_ref[...], lanes_ref[...])
    key1[...] = jnp.where(low, lanes_ref[...], k_ref[...])
    val0[:, :PAIR] = jnp.where(low, v_ref[...], zero)
    val0[:, PAIR:] = jnp.where(low, one, zero)
    val1[:, :PAIR] = jnp.where(low, zero, v_ref[...])
    val1[:, PAIR:] = jnp.where(low, zero, one)
    low_block = low_lanes(block)
    causal = lax.broadcasted_iota(jnp.int32, (block, block), 1) <= lax.broadcasted_iota(
        jnp.int32, (block, block), 0
    )
    for number in range(slots // block):
        start = number * block
        rows = q_ref[start : start + block, :] * jnp.bfloat16(0.125)
        total = None
        tops = []
        for head, (key, val) in enumerate(((key0, val0), (key1, val1))):
            extra = jnp.broadcast_to(rows_ref[0, head : head + 1, :], (block, PAIR))
            query = jnp.where(low_block, rows, extra) if head == 0 else jnp.where(
                low_block, extra, rows
            )
            own = jnp.where(causal, mm(query, key[start : start + block, :], NT), masked_score)
            highest = jnp.max(own, 1, keepdims=True)
            if start:
                past = mm(query, key[:start, :], NT)
                highest = jnp.maximum(highest, jnp.max(past, 1, keepdims=True))
                part = mm(jnp.exp(past - highest).astype(jnp.bfloat16), val[:start, :])
                total = part if total is None else total + part
            part = mm(jnp.exp(own - highest).astype(jnp.bfloat16), val[start : start + block, :])
            total = part if total is None else total + part
            tops.append(highest)
        o_ref[start : start + block, :] = (total[:, :PAIR] / total[:, PAIR:]).astype(jnp.bfloat16)
        level = (jnp.where(low_block, tops[0], tops[1]) + jnp.log(total[:, PAIR:])).T
        level_ref[0, 0:1, start : start + block] = level[0:1, :]
        level_ref[0, 1:2, start : start + block] = level[HEAD_DIM : HEAD_DIM + 1, :]


def fill_pair(k_ref, v_ref, lanes_ref, key0, key1, val0, val1, bare0, bare1):
    slots = k_ref.shape[0]
    low = low_lanes(slots)
    zero = jnp.zeros((slots, PAIR), jnp.bfloat16)
    key0[...] = jnp.where(low, k_ref[...], lanes_ref[...])
    key1[...] = jnp.where(low, lanes_ref[...], k_ref[...])
    bare0[...] = jnp.where(low, k_ref[...], zero)
    bare1[...] = jnp.where(low, zero, k_ref[...])
    val0[...] = jnp.where(low, v_ref[...], zero)
    val1[...] = jnp.where(low, zero, v_ref[...])


def pair_grads(
    query, mixed, gradient, level_ref, rows_ref, total_q,
    key0, key1, val0, val1, bare0, bare1, total_k, total_v, between,
):
    slots = query.shape[0]
    block = QUERY_BLOCK
    piece = KEY_BLOCK
    low_block = low_lanes(block)
    nil = jnp.zeros((block, PAIR), jnp.bfloat16)
    causal = lax.broadcasted_iota(jnp.int32, (block, block), 0) <= lax.broadcasted_iota(
        jnp.int32, (block, block), 1
    )
    for number in reversed(range(slots // block)):
        start = number * block
        stop = start + block
        rows = query[start:stop, :] * jnp.bfloat16(0.125)
        grad = gradient[start:stop, :]
        shares = (grad.astype(jnp.float32) * mixed[start:stop, :].astype(jnp.float32)).T
        deltas = [
            jnp.sum(shares[head * HEAD_DIM : (head + 1) * HEAD_DIM, :], 0, keepdims=True)
            for head in range(2)
        ]
        levels = [level_ref[0, head : head + 1, start:stop] for head in range(2)]
        extras = [jnp.broadcast_to(rows_ref[0, h : h + 1, :], (block, PAIR)) for h in range(2)]
        queries = (
            jnp.where(low_block, rows, extras[0]),
            jnp.where(low_block, extras[1], rows),
        )
        grads = jnp.concatenate(
            [jnp.where(low_block, grad, nil), jnp.where(low_block, nil, grad)], 0
        )
        both = jnp.concatenate(
            [jnp.where(low_block, rows, nil), jnp.where(low_block, nil, rows)], 0
        )
        grad_query = None
        for begin in range(0, stop, min(piece, stop)):
            end = min(begin + piece, stop)
            probs, scores = [], []
            for head, (key, val, bare) in enumerate(((key0, val0, bare0), (key1, val1, bare1))):
                score = mm(key[begin:end, :], queries[head], NT)
                if end > start:
                    own = jnp.where(causal, score[start - begin :], masked_score)
                    score = jnp.concatenate([score[: start - begin], own], 0) if start > begin else own
                prob = jnp.exp(score - levels[head])
                grad_prob = mm(val[begin:end, :], grad, NT)
                grad_score = (prob * (grad_prob - deltas[head])).astype(jnp.bfloat16)
                probs.append(prob.astype(jnp.bfloat16))
                scores.append(grad_score)
                part = mm(grad_score, bare[begin:end, :], TN)
                grad_query = part if grad_query is None else grad_query + part
            part_v = mm(jnp.concatenate(probs, 1), grads)
            part_k = mm(jnp.concatenate(scores, 1), both)
            if stop == slots:
                total_v[begin:end, :] = part_v
                total_k[begin:end, :] = part_k
            else:
                total_v[begin:end, :] += part_v
                total_k[begin:end, :] += part_k
        total_q[start:stop, :] = (grad_query * 0.125).astype(jnp.bfloat16)
        if stop == slots:
            between()


def pair_specs(slots):
    part = pl.BlockSpec((slots, PAIR), lambda pair: (0, pair))
    lanes = pl.BlockSpec((slots, PAIR), lambda pair: (0, 0))
    rows = pl.BlockSpec((1, 8, PAIR), lambda pair: (pair, 0, 0))
    levels = pl.BlockSpec((1, 8, slots), lambda pair: (pair, 0, 0))
    return part, lanes, rows, levels


def attention_out(query, keys, values, lanes, rows):
    slots, columns = query.shape
    part, lane_spec, row_spec, level_spec = pair_specs(slots)
    pairs = columns // PAIR
    half = slots * slots * PAIR * pairs
    return pl.pallas_call(
        forward_kernel,
        grid=(pairs,),
        out_shape=(
            jax.ShapeDtypeStruct((slots, columns), jnp.bfloat16),
            jax.ShapeDtypeStruct((pairs, 8, slots), jnp.float32),
        ),
        in_specs=[part, part, part, lane_spec, row_spec],
        out_specs=(part, level_spec),
        scratch_shapes=[pltpu.VMEM((slots, PAIR), jnp.bfloat16)] * 2
        + [pltpu.VMEM((slots, 2 * PAIR), jnp.bfloat16)] * 2,
        cost_estimate=pl.CostEstimate(
            flops=8 * half, bytes_accessed=8 * slots * columns, transcendentals=slots * slots * pairs
        ),
        name="attention_out",
    )(query, keys, values, lanes, rows)


ROW_BLOCK = 256


def whole_spec(array):
    zeros = (0,) * array.ndim
    return pl.BlockSpec(array.shape, lambda *_: zeros)


def row_spec(columns):
    return pl.BlockSpec((ROW_BLOCK, columns), lambda row, *_: (row, 0))


def own_spec(columns):
    return pl.BlockSpec((1, ROW_BLOCK, columns), lambda row, facts: (facts[0], row, 0))


def over_rows(kernel, name, slots, facts, inputs, outputs, flops):
    arrays, in_specs = zip(*inputs)
    shapes, out_specs = zip(*outputs)
    return pl.pallas_call(
        kernel,
        grid_spec=pltpu.PrefetchScalarGridSpec(
            num_scalar_prefetch=1,
            grid=(slots // ROW_BLOCK,),
            in_specs=list(in_specs),
            out_specs=list(out_specs),
        ),
        out_shape=list(shapes),
        cost_estimate=pl.CostEstimate(
            flops=flops,
            bytes_accessed=sum(array.size * array.dtype.itemsize for array in arrays),
            transcendentals=0,
        ),
        name=name,
    )(facts, *arrays)


def project_kernel(facts, tok_ref, gain_ref, shift_ref, w_ref, bias_ref, norm_ref, q_ref, k_ref, v_ref):
    normal, _ = norm_parts(tok_ref[0].astype(jnp.float32))
    normed = (normal * gain_ref[...] + shift_ref[...]).astype(jnp.bfloat16)
    norm_ref[...] = normed
    q_ref[...] = (mm(normed, w_ref[0]) + bias_ref[0:1, :]).astype(jnp.bfloat16)
    k_ref[...] = mm(normed, w_ref[1]).astype(jnp.bfloat16)
    v_ref[...] = (mm(normed, w_ref[2]) + bias_ref[1:2, :]).astype(jnp.bfloat16)


def hidden_kernel(
    facts, tok_ref, a0_ref, a1_ref, w0_ref, w1_ref, bias_ref, gain_ref, shift_ref, hid_ref, norm_ref
):
    hidden = tok_ref[0].astype(jnp.float32) + bias_ref[...]
    hidden = hidden + mm(a0_ref[...], w0_ref[...]) + mm(a1_ref[...], w1_ref[...])
    hid_ref[...] = hidden
    normal, _ = norm_parts(hidden)
    norm_ref[...] = (normal * gain_ref[...] + shift_ref[...]).astype(jnp.bfloat16)


def act_kernel(norm_ref, w_ref, bias_ref, act_ref, slope_ref):
    def rows(number, carry):
        at = pl.ds(pl.multiple_of(number * ROW_BLOCK, ROW_BLOCK), ROW_BLOCK)
        value, slope = gelu_parts(mm(norm_ref[at, :], w_ref[...]) + bias_ref[...])
        act_ref[at, :] = value.astype(jnp.bfloat16)
        slope_ref[at, :] = slope.astype(jnp.bfloat16)
        return carry

    lax.fori_loop(0, norm_ref.shape[0] // ROW_BLOCK, rows, 0, unroll=True)


def activations(normed, weight, bias):
    slots, width = normed.shape
    hidden = weight.shape[1]
    columns = 512
    out = pl.BlockSpec((slots, columns), lambda col: (0, col))
    shape = jax.ShapeDtypeStruct((slots, hidden), jnp.bfloat16)
    return pl.pallas_call(
        act_kernel,
        grid=(hidden // columns,),
        in_specs=[
            whole_spec(normed),
            pl.BlockSpec((width, columns), lambda col: (0, col)),
            pl.BlockSpec((1, columns), lambda col: (0, col)),
        ],
        out_specs=(out, out),
        out_shape=(shape, shape),
        cost_estimate=pl.CostEstimate(
            flops=2 * slots * width * hidden,
            bytes_accessed=8 * slots * hidden,
            transcendentals=slots * hidden,
        ),
        name="activations",
    )(normed, weight, bias)


def output_kernel(facts, hid_ref, a0_ref, a1_ref, w0_ref, w1_ref, bias_ref, tie_ref, out_ref):
    total = hid_ref[...] + bias_ref[...] + mm(a0_ref[...], w0_ref[...])
    out_ref[...] = (total + mm(a1_ref[...], w1_ref[...])).astype(jnp.bfloat16)


def add_sums(sums_ref, rows):
    @pl.when(pl.program_id(0) == 0)
    def _():
        sums_ref[...] = jnp.zeros_like(sums_ref)

    for index, value in enumerate(rows):
        sums_ref[index : index + 1, :] += jnp.sum(value, 0, keepdims=True)


def hidden_grad_kernel(
    facts, g0_ref, g1_ref, w0_ref, w1_ref, hid_ref, gain_ref, dout_ref, grad_ref, one_ref, sums_ref
):
    grad_norm = mm(g0_ref[...], w0_ref[...], NT) + mm(g1_ref[...], w1_ref[...], NT)
    normal, inverse = norm_parts(hid_ref[...])
    place = lax.broadcasted_iota(jnp.int32, grad_norm.shape, 0) + pl.program_id(0) * ROW_BLOCK
    grad_out = jnp.where(place < facts[1], dout_ref[0].astype(jnp.float32), 0.0)
    grad = grad_out + norm_backward(grad_norm, normal, inverse, gain_ref[...])
    one = grad.astype(jnp.bfloat16)
    grad_ref[...] = grad
    one_ref[...] = one
    add_sums(sums_ref, [grad_norm * normal, grad_norm, one.astype(jnp.float32), grad_out])


def token_grad_kernel(
    facts, q0_ref, k0_ref, v0_ref, q1_ref, k1_ref, v1_ref, w0_ref, w1_ref, tok_ref, grad_ref,
    gain_ref, out_ref, sums_ref, heads_ref,
):
    grad_norm = None
    for refs, weight in (((q0_ref, k0_ref, v0_ref), w0_ref), ((q1_ref, k1_ref, v1_ref), w1_ref)):
        for part, ref in enumerate(refs):
            more = mm(ref[...], weight[part], NT)
            grad_norm = more if grad_norm is None else grad_norm + more
    normal, inverse = norm_parts(tok_ref[0].astype(jnp.float32))
    grad = grad_ref[...] + norm_backward(grad_norm, normal, inverse, gain_ref[...])
    out_ref[...] = grad.astype(jnp.bfloat16)
    add_sums(sums_ref, [grad_norm * normal, grad_norm])
    add_sums(heads_ref, [ref[...].astype(jnp.float32) for ref in (q0_ref, q1_ref, v0_ref, v1_ref)])


RING = ((0, 0), (1, 0), (2, 0), (3, 0), (3, 1), (2, 1), (1, 1), (0, 1))
RING_CUTS = 2


def device_of(z, y, core):
    return (z * 2 + y) * 2 + core


def to_tensor(value):
    return lax.ppermute(value, "tensor", [(0, 1), (1, 0)])


def to_core(value):
    return lax.ppermute(value, "dp", [(i, i ^ 1) for i in range(2 * len(RING))])


def rows_at(value, start, size):
    return lax.dynamic_slice_in_dim(value, start, size, value.ndim - 2)


def after(value, *earlier):
    return lax.optimization_barrier((value, *earlier))[0]


def piece_over_x(weight, index, pieces, *earlier):
    size = weight.shape[-2] // pieces
    return to_tensor(after(rows_at(weight, index * size, size), *earlier))


def both_cores(value, core, axis):
    beside = to_core(value)
    first = jnp.where(core == 0, value, beside)
    second = jnp.where(core == 0, beside, value)
    return jnp.concatenate([first, second], axis)


class Ring:
    def __init__(self, values, slots, sums, results, sems, cuts):
        self.values, self.slots, self.sums, self.results = values, slots, sums, results
        self.send_sems, self.recv_sems, self.swap_send_sems, self.swap_recv_sems = sems
        self.cuts = cuts
        self.count = count = len(RING)
        self.device = device = lax.axis_index("dp")
        self.core, self.y, self.z = lax.rem(device, 2), lax.rem(device // 2, 2), device // 4
        self.place = place = self.z * (1 - self.y) + (count - 1 - self.z) * self.y
        self.nexts = tuple(
            self.at_place(lax.rem(place + step, count)) for step in (1, count - 1)
        )
        self.partner = {"dp": device + 1 - 2 * self.core}
        self.streams = [
            (array, way, cut)
            for array in range(len(values))
            for way in range(2)
            for cut in range(cuts)
        ]

    def at_place(self, where):
        side = where // 4
        return {
            "dp": device_of(where * (1 - side) + (self.count - 1 - where) * side, side, self.core)
        }

    def greet(self, others=()):
        barrier = pltpu.get_barrier_semaphore()
        greeted = [*self.nexts, self.partner, *others]
        for target in greeted:
            pl.semaphore_signal(
                barrier, inc=1, device_id=target, device_id_type=pl.DeviceIdType.MESH
            )
        pl.semaphore_wait(barrier, len(greeted))

    def block(self, way, offset):
        return lax.rem(self.place - (1, -1)[way] * offset + 2 * self.count, self.count)

    def rows(self, array, cut):
        size = self.values[array].shape[2] // self.cuts
        return pl.ds(cut * size, size)

    def result(self, stream, step):
        array, way, cut = stream
        return self.results[array].at[
            self.core, way, self.block(way, step), self.rows(array, cut)
        ]

    def copy(self, stream, step):
        array, way, cut = stream
        rows = self.rows(array, cut)
        if step < self.count - 1:
            target = self.slots[array].at[way, step, rows]
            if step:
                source = self.sums[array].at[way, step - 1, rows]
            else:
                source = self.values[array].at[way, self.block(way, 0), rows]
        else:
            source = target = self.result(stream, step)
        index = self.streams.index(stream)
        return pltpu.make_async_remote_copy(
            src_ref=source,
            dst_ref=target,
            send_sem=self.send_sems.at[index, step],
            recv_sem=self.recv_sems.at[index, step],
            device_id=self.nexts[way],
            device_id_type=pl.DeviceIdType.MESH,
        )

    def swap(self, stream, step):
        index = self.streams.index(stream)
        turn = step - self.count + 1
        done = self.result(stream, step)
        return pltpu.make_async_remote_copy(
            src_ref=done,
            dst_ref=done,
            send_sem=self.swap_send_sems.at[index, turn],
            recv_sem=self.swap_recv_sems.at[index, turn],
            device_id=self.partner,
            device_id_type=pl.DeviceIdType.MESH,
        )

    def first(self):
        for stream in self.streams:
            self.copy(stream, 0).start()

    def hop(self, step):
        count = self.count
        for stream in self.streams:
            array, way, cut = stream
            rows = self.rows(array, cut)
            self.copy(stream, step - 1).wait_recv()
            if step < count:
                total = self.values[array][way, self.block(way, step), rows].astype(jnp.float32)
                total = total + self.slots[array][way, step - 1, rows].astype(jnp.float32)
                total = total.astype(jnp.bfloat16)
                if step < count - 1:
                    self.sums[array][way, step - 1, rows] = total
                else:
                    self.results[array][self.core, way, self.block(way, step), rows] = total
            self.copy(stream, step).start()
            if step >= count - 1:
                self.swap(stream, step).start()

    def last(self):
        for stream in self.streams:
            self.copy(stream, 2 * self.count - 3).wait_recv()
            self.swap(stream, 2 * self.count - 2).start()

    def drain(self):
        for stream in self.streams:
            for step in range(2 * self.count - 2):
                self.copy(stream, step).wait_send()
            for step in range(self.count - 1, 2 * self.count - 1):
                self.swap(stream, step).wait()


def ring_shape(value):
    count = len(RING)
    return value.reshape(2, count, value.shape[0] // (2 * count), value.shape[1])


def ring_scratch(shaped, cuts):
    count = len(RING)
    streams = 2 * len(shaped) * cuts
    scratch = [pltpu.VMEM((2, count - 1, *value.shape[2:]), value.dtype) for value in shaped]
    scratch += [pltpu.VMEM((2, count - 2, *value.shape[2:]), value.dtype) for value in shaped]
    scratch += [pltpu.SemaphoreType.DMA((streams, 2 * count - 2))] * 2
    return scratch + [pltpu.SemaphoreType.DMA((streams, count))] * 2


def ring_kernel(blocks, cuts, has_small, has_tie, *refs):
    values, refs = refs[:blocks], refs[blocks:]
    if has_small:
        small_ref, refs = refs[0], refs[1:]
    refs = refs[has_tie:]
    results, refs = refs[:blocks], refs[blocks:]
    if has_small:
        small_out, refs = refs[0], refs[1:]
    slots, refs = refs[:blocks], refs[blocks:]
    sums, refs = refs[:blocks], refs[blocks:]
    ring = Ring(values, slots, sums, results, refs[:4], cuts)
    if has_small:
        small_slots, small_sums, small_send_sems, small_recv_sems = refs[4:]
        device, y, z = ring.device, ring.y, ring.z
        small_targets = [
            ring.partner,
            {"tensor": 1 - lax.axis_index("tensor")},
            {"dp": device + 2 - 4 * y},
            {"dp": device + 4 - 8 * lax.rem(z, 2)},
            {"dp": device + 8 - 16 * (z // 2)},
        ]
        ring.greet(small_targets[1:])
    else:
        ring.greet()

    def exchange(turn):
        return pltpu.make_async_remote_copy(
            src_ref=small_ref if turn == 0 else small_sums.at[turn - 1],
            dst_ref=small_slots.at[turn],
            send_sem=small_send_sems.at[turn],
            recv_sem=small_recv_sems.at[turn],
            device_id=small_targets[turn],
            device_id_type=pl.DeviceIdType.MESH,
        )

    def take_exchange(turn):
        exchange(turn).wait_recv()
        total = (small_ref[...] if turn == 0 else small_sums[turn - 1]) + small_slots[turn]
        if turn == len(small_targets) - 1:
            small_out[...] = total
        else:
            small_sums[turn] = total
            exchange(turn + 1).start()

    ring.first()
    if has_small:
        exchange(0).start()
    for step in range(1, 2 * ring.count - 2):
        if has_small and step % 2 == 0 and step // 2 <= len(small_targets):
            take_exchange(step // 2 - 1)
        ring.hop(step)
    ring.last()
    ring.drain()
    if has_small:
        for turn in range(len(small_targets)):
            exchange(turn).wait_send()


def plane_sums(values, identity, small=None, tie=None, cuts=1):
    blocks = len(values)
    shaped = [ring_shape(value) for value in values]
    size = sum(value.size for value in values)
    vmem = pl.BlockSpec(memory_space=pltpu.VMEM)
    inputs, in_specs = list(shaped), [vmem] * blocks
    shapes = [jax.ShapeDtypeStruct((2, *value.shape), value.dtype) for value in shaped]
    scratch = ring_scratch(shaped, cuts)
    if small is not None:
        inputs.append(small)
        in_specs.append(vmem)
        shapes.append(jax.ShapeDtypeStruct(small.shape, small.dtype))
        scratch += [pltpu.VMEM((5, *small.shape), small.dtype)] * 2
        scratch += [pltpu.SemaphoreType.DMA((5,))] * 2
    if tie is not None:
        inputs.append(tie)
        in_specs.append(pl.BlockSpec(memory_space=pl.ANY))
    results = pl.pallas_call(
        functools.partial(ring_kernel, blocks, cuts, small is not None, int(tie is not None)),
        out_shape=shapes,
        in_specs=in_specs,
        out_specs=[vmem] * len(shapes),
        scratch_shapes=scratch,
        compiler_params=pltpu.CompilerParams(collective_id=identity, has_side_effects=True),
        cost_estimate=pl.CostEstimate(flops=size, bytes_accessed=6 * size, transcendentals=0),
        name="plane_sums",
    )(*inputs)
    sums = [
        result.reshape(2 * value.shape[0], value.shape[1]) for result, value in zip(results, values)
    ]
    return sums if small is None else (sums, results[-1])


def grads_ring_kernel(
    q0_ref, k0_ref, v0_ref, o0_ref, g0_ref, q1_ref, k1_ref, v1_ref, o1_ref, g1_ref,
    level_ref, lanes_ref, rows_ref, value_ref,
    dq0_ref, dk0_ref, dv0_ref, dq1_ref, dk1_ref, dv1_ref, sum_ref,
    query, mixed, grad, key0, key1, val0, val1, bare0, bare1, total_q, total_k, total_v,
    result, slots, sums, send_sems, recv_sems, swap_send_sems, swap_recv_sems, out_sem,
):
    pair = pl.program_id(0)
    pairs = HEADS // 2
    ring = Ring(
        [value_ref], [slots], [sums], [result],
        (send_sems, recv_sems, swap_send_sems, swap_recv_sems), RING_CUTS,
    )

    def turn(number):
        if number == 0:
            ring.greet()
            ring.first()
        elif number < 2 * ring.count - 2:
            ring.hop(number)
        elif number == 2 * ring.count - 2:
            ring.last()
        else:
            ring.drain()
            out = pltpu.make_async_copy(result, sum_ref, out_sem)
            out.start()
            out.wait()

    def turns(second):
        for number in range(pairs):
            pl.when(pair == number)(functools.partial(turn, 2 * number + second))

    def take(q_ref, k_ref, v_ref, o_ref, g_ref):
        query[...] = q_ref[...]
        mixed[...] = o_ref[...]
        grad[...] = g_ref[...]
        fill_pair(k_ref, v_ref, lanes_ref, key0, key1, val0, val1, bare0, bare1)

    def give(dq_ref, dk_ref, dv_ref):
        dq_ref[...] = total_q[...]
        dk_ref[...] = total_k[...].astype(jnp.bfloat16)
        dv_ref[...] = total_v[...].astype(jnp.bfloat16)

    turns(0)
    pl.when(pair < pairs // 2)(lambda: take(q0_ref, k0_ref, v0_ref, o0_ref, g0_ref))
    pl.when(pair >= pairs // 2)(lambda: take(q1_ref, k1_ref, v1_ref, o1_ref, g1_ref))
    pair_grads(
        query, mixed, grad, level_ref, rows_ref, total_q,
        key0, key1, val0, val1, bare0, bare1, total_k, total_v, lambda: turns(1),
    )
    pl.when(pair < pairs // 2)(lambda: give(dq0_ref, dk0_ref, dv0_ref))
    pl.when(pair >= pairs // 2)(lambda: give(dq1_ref, dk1_ref, dv1_ref))


def attention_grads_ring(first, second, levels, lanes, rows, value):
    slots, columns = first[0].shape
    half = columns // PAIR
    shaped = ring_shape(value)
    whole = jax.ShapeDtypeStruct((2, *shaped.shape), value.dtype)

    part0 = pl.BlockSpec((slots, PAIR), lambda pair: (0, pair - (pair // half) * (pair - half + 1)))
    part1 = pl.BlockSpec((slots, PAIR), lambda pair: (0, (pair // half) * (pair - half)))
    shape = jax.ShapeDtypeStruct((slots, columns), jnp.bfloat16)
    work = slots * slots * PAIR * 2 * half
    *grads, total = pl.pallas_call(
        grads_ring_kernel,
        grid=(2 * half,),
        out_shape=[shape] * 6 + [whole],
        in_specs=[part0] * 5
        + [part1] * 5
        + [
            pl.BlockSpec((1, 8, slots), lambda pair: (pair, 0, 0)),
            pl.BlockSpec((slots, PAIR), lambda pair: (0, 0)),
            pl.BlockSpec((1, 8, PAIR), lambda pair: (pair, 0, 0)),
            pl.BlockSpec(shaped.shape, lambda pair: (0, 0, 0, 0)),
        ],
        out_specs=[part0] * 3 + [part1] * 3 + [pl.BlockSpec(memory_space=pl.ANY)],
        scratch_shapes=[pltpu.VMEM((slots, PAIR), jnp.bfloat16)] * 10
        + [pltpu.VMEM((slots, PAIR), jnp.float32)] * 2
        + [pltpu.VMEM(whole.shape, whole.dtype)]
        + ring_scratch([shaped], RING_CUTS)
        + [pltpu.SemaphoreType.DMA],
        compiler_params=pltpu.CompilerParams(collective_id=3, has_side_effects=True),
        cost_estimate=pl.CostEstimate(
            flops=20 * work,
            bytes_accessed=32 * slots * columns,
            transcendentals=2 * slots * slots * half,
        ),
        name="attention_grads_ring",
    )(*first, *second, levels, lanes, rows, shaped)
    return grads[:3], grads[3:], total.reshape(2 * value.shape[0], value.shape[1])


def core_send(left, rights, core):
    half = left.shape[1] // 2
    sent = lax.dynamic_slice_in_dim(left, (1 - core) * half, half, 1)
    return [to_core(contract_rows(sent, right).astype(jnp.bfloat16)) for right in rights]


def core_sum(left, rights, arrived, core):
    half = left.shape[1] // 2
    kept = lax.dynamic_slice_in_dim(left, core * half, half, 1)
    return [
        contract_rows(kept, right) + part.astype(jnp.float32)
        for right, part in zip(rights, arrived)
    ]


def start_grad(left, rights, core):
    other = core_send(left[1], rights[1], core)
    local = core_send(left[0], rights[0], core)
    summed = [
        part.astype(jnp.bfloat16) for part in core_sum(left[1], rights[1], other, core)
    ]
    return local, summed, [to_tensor(part) for part in summed]


def pair_grad(left, rights, local, passed, core):
    mine = [
        (part + more.astype(jnp.float32)).astype(jnp.bfloat16)
        for part, more in zip(core_sum(left, rights, local, core), passed)
    ]
    return mine


def trade_rows(value, own):
    share = value.shape[0] // 2
    arrived = to_tensor(lax.dynamic_slice_in_dim(value, (1 - own) * share, share, 0))
    kept = lax.dynamic_slice_in_dim(value, own * share, share, 0)
    return jnp.stack(
        [jnp.where(own == 0, kept, arrived), jnp.where(own == 0, arrived, kept)], 0
    )


def whole_sequence(
    tokens,
    d_output,
    lengths,
    ln1_gain,
    ln1_bias,
    w_qkv,
    qv_bias,
    w_out,
    bias_out,
    ln2_gain,
    ln2_bias,
    w_up,
    b_up,
    w_down,
    b_down,
):
    own = lax.axis_index("tensor")
    device = lax.axis_index("dp")
    core = device % 2
    slots, width = tokens.shape[1:]
    local_width = w_qkv.shape[2]
    hidden_local = w_up.shape[1]
    table = jnp.asarray(slope_rows())
    pairs = local_width // PAIR
    f32 = jnp.float32

    weight_qkv = w_qkv.transpose(1, 0, 2)
    biases = jnp.concatenate([qv_bias.reshape(-1), b_up])
    other_biases = to_tensor(biases)
    far_qkv = piece_over_x(weight_qkv, core, 2)
    far_up = piece_over_x(w_up, device, 2 * len(RING))
    qv = [b[: 2 * local_width].reshape(2, local_width).astype(f32) for b in (biases, other_biases)]
    ups = [b[2 * local_width :].astype(f32)[None] for b in (biases, other_biases)]
    rows = [lax.dynamic_slice_in_dim(table, index * pairs, pairs, 0) for index in (own, 1 - own)]
    gain_one, shift_one = ln1_gain.astype(f32)[None], ln1_bias.astype(f32)[None]
    gain_two, shift_two = ln2_gain.astype(f32)[None], ln2_bias.astype(f32)[None]

    length = lax.dynamic_index_in_dim(lengths, own, 0, keepdims=False)
    facts = jnp.stack([own.astype(jnp.int32), length])
    lanes = key_lanes(slots, length)
    low = jnp.bfloat16

    def run(kernel, name, inputs, outputs, flops):
        return over_rows(kernel, name, slots, facts, inputs, outputs, flops)

    def fixed(array):
        return array, whole_spec(array)

    def by_row(array):
        return array, row_spec(array.shape[1])

    def rows_out(columns, dtype):
        return jax.ShapeDtypeStruct((slots, columns), dtype), row_spec(columns)

    def sums_out(columns):
        shape = jax.ShapeDtypeStruct((8, columns), f32)
        return shape, whole_spec(shape)

    square = 2 * slots * width
    tokens_in, d_output_in = (tokens, own_spec(width)), (d_output, own_spec(width))
    normed_one, *local_heads = run(
        project_kernel,
        "project",
        [tokens_in, fixed(gain_one), fixed(shift_one), fixed(weight_qkv), fixed(qv[0])],
        [rows_out(width, low)] + [rows_out(local_width, low)] * 3,
        3 * square * local_width,
    )
    attn, level = attention_out(*local_heads, lanes, rows[0])
    heads, mixed, levels = [tuple(local_heads)], [attn], [level]
    far_down = piece_over_x(w_down, device, 2 * len(RING), normed_one)
    far_out = piece_over_x(w_out, core, 2, normed_one)
    up = (w_up, lax.all_gather(after(far_up, normed_one), "dp", axis=0, tiled=True))
    down = (w_down, lax.all_gather(after(far_down, attn), "dp", axis=0, tiled=True))
    qkv = (weight_qkv, both_cores(far_qkv, core, 1))
    query = (matmul(normed_one, qkv[1][0]) + qv[1][0]).astype(low)
    keys = matmul(normed_one, qkv[1][1]).astype(low)
    values = (matmul(normed_one, qkv[1][2]) + qv[1][1]).astype(low)
    heads.append((query, keys, values))
    attn, level = attention_out(query, keys, values, lanes, rows[1])
    mixed.append(attn)
    levels.append(level)
    out = (w_out, both_cores(far_out, core, 0))
    hidden, normed_two = run(
        hidden_kernel,
        "hidden_state",
        [tokens_in, by_row(mixed[0]), by_row(mixed[1]), fixed(out[0]), fixed(out[1])]
        + [fixed(bias_out.astype(f32)[None]), fixed(gain_two), fixed(shift_two)],
        [rows_out(width, f32), rows_out(width, low)],
        2 * square * local_width,
    )
    acts = [activations(normed_two, up[half], ups[half]) for half in range(2)]

    valid = (jnp.arange(slots, dtype=jnp.int32) < length).astype(f32)[:, None]
    grad_out = lax.dynamic_index_in_dim(d_output, own, 0, keepdims=False).astype(f32) * valid
    grad_two = grad_out.astype(low)
    left_down, right_down = (acts[0][0], acts[1][0]), ([grad_two], [grad_two])
    local_down, sent_down, passed_down = start_grad(left_down, right_down, core)
    late_two = after(grad_two, *sent_down, *local_down)
    grad_pre = [
        (contract_cols(late_two, down[half]) * acts[half][1].astype(f32)).astype(low)
        for half in range(2)
    ]
    left_up, right_up = (normed_two, normed_two), ([grad_pre[0]], [grad_pre[1]])
    local_up, sent_up, passed_up = start_grad(left_up, right_up, core)
    late_pre = lax.optimization_barrier((*grad_pre, *sent_up, *local_up))
    grad_hidden, grad_one, sums_two = run(
        hidden_grad_kernel,
        "hidden_grad",
        [by_row(late_pre[0]), by_row(late_pre[1]), fixed(up[0]), fixed(up[1]), by_row(hidden)]
        + [fixed(gain_two), d_output_in],
        [rows_out(width, f32), rows_out(width, low), sums_out(width)],
        2 * square * hidden_local,
    )
    tie = (sent_up[0], pl.BlockSpec(memory_space=pl.ANY))
    (result,) = run(
        output_kernel,
        "layer_output",
        [by_row(hidden), by_row(acts[0][0]), by_row(acts[1][0]), fixed(down[0]), fixed(down[1])]
        + [fixed(b_down.astype(f32)[None]), tie],
        [rows_out(width, low)],
        2 * square * hidden_local,
    )
    output = trade_rows(result, own)
    left_out, right_out = (mixed[0], mixed[1]), ([grad_one], [grad_one])
    local_out, sent_out, passed_out = start_grad(left_out, right_out, core)
    late_one = after(grad_one, *sent_out, *local_out)
    grad_attn = [contract_cols(late_one, out[half]).astype(low) for half in range(2)]
    mine_down = pair_grad(left_down[0], right_down[0], local_down, passed_down, core)
    *grads, grad_wdown = attention_grads_ring(
        (*heads[0], mixed[0], grad_attn[0]),
        (*heads[1], mixed[1], grad_attn[1]),
        jnp.concatenate(levels, 0),
        lanes,
        jnp.concatenate(rows, 0),
        mine_down[0],
    )
    local_qkv, sent_qkv, passed_qkv = start_grad((normed_one, normed_one), grads, core)
    grad_tokens, sums_one, sums_heads = run(
        token_grad_kernel,
        "token_grad",
        [by_row(part) for part in (*grads[0], *grads[1])]
        + [fixed(qkv[0]), fixed(qkv[1]), tokens_in, by_row(grad_hidden), fixed(gain_one)],
        [rows_out(width, low), sums_out(width), sums_out(local_width)],
        6 * square * local_width,
    )
    grad_tokens = trade_rows(grad_tokens, own)

    def in_place(first, second):
        return jnp.concatenate(
            [jnp.where(own == 0, first, second), jnp.where(own == 0, second, first)], 0
        )

    bias_up = [jnp.sum(grad_pre[half].astype(f32), 0) for half in range(2)]
    small = jnp.concatenate(
        [
            sums_one[:2],
            sums_two[:4],
            in_place(sums_heads[0], sums_heads[1]).reshape(1, width),
            in_place(sums_heads[2], sums_heads[3]).reshape(1, width),
            in_place(*bias_up).reshape(-1, width),
        ],
        0,
    )
    small = jnp.pad(small, ((0, 16 - small.shape[0]), (0, 0)))
    mine_up = pair_grad(left_up[0], right_up[0], local_up, passed_up, core)
    (grad_wup,) = plane_sums(mine_up, 1, tie=sent_qkv[0], cuts=RING_CUTS)
    mine_out = pair_grad(left_out[0], right_out[0], local_out, passed_out, core)
    mine_qkv = pair_grad(normed_one, grads[0], local_qkv, passed_qkv, core)
    (grad_wout, *grad_wqkv), small = plane_sums(mine_out + mine_qkv, 2, small, grad_wup)
    grad_wqkv = jnp.stack(grad_wqkv, 0).astype(f32)
    wide = [lax.dynamic_slice_in_dim(small[i], own * local_width, local_width, 0) for i in (6, 7)]
    grad_bup = lax.dynamic_slice_in_dim(
        small[8:12].reshape(-1), own * hidden_local, hidden_local, 0
    )
    return (
        output,
        grad_tokens,
        small[0],
        small[1],
        grad_wqkv.transpose(1, 0, 2),
        jnp.stack(wide, 0),
        grad_wout.astype(f32),
        small[4],
        small[2],
        small[3],
        grad_wup.astype(f32),
        grad_bup,
        grad_wdown.astype(f32),
        small[5],
    )


def on_device(
    tokens,
    d_output,
    lengths,
    ln1_gain,
    ln1_bias,
    w_qkv,
    qv_bias,
    w_out,
    bias_out,
    ln2_gain,
    ln2_bias,
    w_up,
    b_up,
    w_down,
    b_down,
):
    parts = lax.axis_size("tensor")
    place = lax.axis_index("tensor")
    batches, slots, width = tokens.shape
    share = slots // parts
    row_start = place * share
    local_width = w_qkv.shape[2]
    hidden_local = w_up.shape[1]
    heads_local = local_width // HEAD_DIM
    scale = 1.0 / math.sqrt(HEAD_DIM)
    first_head = place * heads_local
    slopes = jnp.exp2(
        -8.0
        * ((first_head + jnp.arange(heads_local, dtype=jnp.int32)).astype(jnp.float32) + 1.0)
        / HEADS
    )
    weight_qkv = w_qkv.reshape(width, 3 * local_width)
    qkv_shift = jnp.concatenate(
        [
            qv_bias[0].astype(jnp.float32),
            jnp.zeros((local_width,), jnp.float32),
            qv_bias[1].astype(jnp.float32),
        ]
    )
    gain_one = ln1_gain.astype(jnp.float32)
    shift_one = ln1_bias.astype(jnp.float32)
    gain_two = ln2_gain.astype(jnp.float32)
    shift_two = ln2_bias.astype(jnp.float32)
    out_shift = bias_out.astype(jnp.float32)
    up_shift = b_up.astype(jnp.float32)
    down_shift = b_down.astype(jnp.float32)
    grad_qkv = jnp.zeros((width, 3 * local_width), jnp.float32)
    grad_qvb = jnp.zeros((2, local_width), jnp.float32)
    grad_wout = jnp.zeros((local_width, width), jnp.float32)
    grad_wup = jnp.zeros((width, hidden_local), jnp.float32)
    grad_bup = jnp.zeros((hidden_local,), jnp.float32)
    grad_wdown = jnp.zeros((hidden_local, width), jnp.float32)
    grad_gain_one = jnp.zeros((width,), jnp.float32)
    grad_shift_one = jnp.zeros((width,), jnp.float32)
    grad_gain_two = jnp.zeros((width,), jnp.float32)
    grad_shift_two = jnp.zeros((width,), jnp.float32)
    grad_out_shift = jnp.zeros((width,), jnp.float32)
    grad_down_shift = jnp.zeros((width,), jnp.float32)
    output_rows = []
    input_rows = []
    for index in range(batches):
        tokens_f = tokens[index].astype(jnp.float32)
        length = lengths[index]
        normal_one, inverse_one = norm_parts(tokens_f)
        normed_one = (normal_one * gain_one + shift_one).astype(jnp.bfloat16)
        projected = (matmul(normed_one, weight_qkv) + qkv_shift).astype(jnp.bfloat16)
        query = projected[:, :local_width].reshape(slots, heads_local, HEAD_DIM)
        keys = projected[:, local_width : 2 * local_width].reshape(slots, heads_local, HEAD_DIM)
        values = projected[:, 2 * local_width :].reshape(slots, heads_local, HEAD_DIM)
        attn = attention_forward(query, keys, values, length, slopes, scale)
        partial_value = matmul(attn, w_out)
        summed = lax.psum(partial_value.astype(jnp.bfloat16), "tensor").astype(jnp.float32)
        hidden_full = tokens_f + summed + out_shift
        normal_full, inverse_full = norm_parts(hidden_full)
        normed_two = (normal_full * gain_two + shift_two).astype(jnp.bfloat16)
        hidden_rows = lax.dynamic_slice_in_dim(hidden_full, row_start, share, 0)
        normal_two = lax.dynamic_slice_in_dim(normal_full, row_start, share, 0)
        inverse_two = lax.dynamic_slice_in_dim(inverse_full, row_start, share, 0)
        pre = matmul(normed_two, w_up) + up_shift
        act_value, act_slope = gelu_parts(pre)
        act = act_value.astype(jnp.bfloat16)
        mlp_part = lax.psum_scatter(
            matmul(act, w_down).astype(jnp.bfloat16), "tensor", scatter_dimension=0, tiled=True
        ).astype(jnp.float32)
        output_rows.append((hidden_rows + mlp_part + down_shift).astype(jnp.bfloat16))
        valid = (jnp.arange(slots, dtype=jnp.int32) < length).astype(jnp.float32)[:, None]
        grad_out = d_output[index].astype(jnp.float32) * valid
        grad_two = grad_out.astype(jnp.bfloat16)
        grad_wdown = grad_wdown + contract_rows(act, grad_two)
        grad_pre = (contract_cols(grad_two, w_down) * act_slope).astype(jnp.bfloat16)
        grad_wup = grad_wup + contract_rows(normed_two, grad_pre)
        grad_bup = grad_bup + jnp.sum(grad_pre.astype(jnp.float32), 0)
        grad_norm_two = lax.psum_scatter(
            contract_cols(grad_pre, w_up).astype(jnp.bfloat16),
            "tensor",
            scatter_dimension=0,
            tiled=True,
        ).astype(jnp.float32)
        grad_gain_two = grad_gain_two + jnp.sum(grad_norm_two * normal_two, 0)
        grad_shift_two = grad_shift_two + jnp.sum(grad_norm_two, 0)
        grad_out_rows = lax.dynamic_slice_in_dim(grad_out, row_start, share, 0)
        grad_hidden_rows = grad_out_rows + norm_backward(
            grad_norm_two, normal_two, inverse_two, gain_two
        )
        grad_one_rows = grad_hidden_rows.astype(jnp.bfloat16)
        grad_down_shift = grad_down_shift + jnp.sum(
            lax.dynamic_slice_in_dim(grad_two, row_start, share, 0).astype(jnp.float32), 0
        )
        grad_out_shift = grad_out_shift + jnp.sum(grad_one_rows.astype(jnp.float32), 0)
        grad_one = lax.all_gather(grad_one_rows, "tensor", axis=0, tiled=True)
        grad_wout = grad_wout + contract_rows(attn, grad_one)
        grad_attn = (
            contract_cols(grad_one, w_out)
            .astype(jnp.bfloat16)
            .reshape(slots, heads_local, HEAD_DIM)
        )
        grad_query, grad_keys, grad_values = attention_backward(
            query, keys, values, grad_attn, length, slopes, scale
        )
        grad_proj = jnp.concatenate([grad_query, grad_keys, grad_values], 1)
        grad_qkv = grad_qkv + contract_rows(normed_one, grad_proj)
        grad_qvb = grad_qvb + jnp.stack(
            [
                jnp.sum(grad_query.astype(jnp.float32), 0),
                jnp.sum(grad_values.astype(jnp.float32), 0),
            ],
            0,
        )
        grad_norm_one = lax.psum_scatter(
            contract_cols(grad_proj, weight_qkv).astype(jnp.bfloat16),
            "tensor",
            scatter_dimension=0,
            tiled=True,
        ).astype(jnp.float32)
        normal_one_rows = lax.dynamic_slice_in_dim(normal_one, row_start, share, 0)
        inverse_one_rows = lax.dynamic_slice_in_dim(inverse_one, row_start, share, 0)
        grad_gain_one = grad_gain_one + jnp.sum(grad_norm_one * normal_one_rows, 0)
        grad_shift_one = grad_shift_one + jnp.sum(grad_norm_one, 0)
        input_rows.append(
            (
                grad_hidden_rows
                + norm_backward(grad_norm_one, normal_one_rows, inverse_one_rows, gain_one)
            ).astype(jnp.bfloat16)
        )
    grad_qkv, grad_qvb, grad_wout, grad_wup, grad_bup, grad_wdown = (
        lax.psum(grad_qkv.astype(jnp.bfloat16), "dp").astype(jnp.float32),
        lax.psum(grad_qvb.astype(jnp.bfloat16), "dp").astype(jnp.float32),
        lax.psum(grad_wout.astype(jnp.bfloat16), "dp").astype(jnp.float32),
        lax.psum(grad_wup.astype(jnp.bfloat16), "dp").astype(jnp.float32),
        lax.psum(grad_bup.astype(jnp.bfloat16), "dp").astype(jnp.float32),
        lax.psum(grad_wdown.astype(jnp.bfloat16), "dp").astype(jnp.float32),
    )
    (
        grad_gain_one,
        grad_shift_one,
        grad_gain_two,
        grad_shift_two,
        grad_out_shift,
        grad_down_shift,
    ) = lax.psum(
        (
            grad_gain_one,
            grad_shift_one,
            grad_gain_two,
            grad_shift_two,
            grad_out_shift,
            grad_down_shift,
        ),
        ("dp", "tensor"),
    )
    return (
        jnp.stack(output_rows, 0),
        jnp.stack(input_rows, 0),
        grad_gain_one,
        grad_shift_one,
        grad_qkv.reshape(width, 3, local_width),
        grad_qvb,
        grad_wout,
        grad_out_shift,
        grad_gain_two,
        grad_shift_two,
        grad_wup,
        grad_bup,
        grad_wdown,
        grad_down_shift,
    )


def solution(mesh):
    whole = mesh.shape["tensor"] == 2 and mesh.shape["dp"] == 2 * len(RING)
    return jax.shard_map(
        whole_sequence if whole else on_device,
        mesh=mesh,
        in_specs=(
            P("dp", None, None),
            P("dp", None, None),
            P("dp"),
            P(),
            P(),
            P(None, None, "tensor"),
            P(None, "tensor"),
            P("tensor", None),
            P(),
            P(),
            P(),
            P(None, "tensor"),
            P("tensor"),
            P("tensor", None),
            P(),
        ),
        out_specs=(
            P("dp", "tensor", None),
            P("dp", "tensor", None),
            P(),
            P(),
            P(None, None, "tensor"),
            P(None, "tensor"),
            P("tensor", None),
            P(),
            P(),
            P(),
            P(None, "tensor"),
            P("tensor"),
            P("tensor", None),
            P(),
        ),
        check_vma=False,
    )
```

```python
import functools
import math

import jax
import jax.numpy as jnp
import numpy as np
from jax import lax
from jax.experimental import pallas as pl
from jax.experimental.pallas import tpu as pltpu
from jax.sharding import PartitionSpec as P

HEADS = 16
HEAD_DIM = 64


epsilon = 1e-05
root_two_pi = math.sqrt(2.0 / math.pi)
masked_score = -1e30


def matmul(left, right):
    return jnp.dot(left, right, preferred_element_type=jnp.float32)


def contract_rows(left, right):
    return lax.dot_general(
        left, right, (((0,), (0,)), ((), ())), preferred_element_type=jnp.float32
    )


def contract_cols(left, right):
    return lax.dot_general(
        left, right, (((1,), (1,)), ((), ())), preferred_element_type=jnp.float32
    )


def norm_parts(values):
    centre = jnp.mean(values, -1, keepdims=True)
    shifted = values - centre
    inverse = lax.rsqrt(jnp.mean(shifted * shifted, -1, keepdims=True) + epsilon)
    return (shifted * inverse, inverse)


def norm_backward(grad_normed, normal, inverse, gain):
    scaled = grad_normed * gain
    return inverse * (
        scaled
        - jnp.mean(scaled, -1, keepdims=True)
        - normal * jnp.mean(scaled * normal, -1, keepdims=True)
    )


def gelu_parts(pre):
    tangent = jnp.tanh(root_two_pi * (pre + 0.044715 * pre * pre * pre))
    value = 0.5 * pre * (1.0 + tangent)
    slope = 0.5 * (1.0 + tangent) + 0.5 * pre * (1.0 - tangent * tangent) * root_two_pi * (
        1.0 + 3.0 * 0.044715 * pre * pre
    )
    return (value, slope)


def block_probs(query_rows, key_rows, start, length, slopes, scale):
    rows = query_rows.shape[0]
    cols = key_rows.shape[0]
    products = jnp.einsum("ihd,jhd->hij", query_rows, key_rows, preferred_element_type=jnp.float32)
    key_place = jnp.arange(cols, dtype=jnp.int32)
    distance = (start + jnp.arange(rows, dtype=jnp.int32))[:, None] - key_place[None, :]
    scores = products * scale - slopes[:, None, None] * distance.astype(jnp.float32)[None]
    allowed = (distance >= 0) & (key_place[None, :] < length)
    masked = jnp.where(allowed[None], scores, masked_score)
    highest = jnp.max(masked, -1, keepdims=True)
    exponent = jnp.exp(masked - highest)
    return exponent / jnp.sum(exponent, -1, keepdims=True)


def attention_forward(query, keys, values, length, slopes, scale):
    slots = query.shape[0]
    block = min(512, slots)
    outputs = []
    for number in range(slots // block):
        start = number * block
        probs = block_probs(query[start : start + block], keys, start, length, slopes, scale)
        mixed = jnp.einsum(
            "hij,jhd->ihd", probs.astype(jnp.bfloat16), values, preferred_element_type=jnp.float32
        )
        outputs.append(mixed.reshape(block, -1).astype(jnp.bfloat16))
    return jnp.concatenate(outputs, 0)


def attention_backward(query, keys, values, grad_attn, length, slopes, scale):
    slots, heads_local, head_width = query.shape
    block = min(512, slots)
    grad_keys = jnp.zeros((slots, heads_local, head_width), jnp.float32)
    grad_values = jnp.zeros((slots, heads_local, head_width), jnp.float32)
    query_parts = []
    for number in range(slots // block):
        start = number * block
        query_rows = query[start : start + block]
        grad_rows = grad_attn[start : start + block]
        probs = block_probs(query_rows, keys, start, length, slopes, scale)
        grad_probs = jnp.einsum(
            "ihd,jhd->hij", grad_rows, values, preferred_element_type=jnp.float32
        )
        delta = jnp.sum(probs * grad_probs, -1, keepdims=True)
        grad_scores = (probs * (grad_probs - delta)).astype(jnp.bfloat16)
        part_query = (
            jnp.einsum("hij,jhd->ihd", grad_scores, keys, preferred_element_type=jnp.float32)
            * scale
        )
        part_keys = (
            jnp.einsum("hij,ihd->jhd", grad_scores, query_rows, preferred_element_type=jnp.float32)
            * scale
        )
        part_values = jnp.einsum(
            "hij,ihd->jhd",
            probs.astype(jnp.bfloat16),
            grad_rows,
            preferred_element_type=jnp.float32,
        )
        part_query, part_keys, part_values = (part_query, part_keys, part_values)
        query_parts.append(part_query)
        grad_keys = grad_keys.at[:slots].add(part_keys)
        grad_values = grad_values.at[:slots].add(part_values)
    grad_query = jnp.concatenate(query_parts, 0).reshape(slots, -1).astype(jnp.bfloat16)
    return (
        grad_query,
        grad_keys.reshape(slots, -1).astype(jnp.bfloat16),
        grad_values.reshape(slots, -1).astype(jnp.bfloat16),
    )


QUERY_BLOCK = 256
KEY_BLOCK = 1024
PAIR = 128
NT = (((1,), (1,)), ((), ()))
TN = (((0,), (0,)), ((), ()))


def mm(left, right, dims=(((1,), (0,)), ((), ()))):
    return lax.dot_general(left, right, dims, preferred_element_type=jnp.float32)


def low_lanes(rows):
    return lax.broadcasted_iota(jnp.int32, (rows, PAIR), 1) < HEAD_DIM


def slope_rows():
    table = np.zeros((HEADS // 2, 8, PAIR), np.float64)
    for head in range(HEADS):
        rest = np.float64(np.float32(2.0 ** (-8.0 * (head + 1) / HEADS)))
        base = HEAD_DIM * (1 - head % 2)
        for part in range(3):
            piece = np.float64(np.asarray(rest).astype(jnp.bfloat16))
            rest = rest - piece
            table[head // 2, head % 2, base + part] = 32.0 * piece
            table[head // 2, head % 2, base + 3 + part] = piece
        table[head // 2, head % 2, base + 6] = 1.0
    return table.astype(jnp.bfloat16)


def key_lanes(slots, length):
    place = jnp.arange(slots, dtype=jnp.int32)[:, None]
    lane = jnp.arange(PAIR, dtype=jnp.int32)[None, :] % HEAD_DIM
    high = (place // 32).astype(jnp.float32)
    low = (place % 32).astype(jnp.float32)
    mask = jnp.where(place < length, 0.0, masked_score)
    return jnp.where(
        lane < 3, high, jnp.where(lane < 6, low, jnp.where(lane == 6, mask, 0.0))
    ).astype(jnp.bfloat16)


def forward_kernel(
    q_ref, k_ref, v_ref, lanes_ref, rows_ref, o_ref, level_ref, key0, key1, val0, val1
):
    slots = q_ref.shape[0]
    block = QUERY_BLOCK
    low = low_lanes(slots)
    zero = jnp.zeros((slots, PAIR), jnp.bfloat16)
    one = jnp.ones((slots, PAIR), jnp.bfloat16)
    key0[...] = jnp.where(low, k_ref[...], lanes_ref[...])
    key1[...] = jnp.where(low, lanes_ref[...], k_ref[...])
    val0[:, :PAIR] = jnp.where(low, v_ref[...], zero)
    val0[:, PAIR:] = jnp.where(low, one, zero)
    val1[:, :PAIR] = jnp.where(low, zero, v_ref[...])
    val1[:, PAIR:] = jnp.where(low, zero, one)
    low_block = low_lanes(block)
    causal = lax.broadcasted_iota(jnp.int32, (block, block), 1) <= lax.broadcasted_iota(
        jnp.int32, (block, block), 0
    )
    for number in range(slots // block):
        start = number * block
        rows = q_ref[start : start + block, :] * jnp.bfloat16(0.125)
        total = None
        tops = []
        for head, (key, val) in enumerate(((key0, val0), (key1, val1))):
            extra = jnp.broadcast_to(rows_ref[0, head : head + 1, :], (block, PAIR))
            query = jnp.where(low_block, rows, extra) if head == 0 else jnp.where(
                low_block, extra, rows
            )
            own = jnp.where(causal, mm(query, key[start : start + block, :], NT), masked_score)
            highest = jnp.max(own, 1, keepdims=True)
            if start:
                past = mm(query, key[:start, :], NT)
                highest = jnp.maximum(highest, jnp.max(past, 1, keepdims=True))
                part = mm(jnp.exp(past - highest).astype(jnp.bfloat16), val[:start, :])
                total = part if total is None else total + part
            part = mm(jnp.exp(own - highest).astype(jnp.bfloat16), val[start : start + block, :])
            total = part if total is None else total + part
            tops.append(highest)
        o_ref[start : start + block, :] = (total[:, :PAIR] / total[:, PAIR:]).astype(jnp.bfloat16)
        level = (jnp.where(low_block, tops[0], tops[1]) + jnp.log(total[:, PAIR:])).T
        level_ref[0, 0:1, start : start + block] = level[0:1, :]
        level_ref[0, 1:2, start : start + block] = level[HEAD_DIM : HEAD_DIM + 1, :]


def fill_pair(k_ref, v_ref, lanes_ref, key0, key1, val0, val1, bare0, bare1):
    slots = k_ref.shape[0]
    low = low_lanes(slots)
    zero = jnp.zeros((slots, PAIR), jnp.bfloat16)
    key0[...] = jnp.where(low, k_ref[...], lanes_ref[...])
    key1[...] = jnp.where(low, lanes_ref[...], k_ref[...])
    bare0[...] = jnp.where(low, k_ref[...], zero)
    bare1[...] = jnp.where(low, zero, k_ref[...])
    val0[...] = jnp.where(low, v_ref[...], zero)
    val1[...] = jnp.where(low, zero, v_ref[...])


def pair_grads(
    query, mixed, gradient, level_ref, rows_ref, total_q,
    key0, key1, val0, val1, bare0, bare1, total_k, total_v, between,
):
    slots = query.shape[0]
    block = QUERY_BLOCK
    piece = KEY_BLOCK
    low_block = low_lanes(block)
    nil = jnp.zeros((block, PAIR), jnp.bfloat16)
    causal = lax.broadcasted_iota(jnp.int32, (block, block), 0) <= lax.broadcasted_iota(
        jnp.int32, (block, block), 1
    )
    for number in reversed(range(slots // block)):
        start = number * block
        stop = start + block
        rows = query[start:stop, :] * jnp.bfloat16(0.125)
        grad = gradient[start:stop, :]
        shares = (grad.astype(jnp.float32) * mixed[start:stop, :].astype(jnp.float32)).T
        deltas = [
            jnp.sum(shares[head * HEAD_DIM : (head + 1) * HEAD_DIM, :], 0, keepdims=True)
            for head in range(2)
        ]
        levels = [level_ref[0, head : head + 1, start:stop] for head in range(2)]
        extras = [jnp.broadcast_to(rows_ref[0, h : h + 1, :], (block, PAIR)) for h in range(2)]
        queries = (
            jnp.where(low_block, rows, extras[0]),
            jnp.where(low_block, extras[1], rows),
        )
        grads = jnp.concatenate(
            [jnp.where(low_block, grad, nil), jnp.where(low_block, nil, grad)], 0
        )
        both = jnp.concatenate(
            [jnp.where(low_block, rows, nil), jnp.where(low_block, nil, rows)], 0
        )
        grad_query = None
        for begin in range(0, stop, min(piece, stop)):
            end = min(begin + piece, stop)
            probs, scores = [], []
            for head, (key, val, bare) in enumerate(((key0, val0, bare0), (key1, val1, bare1))):
                score = mm(key[begin:end, :], queries[head], NT)
                if end > start:
                    own = jnp.where(causal, score[start - begin :], masked_score)
                    score = jnp.concatenate([score[: start - begin], own], 0) if start > begin else own
                prob = jnp.exp(score - levels[head])
                grad_prob = mm(val[begin:end, :], grad, NT)
                grad_score = (prob * (grad_prob - deltas[head])).astype(jnp.bfloat16)
                probs.append(prob.astype(jnp.bfloat16))
                scores.append(grad_score)
                part = mm(grad_score, bare[begin:end, :], TN)
                grad_query = part if grad_query is None else grad_query + part
                if stop == slots and head == 0:
                    between(1)
            part_v = mm(jnp.concatenate(probs, 1), grads)
            part_k = mm(jnp.concatenate(scores, 1), both)
            if stop == slots:
                total_v[begin:end, :] = part_v
                total_k[begin:end, :] = part_k
            else:
                total_v[begin:end, :] += part_v
                total_k[begin:end, :] += part_k
        total_q[start:stop, :] = (grad_query * 0.125).astype(jnp.bfloat16)
        if stop == slots:
            between(2)
        elif stop == slots - block:
            between(3)


def pair_specs(slots):
    part = pl.BlockSpec((slots, PAIR), lambda pair: (0, pair))
    lanes = pl.BlockSpec((slots, PAIR), lambda pair: (0, 0))
    rows = pl.BlockSpec((1, 8, PAIR), lambda pair: (pair, 0, 0))
    levels = pl.BlockSpec((1, 8, slots), lambda pair: (pair, 0, 0))
    return part, lanes, rows, levels


def attention_out(query, keys, values, lanes, rows):
    slots, columns = query.shape
    part, lane_spec, row_spec, level_spec = pair_specs(slots)
    pairs = columns // PAIR
    half = slots * slots * PAIR * pairs
    return pl.pallas_call(
        forward_kernel,
        grid=(pairs,),
        out_shape=(
            jax.ShapeDtypeStruct((slots, columns), jnp.bfloat16),
            jax.ShapeDtypeStruct((pairs, 8, slots), jnp.float32),
        ),
        in_specs=[part, part, part, lane_spec, row_spec],
        out_specs=(part, level_spec),
        scratch_shapes=[pltpu.VMEM((slots, PAIR), jnp.bfloat16)] * 2
        + [pltpu.VMEM((slots, 2 * PAIR), jnp.bfloat16)] * 2,
        cost_estimate=pl.CostEstimate(
            flops=8 * half, bytes_accessed=8 * slots * columns, transcendentals=slots * slots * pairs
        ),
        name="attention_out",
    )(query, keys, values, lanes, rows)


ROW_BLOCK = 256


def whole_spec(array):
    zeros = (0,) * array.ndim
    return pl.BlockSpec(array.shape, lambda *_: zeros)


def row_spec(columns):
    return pl.BlockSpec((ROW_BLOCK, columns), lambda row, *_: (row, 0))


def own_spec(columns):
    return pl.BlockSpec((1, ROW_BLOCK, columns), lambda row, facts: (facts[0], row, 0))


def over_rows(kernel, name, slots, facts, inputs, outputs, flops):
    arrays, in_specs = zip(*inputs)
    shapes, out_specs = zip(*outputs)
    return pl.pallas_call(
        kernel,
        grid_spec=pltpu.PrefetchScalarGridSpec(
            num_scalar_prefetch=1,
            grid=(slots // ROW_BLOCK,),
            in_specs=list(in_specs),
            out_specs=list(out_specs),
        ),
        out_shape=list(shapes),
        cost_estimate=pl.CostEstimate(
            flops=flops,
            bytes_accessed=sum(array.size * array.dtype.itemsize for array in arrays),
            transcendentals=0,
        ),
        name=name,
    )(facts, *arrays)


def project_kernel(facts, tok_ref, gain_ref, shift_ref, w_ref, bias_ref, *refs):
    norm_ref, q_ref, k_ref, v_ref = refs[-4:]
    normal, _ = norm_parts(tok_ref[0].astype(jnp.float32))
    normed = (normal * gain_ref[...] + shift_ref[...]).astype(jnp.bfloat16)
    norm_ref[...] = normed
    q_ref[...] = (mm(normed, w_ref[0]) + bias_ref[0:1, :]).astype(jnp.bfloat16)
    k_ref[...] = mm(normed, w_ref[1]).astype(jnp.bfloat16)
    v_ref[...] = (mm(normed, w_ref[2]) + bias_ref[1:2, :]).astype(jnp.bfloat16)


def hidden_kernel(
    facts, tok_ref, a0_ref, a1_ref, w0_ref, w1_ref, bias_ref, gain_ref, shift_ref, hid_ref, norm_ref
):
    hidden = tok_ref[0].astype(jnp.float32) + bias_ref[...]
    hidden = hidden + mm(a0_ref[...], w0_ref[...]) + mm(a1_ref[...], w1_ref[...])
    hid_ref[...] = hidden
    normal, _ = norm_parts(hidden)
    norm_ref[...] = (normal * gain_ref[...] + shift_ref[...]).astype(jnp.bfloat16)


def act_kernel(norm_ref, w_ref, bias_ref, act_ref, slope_ref):
    def rows(number, carry):
        at = pl.ds(pl.multiple_of(number * ROW_BLOCK, ROW_BLOCK), ROW_BLOCK)
        value, slope = gelu_parts(mm(norm_ref[at, :], w_ref[...]) + bias_ref[...])
        act_ref[at, :] = value.astype(jnp.bfloat16)
        slope_ref[at, :] = slope.astype(jnp.bfloat16)
        return carry

    lax.fori_loop(0, norm_ref.shape[0] // ROW_BLOCK, rows, 0, unroll=True)


def activations(normed, weight, bias):
    slots, width = normed.shape
    hidden = weight.shape[1]
    columns = 512
    out = pl.BlockSpec((slots, columns), lambda col: (0, col))
    shape = jax.ShapeDtypeStruct((slots, hidden), jnp.bfloat16)
    return pl.pallas_call(
        act_kernel,
        grid=(hidden // columns,),
        in_specs=[
            whole_spec(normed),
            pl.BlockSpec((width, columns), lambda col: (0, col)),
            pl.BlockSpec((1, columns), lambda col: (0, col)),
        ],
        out_specs=(out, out),
        out_shape=(shape, shape),
        cost_estimate=pl.CostEstimate(
            flops=2 * slots * width * hidden,
            bytes_accessed=8 * slots * hidden,
            transcendentals=slots * hidden,
        ),
        name="activations",
    )(normed, weight, bias)


def output_kernel(facts, hid_ref, a0_ref, a1_ref, w0_ref, w1_ref, bias_ref, tie_ref, out_ref):
    total = hid_ref[...] + bias_ref[...] + mm(a0_ref[...], w0_ref[...])
    out_ref[...] = (total + mm(a1_ref[...], w1_ref[...])).astype(jnp.bfloat16)


def add_sums(sums_ref, rows):
    @pl.when(pl.program_id(0) == 0)
    def _():
        sums_ref[...] = jnp.zeros_like(sums_ref)

    for index, value in enumerate(rows):
        sums_ref[index : index + 1, :] += jnp.sum(value, 0, keepdims=True)


def hidden_grad_kernel(
    facts, g0_ref, g1_ref, w0_ref, w1_ref, hid_ref, gain_ref, dout_ref, grad_ref, one_ref, sums_ref
):
    grad_norm = mm(g0_ref[...], w0_ref[...], NT) + mm(g1_ref[...], w1_ref[...], NT)
    normal, inverse = norm_parts(hid_ref[...])
    place = lax.broadcasted_iota(jnp.int32, grad_norm.shape, 0) + pl.program_id(0) * ROW_BLOCK
    grad_out = jnp.where(place < facts[1], dout_ref[0].astype(jnp.float32), 0.0)
    grad = grad_out + norm_backward(grad_norm, normal, inverse, gain_ref[...])
    one = grad.astype(jnp.bfloat16)
    grad_ref[...] = grad
    one_ref[...] = one
    add_sums(sums_ref, [grad_norm * normal, grad_norm, one.astype(jnp.float32), grad_out])


def token_grad_kernel(
    facts, q0_ref, k0_ref, v0_ref, q1_ref, k1_ref, v1_ref, w0_ref, w1_ref, tok_ref, grad_ref,
    gain_ref, *refs,
):
    out_ref, sums_ref, heads_ref = refs[-3:]
    grad_norm = None
    for refs, weight in (((q0_ref, k0_ref, v0_ref), w0_ref), ((q1_ref, k1_ref, v1_ref), w1_ref)):
        for part, ref in enumerate(refs):
            more = mm(ref[...], weight[part], NT)
            grad_norm = more if grad_norm is None else grad_norm + more
    normal, inverse = norm_parts(tok_ref[0].astype(jnp.float32))
    grad = grad_ref[...] + norm_backward(grad_norm, normal, inverse, gain_ref[...])
    out_ref[...] = grad.astype(jnp.bfloat16)
    add_sums(sums_ref, [grad_norm * normal, grad_norm])
    add_sums(heads_ref, [ref[...].astype(jnp.float32) for ref in (q0_ref, q1_ref, v0_ref, v1_ref)])


RING = ((0, 0), (1, 0), (2, 0), (3, 0), (3, 1), (2, 1), (1, 1), (0, 1))
RING_CUTS = 2


def device_of(z, y, core):
    return (z * 2 + y) * 2 + core


def to_tensor(value):
    return lax.ppermute(value, "tensor", [(0, 1), (1, 0)])


def to_core(value):
    return lax.ppermute(value, "dp", [(i, i ^ 1) for i in range(2 * len(RING))])


def rows_at(value, start, size):
    return lax.dynamic_slice_in_dim(value, start, size, value.ndim - 2)


def after(value, *earlier):
    return lax.optimization_barrier((value, *earlier))[0]


def piece(weight, index, pieces):
    size = weight.shape[-2] // pieces
    return rows_at(weight, index * size, size)


def both_cores(value, core, axis):
    beside = to_core(value)
    first = jnp.where(core == 0, value, beside)
    second = jnp.where(core == 0, beside, value)
    return jnp.concatenate([first, second], axis)


class Ring:
    def __init__(self, values, slots, sums, results, sems, cuts):
        self.values, self.slots, self.sums, self.results = values, slots, sums, results
        self.send_sems, self.recv_sems, self.swap_send_sems, self.swap_recv_sems = sems
        self.cuts = cuts
        self.count = count = len(RING)
        self.device = device = lax.axis_index("dp")
        self.core, self.y, self.z = lax.rem(device, 2), lax.rem(device // 2, 2), device // 4
        self.place = place = self.z * (1 - self.y) + (count - 1 - self.z) * self.y
        self.nexts = tuple(
            self.at_place(lax.rem(place + step, count)) for step in (1, count - 1)
        )
        self.partner = {"dp": device + 1 - 2 * self.core}
        self.streams = [
            (array, way, cut)
            for cut in range(cuts)
            for array in range(len(values))
            for way in range(2)
        ]

    def at_place(self, where):
        side = where // 4
        return {
            "dp": device_of(where * (1 - side) + (self.count - 1 - where) * side, side, self.core)
        }

    def greet(self, others=()):
        barrier = pltpu.get_barrier_semaphore()
        greeted = [*self.nexts, self.partner, *others]
        for target in greeted:
            pl.semaphore_signal(
                barrier, inc=1, device_id=target, device_id_type=pl.DeviceIdType.MESH
            )
        pl.semaphore_wait(barrier, len(greeted))

    def block(self, way, offset):
        return lax.rem(self.place - (1, -1)[way] * offset + 2 * self.count, self.count)

    def rows(self, array, cut):
        size = self.values[array].shape[2] // self.cuts
        return pl.ds(cut * size, size)

    def result(self, stream, step):
        array, way, cut = stream
        return self.results[array].at[
            self.core, way, self.block(way, step), self.rows(array, cut)
        ]

    def copy(self, stream, step):
        array, way, cut = stream
        rows = self.rows(array, cut)
        if step < self.count - 1:
            target = self.slots[array].at[way, step, rows]
            if step:
                source = self.sums[array].at[way, step - 1, rows]
            else:
                source = self.values[array].at[way, self.block(way, 0), rows]
        else:
            source = target = self.result(stream, step)
        index = self.streams.index(stream)
        return pltpu.make_async_remote_copy(
            src_ref=source,
            dst_ref=target,
            send_sem=self.send_sems.at[index, step],
            recv_sem=self.recv_sems.at[index, step],
            device_id=self.nexts[way],
            device_id_type=pl.DeviceIdType.MESH,
        )

    def swap(self, stream, step):
        index = self.streams.index(stream)
        turn = step - self.count + 1
        done = self.result(stream, step)
        return pltpu.make_async_remote_copy(
            src_ref=done,
            dst_ref=done,
            send_sem=self.swap_send_sems.at[index, turn],
            recv_sem=self.swap_recv_sems.at[index, turn],
            device_id=self.partner,
            device_id_type=pl.DeviceIdType.MESH,
        )

    def chosen(self, only):
        return [stream for stream in self.streams if only is None or stream[2] == only]

    def first(self, only=None):
        for stream in self.chosen(only):
            self.copy(stream, 0).start()

    def hop(self, step, only=None):
        count = self.count
        for stream in self.chosen(only):
            array, way, cut = stream
            rows = self.rows(array, cut)
            self.copy(stream, step - 1).wait_recv()
            if step < count:
                total = self.values[array][way, self.block(way, step), rows].astype(jnp.float32)
                total = total + self.slots[array][way, step - 1, rows].astype(jnp.float32)
                total = total.astype(jnp.bfloat16)
                if step < count - 1:
                    self.sums[array][way, step - 1, rows] = total
                else:
                    self.results[array][self.core, way, self.block(way, step), rows] = total
            self.copy(stream, step).start()
            if step >= count - 1:
                self.swap(stream, step).start()

    def last(self, only=None):
        for stream in self.chosen(only):
            self.copy(stream, 2 * self.count - 3).wait_recv()
            self.swap(stream, 2 * self.count - 2).start()

    def drain(self):
        for stream in self.streams:
            for step in range(2 * self.count - 2):
                self.copy(stream, step).wait_send()
            for step in range(self.count - 1, 2 * self.count - 1):
                self.swap(stream, step).wait()


def ring_shape(value):
    count = len(RING)
    return value.reshape(2, count, value.shape[0] // (2 * count), value.shape[1])


def ring_scratch(shaped, cuts):
    count = len(RING)
    streams = 2 * len(shaped) * cuts
    scratch = [pltpu.VMEM((2, count - 1, *value.shape[2:]), value.dtype) for value in shaped]
    scratch += [pltpu.VMEM((2, count - 2, *value.shape[2:]), value.dtype) for value in shaped]
    scratch += [pltpu.SemaphoreType.DMA((streams, 2 * count - 2))] * 2
    return scratch + [pltpu.SemaphoreType.DMA((streams, count))] * 2


def ring_kernel(blocks, cuts, has_small, has_tie, *refs):
    values, refs = refs[:blocks], refs[blocks:]
    if has_small:
        small_ref, refs = refs[0], refs[1:]
    refs = refs[has_tie:]
    results, refs = refs[:blocks], refs[blocks:]
    if has_small:
        small_out, refs = refs[0], refs[1:]
    slots, refs = refs[:blocks], refs[blocks:]
    sums, refs = refs[:blocks], refs[blocks:]
    ring = Ring(values, slots, sums, results, refs[:4], cuts)
    if has_small:
        small_slots, small_sums, small_send_sems, small_recv_sems = refs[4:]
        device, y, z = ring.device, ring.y, ring.z
        small_targets = [
            ring.partner,
            {"tensor": 1 - lax.axis_index("tensor")},
            {"dp": device + 2 - 4 * y},
            {"dp": device + 4 - 8 * lax.rem(z, 2)},
            {"dp": device + 8 - 16 * (z // 2)},
        ]
        ring.greet(small_targets[1:])
    else:
        ring.greet()

    def exchange(turn):
        return pltpu.make_async_remote_copy(
            src_ref=small_ref if turn == 0 else small_sums.at[turn - 1],
            dst_ref=small_slots.at[turn],
            send_sem=small_send_sems.at[turn],
            recv_sem=small_recv_sems.at[turn],
            device_id=small_targets[turn],
            device_id_type=pl.DeviceIdType.MESH,
        )

    def take_exchange(turn):
        exchange(turn).wait_recv()
        total = (small_ref[...] if turn == 0 else small_sums[turn - 1]) + small_slots[turn]
        if turn == len(small_targets) - 1:
            small_out[...] = total
        else:
            small_sums[turn] = total
            exchange(turn + 1).start()

    ring.first()
    if has_small:
        exchange(0).start()
    for step in range(1, 2 * ring.count - 2):
        if has_small and step % 2 == 0 and step // 2 <= len(small_targets):
            take_exchange(step // 2 - 1)
        ring.hop(step)
    ring.last()
    ring.drain()
    if has_small:
        for turn in range(len(small_targets)):
            exchange(turn).wait_send()


def plane_sums(values, identity, small=None, tie=None, cuts=1):
    blocks = len(values)
    shaped = [ring_shape(value) for value in values]
    size = sum(value.size for value in values)
    vmem = pl.BlockSpec(memory_space=pltpu.VMEM)
    inputs, in_specs = list(shaped), [vmem] * blocks
    shapes = [jax.ShapeDtypeStruct((2, *value.shape), value.dtype) for value in shaped]
    scratch = ring_scratch(shaped, cuts)
    if small is not None:
        inputs.append(small)
        in_specs.append(vmem)
        shapes.append(jax.ShapeDtypeStruct(small.shape, small.dtype))
        scratch += [pltpu.VMEM((5, *small.shape), small.dtype)] * 2
        scratch += [pltpu.SemaphoreType.DMA((5,))] * 2
    if tie is not None:
        inputs.append(tie)
        in_specs.append(pl.BlockSpec(memory_space=pl.ANY))
    results = pl.pallas_call(
        functools.partial(ring_kernel, blocks, cuts, small is not None, int(tie is not None)),
        out_shape=shapes,
        in_specs=in_specs,
        out_specs=[vmem] * len(shapes),
        scratch_shapes=scratch,
        compiler_params=pltpu.CompilerParams(collective_id=identity, has_side_effects=True),
        cost_estimate=pl.CostEstimate(flops=size, bytes_accessed=6 * size, transcendentals=0),
        name="plane_sums",
    )(*inputs)
    sums = [
        result.reshape(2 * value.shape[0], value.shape[1]) for result, value in zip(results, values)
    ]
    return sums if small is None else (sums, results[-1])


def grads_ring_kernel(
    q0_ref, k0_ref, v0_ref, o0_ref, g0_ref, q1_ref, k1_ref, v1_ref, o1_ref, g1_ref,
    level_ref, lanes_ref, rows_ref, value_ref,
    dq0_ref, dk0_ref, dv0_ref, dq1_ref, dk1_ref, dv1_ref, sum_ref,
    query, mixed, grad, key0, key1, val0, val1, bare0, bare1, total_q, total_k, total_v,
    result, slots, sums, send_sems, recv_sems, swap_send_sems, swap_recv_sems, out_sem,
):
    pair = pl.program_id(0)
    pairs = HEADS // 2
    ring = Ring(
        [value_ref], [slots], [sums], [result],
        (send_sems, recv_sems, swap_send_sems, swap_recv_sems), RING_CUTS,
    )

    def turn(number, cut):
        if number == 0:
            if cut == 0:
                ring.greet()
            ring.first(cut)
        elif number < 2 * ring.count - 2:
            ring.hop(number, cut)
        elif number == 2 * ring.count - 2:
            ring.last(cut)
        elif cut == RING_CUTS - 1:
            ring.drain()
            out = pltpu.make_async_copy(result, sum_ref, out_sem)
            out.start()
            out.wait()

    def turns(place):
        second, cut = divmod(place, RING_CUTS)
        for number in range(pairs):
            pl.when(pair == number)(functools.partial(turn, 2 * number + second, cut))

    def take(q_ref, k_ref, v_ref, o_ref, g_ref):
        query[...] = q_ref[...]
        mixed[...] = o_ref[...]
        grad[...] = g_ref[...]
        fill_pair(k_ref, v_ref, lanes_ref, key0, key1, val0, val1, bare0, bare1)

    def give(dq_ref, dk_ref, dv_ref):
        dq_ref[...] = total_q[...]
        dk_ref[...] = total_k[...].astype(jnp.bfloat16)
        dv_ref[...] = total_v[...].astype(jnp.bfloat16)

    turns(0)
    pl.when(pair < pairs // 2)(lambda: take(q0_ref, k0_ref, v0_ref, o0_ref, g0_ref))
    pl.when(pair >= pairs // 2)(lambda: take(q1_ref, k1_ref, v1_ref, o1_ref, g1_ref))
    pair_grads(
        query, mixed, grad, level_ref, rows_ref, total_q,
        key0, key1, val0, val1, bare0, bare1, total_k, total_v, turns,
    )
    pl.when(pair < pairs // 2)(lambda: give(dq0_ref, dk0_ref, dv0_ref))
    pl.when(pair >= pairs // 2)(lambda: give(dq1_ref, dk1_ref, dv1_ref))


def attention_grads_ring(first, second, levels, lanes, rows, value):
    slots, columns = first[0].shape
    half = columns // PAIR
    shaped = ring_shape(value)
    whole = jax.ShapeDtypeStruct((2, *shaped.shape), value.dtype)

    part0 = pl.BlockSpec((slots, PAIR), lambda pair: (0, pair - (pair // half) * (pair - half + 1)))
    part1 = pl.BlockSpec((slots, PAIR), lambda pair: (0, (pair // half) * (pair - half)))
    shape = jax.ShapeDtypeStruct((slots, columns), jnp.bfloat16)
    work = slots * slots * PAIR * 2 * half
    *grads, total = pl.pallas_call(
        grads_ring_kernel,
        grid=(2 * half,),
        out_shape=[shape] * 6 + [whole],
        in_specs=[part0] * 5
        + [part1] * 5
        + [
            pl.BlockSpec((1, 8, slots), lambda pair: (pair, 0, 0)),
            pl.BlockSpec((slots, PAIR), lambda pair: (0, 0)),
            pl.BlockSpec((1, 8, PAIR), lambda pair: (pair, 0, 0)),
            pl.BlockSpec(shaped.shape, lambda pair: (0, 0, 0, 0)),
        ],
        out_specs=[part0] * 3 + [part1] * 3 + [pl.BlockSpec(memory_space=pl.ANY)],
        scratch_shapes=[pltpu.VMEM((slots, PAIR), jnp.bfloat16)] * 10
        + [pltpu.VMEM((slots, PAIR), jnp.float32)] * 2
        + [pltpu.VMEM(whole.shape, whole.dtype)]
        + ring_scratch([shaped], RING_CUTS)
        + [pltpu.SemaphoreType.DMA],
        compiler_params=pltpu.CompilerParams(collective_id=3, has_side_effects=True),
        cost_estimate=pl.CostEstimate(
            flops=20 * work,
            bytes_accessed=32 * slots * columns,
            transcendentals=2 * slots * slots * half,
        ),
        name="attention_grads_ring",
    )(*first, *second, levels, lanes, rows, shaped)
    return grads[:3], grads[3:], total.reshape(2 * value.shape[0], value.shape[1])


def core_send(left, rights, core):
    half = left.shape[1] // 2
    sent = lax.dynamic_slice_in_dim(left, (1 - core) * half, half, 1)
    return [to_core(contract_rows(sent, right).astype(jnp.bfloat16)) for right in rights]


def core_sum(left, rights, arrived, core):
    half = left.shape[1] // 2
    kept = lax.dynamic_slice_in_dim(left, core * half, half, 1)
    return [
        contract_rows(kept, right) + part.astype(jnp.float32)
        for right, part in zip(rights, arrived)
    ]


def start_grad(left, rights, core):
    other = core_send(left[1], rights[1], core)
    local = core_send(left[0], rights[0], core)
    summed = [
        part.astype(jnp.bfloat16) for part in core_sum(left[1], rights[1], other, core)
    ]
    return local, summed, [to_tensor(part) for part in summed]


def pair_grad(left, rights, local, passed, core):
    mine = [
        (part + more.astype(jnp.float32)).astype(jnp.bfloat16)
        for part, more in zip(core_sum(left, rights, local, core), passed)
    ]
    return mine


def trade_rows(value, own):
    share = value.shape[0] // 2
    arrived = to_tensor(lax.dynamic_slice_in_dim(value, (1 - own) * share, share, 0))
    kept = lax.dynamic_slice_in_dim(value, own * share, share, 0)
    return jnp.stack(
        [jnp.where(own == 0, kept, arrived), jnp.where(own == 0, arrived, kept)], 0
    )


def whole_sequence(
    tokens,
    d_output,
    lengths,
    ln1_gain,
    ln1_bias,
    w_qkv,
    qv_bias,
    w_out,
    bias_out,
    ln2_gain,
    ln2_bias,
    w_up,
    b_up,
    w_down,
    b_down,
):
    own = lax.axis_index("tensor")
    device = lax.axis_index("dp")
    core = device % 2
    slots, width = tokens.shape[1:]
    local_width = w_qkv.shape[2]
    hidden_local = w_up.shape[1]
    table = jnp.asarray(slope_rows())
    pairs = local_width // PAIR
    f32 = jnp.float32

    weight_qkv = w_qkv.transpose(1, 0, 2)
    biases = jnp.concatenate([qv_bias.reshape(-1), b_up])
    other_biases = to_tensor(biases)
    piece_up, piece_qkv = piece(w_up, device, 2 * len(RING)), piece(weight_qkv, core, 2)
    far_up, far_qkv = to_tensor(piece_up), to_tensor(piece_qkv)
    qv = [b[: 2 * local_width].reshape(2, local_width).astype(f32) for b in (biases, other_biases)]
    ups = [b[2 * local_width :].astype(f32)[None] for b in (biases, other_biases)]
    rows = [lax.dynamic_slice_in_dim(table, index * pairs, pairs, 0) for index in (own, 1 - own)]
    gain_one, shift_one = ln1_gain.astype(f32)[None], ln1_bias.astype(f32)[None]
    gain_two, shift_two = ln2_gain.astype(f32)[None], ln2_bias.astype(f32)[None]

    length = lax.dynamic_index_in_dim(lengths, own, 0, keepdims=False)
    facts = jnp.stack([own.astype(jnp.int32), length])
    lanes = key_lanes(slots, length)
    low = jnp.bfloat16

    def run(kernel, name, inputs, outputs, flops):
        return over_rows(kernel, name, slots, facts, inputs, outputs, flops)

    def fixed(array):
        return array, whole_spec(array)

    def tied(array):
        return array, pl.BlockSpec(memory_space=pl.ANY)

    def by_row(array):
        return array, row_spec(array.shape[1])

    def rows_out(columns, dtype):
        return jax.ShapeDtypeStruct((slots, columns), dtype), row_spec(columns)

    def sums_out(columns):
        shape = jax.ShapeDtypeStruct((8, columns), f32)
        return shape, whole_spec(shape)

    square = 2 * slots * width
    tokens_in, d_output_in = (tokens, own_spec(width)), (d_output, own_spec(width))
    normed_one, *local_heads = run(
        project_kernel,
        "project",
        [tokens_in, fixed(gain_one), fixed(shift_one), fixed(weight_qkv), fixed(qv[0])]
        + [tied(piece_up), tied(piece_qkv)],
        [rows_out(width, low)] + [rows_out(local_width, low)] * 3,
        3 * square * local_width,
    )
    attn, level = attention_out(*local_heads, lanes, rows[0])
    heads, mixed, levels = [tuple(local_heads)], [attn], [level]
    far_out = to_tensor(after(piece(w_out, core, 2), normed_one))
    far_down = to_tensor(after(piece(w_down, device, 2 * len(RING)), normed_one))
    up = (w_up, lax.all_gather(after(far_up, normed_one), "dp", axis=0, tiled=True))
    qkv = (weight_qkv, both_cores(far_qkv, core, 1))
    query = (matmul(normed_one, qkv[1][0]) + qv[1][0]).astype(low)
    keys = matmul(normed_one, qkv[1][1]).astype(low)
    values = (matmul(normed_one, qkv[1][2]) + qv[1][1]).astype(low)
    heads.append((query, keys, values))
    down = (w_down, lax.all_gather(after(far_down, keys), "dp", axis=0, tiled=True))
    attn, level = attention_out(query, keys, values, lanes, rows[1])
    mixed.append(attn)
    levels.append(level)
    out = (w_out, both_cores(far_out, core, 0))
    hidden, normed_two = run(
        hidden_kernel,
        "hidden_state",
        [tokens_in, by_row(mixed[0]), by_row(mixed[1]), fixed(out[0]), fixed(out[1])]
        + [fixed(bias_out.astype(f32)[None]), fixed(gain_two), fixed(shift_two)],
        [rows_out(width, f32), rows_out(width, low)],
        2 * square * local_width,
    )
    acts = [activations(normed_two, up[half], ups[half]) for half in range(2)]

    valid = (jnp.arange(slots, dtype=jnp.int32) < length).astype(f32)[:, None]
    grad_out = lax.dynamic_index_in_dim(d_output, own, 0, keepdims=False).astype(f32) * valid
    grad_two = grad_out.astype(low)
    left_down, right_down = (acts[0][0], acts[1][0]), ([grad_two], [grad_two])
    local_down, sent_down, passed_down = start_grad(left_down, right_down, core)
    late_two = after(grad_two, *sent_down, *local_down)
    grad_pre = [
        (contract_cols(late_two, down[half]) * acts[half][1].astype(f32)).astype(low)
        for half in range(2)
    ]
    left_up, right_up = (normed_two, normed_two), ([grad_pre[0]], [grad_pre[1]])
    local_up, sent_up, passed_up = start_grad(left_up, right_up, core)
    late_pre = lax.optimization_barrier((*grad_pre, *sent_up, *local_up))
    grad_hidden, grad_one, sums_two = run(
        hidden_grad_kernel,
        "hidden_grad",
        [by_row(late_pre[0]), by_row(late_pre[1]), fixed(up[0]), fixed(up[1]), by_row(hidden)]
        + [fixed(gain_two), d_output_in],
        [rows_out(width, f32), rows_out(width, low), sums_out(width)],
        2 * square * hidden_local,
    )
    (result,) = run(
        output_kernel,
        "layer_output",
        [by_row(hidden), by_row(acts[0][0]), by_row(acts[1][0]), fixed(down[0]), fixed(down[1])]
        + [fixed(b_down.astype(f32)[None]), tied(sent_up[0])],
        [rows_out(width, low)],
        2 * square * hidden_local,
    )
    output = trade_rows(result, own)
    left_out, right_out = (mixed[0], mixed[1]), ([grad_one], [grad_one])
    local_out, sent_out, passed_out = start_grad(left_out, right_out, core)
    late_one = after(grad_one, *sent_out, *local_out)
    grad_attn = [contract_cols(late_one, out[half]).astype(low) for half in range(2)]
    mine_down = pair_grad(left_down[0], right_down[0], local_down, passed_down, core)
    *grads, grad_wdown = attention_grads_ring(
        (*heads[0], mixed[0], grad_attn[0]),
        (*heads[1], mixed[1], grad_attn[1]),
        jnp.concatenate(levels, 0),
        lanes,
        jnp.concatenate(rows, 0),
        mine_down[0],
    )
    local_qkv, sent_qkv, passed_qkv = start_grad((normed_one, normed_one), grads, core)
    grad_tokens, sums_one, sums_heads = run(
        token_grad_kernel,
        "token_grad",
        [by_row(part) for part in (*grads[0], *grads[1])]
        + [fixed(qkv[0]), fixed(qkv[1]), tokens_in, by_row(grad_hidden), fixed(gain_one)]
        + [tied(part) for part in sent_qkv],
        [rows_out(width, low), sums_out(width), sums_out(local_width)],
        6 * square * local_width,
    )
    grad_tokens = trade_rows(grad_tokens, own)

    def in_place(first, second):
        return jnp.concatenate(
            [jnp.where(own == 0, first, second), jnp.where(own == 0, second, first)], 0
        )

    bias_up = [jnp.sum(grad_pre[half].astype(f32), 0) for half in range(2)]
    small = jnp.concatenate(
        [
            sums_one[:2],
            sums_two[:4],
            in_place(sums_heads[0], sums_heads[1]).reshape(1, width),
            in_place(sums_heads[2], sums_heads[3]).reshape(1, width),
            in_place(*bias_up).reshape(-1, width),
        ],
        0,
    )
    small = jnp.pad(small, ((0, 16 - small.shape[0]), (0, 0)))
    mine_up = pair_grad(left_up[0], right_up[0], local_up, passed_up, core)
    (grad_wup,) = plane_sums(mine_up, 1, tie=sent_qkv[0], cuts=RING_CUTS)
    mine_out = pair_grad(left_out[0], right_out[0], local_out, passed_out, core)
    mine_qkv = pair_grad(normed_one, grads[0], local_qkv, passed_qkv, core)
    (grad_wout, *grad_wqkv), small = plane_sums(mine_out + mine_qkv, 2, small, grad_wup)
    grad_wqkv = jnp.stack(grad_wqkv, 0).astype(f32)
    wide = [lax.dynamic_slice_in_dim(small[i], own * local_width, local_width, 0) for i in (6, 7)]
    grad_bup = lax.dynamic_slice_in_dim(
        small[8:12].reshape(-1), own * hidden_local, hidden_local, 0
    )
    return (
        output,
        grad_tokens,
        small[0],
        small[1],
        grad_wqkv.transpose(1, 0, 2),
        jnp.stack(wide, 0),
        grad_wout.astype(f32),
        small[4],
        small[2],
        small[3],
        grad_wup.astype(f32),
        grad_bup,
        grad_wdown.astype(f32),
        small[5],
    )


def on_device(
    tokens,
    d_output,
    lengths,
    ln1_gain,
    ln1_bias,
    w_qkv,
    qv_bias,
    w_out,
    bias_out,
    ln2_gain,
    ln2_bias,
    w_up,
    b_up,
    w_down,
    b_down,
):
    parts = lax.axis_size("tensor")
    place = lax.axis_index("tensor")
    batches, slots, width = tokens.shape
    share = slots // parts
    row_start = place * share
    local_width = w_qkv.shape[2]
    hidden_local = w_up.shape[1]
    heads_local = local_width // HEAD_DIM
    scale = 1.0 / math.sqrt(HEAD_DIM)
    first_head = place * heads_local
    slopes = jnp.exp2(
        -8.0
        * ((first_head + jnp.arange(heads_local, dtype=jnp.int32)).astype(jnp.float32) + 1.0)
        / HEADS
    )
    weight_qkv = w_qkv.reshape(width, 3 * local_width)
    qkv_shift = jnp.concatenate(
        [
            qv_bias[0].astype(jnp.float32),
            jnp.zeros((local_width,), jnp.float32),
            qv_bias[1].astype(jnp.float32),
        ]
    )
    gain_one = ln1_gain.astype(jnp.float32)
    shift_one = ln1_bias.astype(jnp.float32)
    gain_two = ln2_gain.astype(jnp.float32)
    shift_two = ln2_bias.astype(jnp.float32)
    out_shift = bias_out.astype(jnp.float32)
    up_shift = b_up.astype(jnp.float32)
    down_shift = b_down.astype(jnp.float32)
    grad_qkv = jnp.zeros((width, 3 * local_width), jnp.float32)
    grad_qvb = jnp.zeros((2, local_width), jnp.float32)
    grad_wout = jnp.zeros((local_width, width), jnp.float32)
    grad_wup = jnp.zeros((width, hidden_local), jnp.float32)
    grad_bup = jnp.zeros((hidden_local,), jnp.float32)
    grad_wdown = jnp.zeros((hidden_local, width), jnp.float32)
    grad_gain_one = jnp.zeros((width,), jnp.float32)
    grad_shift_one = jnp.zeros((width,), jnp.float32)
    grad_gain_two = jnp.zeros((width,), jnp.float32)
    grad_shift_two = jnp.zeros((width,), jnp.float32)
    grad_out_shift = jnp.zeros((width,), jnp.float32)
    grad_down_shift = jnp.zeros((width,), jnp.float32)
    output_rows = []
    input_rows = []
    for index in range(batches):
        tokens_f = tokens[index].astype(jnp.float32)
        length = lengths[index]
        normal_one, inverse_one = norm_parts(tokens_f)
        normed_one = (normal_one * gain_one + shift_one).astype(jnp.bfloat16)
        projected = (matmul(normed_one, weight_qkv) + qkv_shift).astype(jnp.bfloat16)
        query = projected[:, :local_width].reshape(slots, heads_local, HEAD_DIM)
        keys = projected[:, local_width : 2 * local_width].reshape(slots, heads_local, HEAD_DIM)
        values = projected[:, 2 * local_width :].reshape(slots, heads_local, HEAD_DIM)
        attn = attention_forward(query, keys, values, length, slopes, scale)
        partial_value = matmul(attn, w_out)
        summed = lax.psum(partial_value.astype(jnp.bfloat16), "tensor").astype(jnp.float32)
        hidden_full = tokens_f + summed + out_shift
        normal_full, inverse_full = norm_parts(hidden_full)
        normed_two = (normal_full * gain_two + shift_two).astype(jnp.bfloat16)
        hidden_rows = lax.dynamic_slice_in_dim(hidden_full, row_start, share, 0)
        normal_two = lax.dynamic_slice_in_dim(normal_full, row_start, share, 0)
        inverse_two = lax.dynamic_slice_in_dim(inverse_full, row_start, share, 0)
        pre = matmul(normed_two, w_up) + up_shift
        act_value, act_slope = gelu_parts(pre)
        act = act_value.astype(jnp.bfloat16)
        mlp_part = lax.psum_scatter(
            matmul(act, w_down).astype(jnp.bfloat16), "tensor", scatter_dimension=0, tiled=True
        ).astype(jnp.float32)
        output_rows.append((hidden_rows + mlp_part + down_shift).astype(jnp.bfloat16))
        valid = (jnp.arange(slots, dtype=jnp.int32) < length).astype(jnp.float32)[:, None]
        grad_out = d_output[index].astype(jnp.float32) * valid
        grad_two = grad_out.astype(jnp.bfloat16)
        grad_wdown = grad_wdown + contract_rows(act, grad_two)
        grad_pre = (contract_cols(grad_two, w_down) * act_slope).astype(jnp.bfloat16)
        grad_wup = grad_wup + contract_rows(normed_two, grad_pre)
        grad_bup = grad_bup + jnp.sum(grad_pre.astype(jnp.float32), 0)
        grad_norm_two = lax.psum_scatter(
            contract_cols(grad_pre, w_up).astype(jnp.bfloat16),
            "tensor",
            scatter_dimension=0,
            tiled=True,
        ).astype(jnp.float32)
        grad_gain_two = grad_gain_two + jnp.sum(grad_norm_two * normal_two, 0)
        grad_shift_two = grad_shift_two + jnp.sum(grad_norm_two, 0)
        grad_out_rows = lax.dynamic_slice_in_dim(grad_out, row_start, share, 0)
        grad_hidden_rows = grad_out_rows + norm_backward(
            grad_norm_two, normal_two, inverse_two, gain_two
        )
        grad_one_rows = grad_hidden_rows.astype(jnp.bfloat16)
        grad_down_shift = grad_down_shift + jnp.sum(
            lax.dynamic_slice_in_dim(grad_two, row_start, share, 0).astype(jnp.float32), 0
        )
        grad_out_shift = grad_out_shift + jnp.sum(grad_one_rows.astype(jnp.float32), 0)
        grad_one = lax.all_gather(grad_one_rows, "tensor", axis=0, tiled=True)
        grad_wout = grad_wout + contract_rows(attn, grad_one)
        grad_attn = (
            contract_cols(grad_one, w_out)
            .astype(jnp.bfloat16)
            .reshape(slots, heads_local, HEAD_DIM)
        )
        grad_query, grad_keys, grad_values = attention_backward(
            query, keys, values, grad_attn, length, slopes, scale
        )
        grad_proj = jnp.concatenate([grad_query, grad_keys, grad_values], 1)
        grad_qkv = grad_qkv + contract_rows(normed_one, grad_proj)
        grad_qvb = grad_qvb + jnp.stack(
            [
                jnp.sum(grad_query.astype(jnp.float32), 0),
                jnp.sum(grad_values.astype(jnp.float32), 0),
            ],
            0,
        )
        grad_norm_one = lax.psum_scatter(
            contract_cols(grad_proj, weight_qkv).astype(jnp.bfloat16),
            "tensor",
            scatter_dimension=0,
            tiled=True,
        ).astype(jnp.float32)
        normal_one_rows = lax.dynamic_slice_in_dim(normal_one, row_start, share, 0)
        inverse_one_rows = lax.dynamic_slice_in_dim(inverse_one, row_start, share, 0)
        grad_gain_one = grad_gain_one + jnp.sum(grad_norm_one * normal_one_rows, 0)
        grad_shift_one = grad_shift_one + jnp.sum(grad_norm_one, 0)
        input_rows.append(
            (
                grad_hidden_rows
                + norm_backward(grad_norm_one, normal_one_rows, inverse_one_rows, gain_one)
            ).astype(jnp.bfloat16)
        )
    grad_qkv, grad_qvb, grad_wout, grad_wup, grad_bup, grad_wdown = (
        lax.psum(grad_qkv.astype(jnp.bfloat16), "dp").astype(jnp.float32),
        lax.psum(grad_qvb.astype(jnp.bfloat16), "dp").astype(jnp.float32),
        lax.psum(grad_wout.astype(jnp.bfloat16), "dp").astype(jnp.float32),
        lax.psum(grad_wup.astype(jnp.bfloat16), "dp").astype(jnp.float32),
        lax.psum(grad_bup.astype(jnp.bfloat16), "dp").astype(jnp.float32),
        lax.psum(grad_wdown.astype(jnp.bfloat16), "dp").astype(jnp.float32),
    )
    (
        grad_gain_one,
        grad_shift_one,
        grad_gain_two,
        grad_shift_two,
        grad_out_shift,
        grad_down_shift,
    ) = lax.psum(
        (
            grad_gain_one,
            grad_shift_one,
            grad_gain_two,
            grad_shift_two,
            grad_out_shift,
            grad_down_shift,
        ),
        ("dp", "tensor"),
    )
    return (
        jnp.stack(output_rows, 0),
        jnp.stack(input_rows, 0),
        grad_gain_one,
        grad_shift_one,
        grad_qkv.reshape(width, 3, local_width),
        grad_qvb,
        grad_wout,
        grad_out_shift,
        grad_gain_two,
        grad_shift_two,
        grad_wup,
        grad_bup,
        grad_wdown,
        grad_down_shift,
    )


def solution(mesh):
    whole = mesh.shape["tensor"] == 2 and mesh.shape["dp"] == 2 * len(RING)
    return jax.shard_map(
        whole_sequence if whole else on_device,
        mesh=mesh,
        in_specs=(
            P("dp", None, None),
            P("dp", None, None),
            P("dp"),
            P(),
            P(),
            P(None, None, "tensor"),
            P(None, "tensor"),
            P("tensor", None),
            P(),
            P(),
            P(),
            P(None, "tensor"),
            P("tensor"),
            P("tensor", None),
            P(),
        ),
        out_specs=(
            P("dp", "tensor", None),
            P("dp", "tensor", None),
            P(),
            P(),
            P(None, None, "tensor"),
            P(None, "tensor"),
            P("tensor", None),
            P(),
            P(),
            P(),
            P(None, "tensor"),
            P("tensor"),
            P("tensor", None),
            P(),
        ),
        check_vma=False,
    )
```

```python
import functools
import math

import jax
import jax.numpy as jnp
import numpy as np
from jax import lax
from jax.experimental import pallas as pl
from jax.experimental.pallas import tpu as pltpu
from jax.sharding import PartitionSpec as P

HEADS = 16
HEAD_DIM = 64


epsilon = 1e-05
root_two_pi = math.sqrt(2.0 / math.pi)
masked_score = -1e30


def matmul(left, right):
    return jnp.dot(left, right, preferred_element_type=jnp.float32)


def contract_rows(left, right):
    return lax.dot_general(
        left, right, (((0,), (0,)), ((), ())), preferred_element_type=jnp.float32
    )


def contract_cols(left, right):
    return lax.dot_general(
        left, right, (((1,), (1,)), ((), ())), preferred_element_type=jnp.float32
    )


def norm_parts(values):
    centre = jnp.mean(values, -1, keepdims=True)
    shifted = values - centre
    inverse = lax.rsqrt(jnp.mean(shifted * shifted, -1, keepdims=True) + epsilon)
    return (shifted * inverse, inverse)


def norm_backward(grad_normed, normal, inverse, gain):
    scaled = grad_normed * gain
    return inverse * (
        scaled
        - jnp.mean(scaled, -1, keepdims=True)
        - normal * jnp.mean(scaled * normal, -1, keepdims=True)
    )


def gelu_parts(pre):
    tangent = jnp.tanh(root_two_pi * (pre + 0.044715 * pre * pre * pre))
    value = 0.5 * pre * (1.0 + tangent)
    slope = 0.5 * (1.0 + tangent) + 0.5 * pre * (1.0 - tangent * tangent) * root_two_pi * (
        1.0 + 3.0 * 0.044715 * pre * pre
    )
    return (value, slope)


def block_probs(query_rows, key_rows, start, length, slopes, scale):
    rows = query_rows.shape[0]
    cols = key_rows.shape[0]
    products = jnp.einsum("ihd,jhd->hij", query_rows, key_rows, preferred_element_type=jnp.float32)
    key_place = jnp.arange(cols, dtype=jnp.int32)
    distance = (start + jnp.arange(rows, dtype=jnp.int32))[:, None] - key_place[None, :]
    scores = products * scale - slopes[:, None, None] * distance.astype(jnp.float32)[None]
    allowed = (distance >= 0) & (key_place[None, :] < length)
    masked = jnp.where(allowed[None], scores, masked_score)
    highest = jnp.max(masked, -1, keepdims=True)
    exponent = jnp.exp(masked - highest)
    return exponent / jnp.sum(exponent, -1, keepdims=True)


def attention_forward(query, keys, values, length, slopes, scale):
    slots = query.shape[0]
    block = min(512, slots)
    outputs = []
    for number in range(slots // block):
        start = number * block
        probs = block_probs(query[start : start + block], keys, start, length, slopes, scale)
        mixed = jnp.einsum(
            "hij,jhd->ihd", probs.astype(jnp.bfloat16), values, preferred_element_type=jnp.float32
        )
        outputs.append(mixed.reshape(block, -1).astype(jnp.bfloat16))
    return jnp.concatenate(outputs, 0)


def attention_backward(query, keys, values, grad_attn, length, slopes, scale):
    slots, heads_local, head_width = query.shape
    block = min(512, slots)
    grad_keys = jnp.zeros((slots, heads_local, head_width), jnp.float32)
    grad_values = jnp.zeros((slots, heads_local, head_width), jnp.float32)
    query_parts = []
    for number in range(slots // block):
        start = number * block
        query_rows = query[start : start + block]
        grad_rows = grad_attn[start : start + block]
        probs = block_probs(query_rows, keys, start, length, slopes, scale)
        grad_probs = jnp.einsum(
            "ihd,jhd->hij", grad_rows, values, preferred_element_type=jnp.float32
        )
        delta = jnp.sum(probs * grad_probs, -1, keepdims=True)
        grad_scores = (probs * (grad_probs - delta)).astype(jnp.bfloat16)
        part_query = (
            jnp.einsum("hij,jhd->ihd", grad_scores, keys, preferred_element_type=jnp.float32)
            * scale
        )
        part_keys = (
            jnp.einsum("hij,ihd->jhd", grad_scores, query_rows, preferred_element_type=jnp.float32)
            * scale
        )
        part_values = jnp.einsum(
            "hij,ihd->jhd",
            probs.astype(jnp.bfloat16),
            grad_rows,
            preferred_element_type=jnp.float32,
        )
        part_query, part_keys, part_values = (part_query, part_keys, part_values)
        query_parts.append(part_query)
        grad_keys = grad_keys.at[:slots].add(part_keys)
        grad_values = grad_values.at[:slots].add(part_values)
    grad_query = jnp.concatenate(query_parts, 0).reshape(slots, -1).astype(jnp.bfloat16)
    return (
        grad_query,
        grad_keys.reshape(slots, -1).astype(jnp.bfloat16),
        grad_values.reshape(slots, -1).astype(jnp.bfloat16),
    )


QUERY_BLOCK = 256
KEY_BLOCK = 1024
PAIR = 128
NT = (((1,), (1,)), ((), ()))
TN = (((0,), (0,)), ((), ()))


def mm(left, right, dims=(((1,), (0,)), ((), ()))):
    return lax.dot_general(left, right, dims, preferred_element_type=jnp.float32)


def low_lanes(rows):
    return lax.broadcasted_iota(jnp.int32, (rows, PAIR), 1) < HEAD_DIM


def slope_rows():
    table = np.zeros((HEADS // 2, 8, PAIR), np.float64)
    for head in range(HEADS):
        rest = np.float64(np.float32(2.0 ** (-8.0 * (head + 1) / HEADS)))
        base = HEAD_DIM * (1 - head % 2)
        for part in range(3):
            piece = np.float64(np.asarray(rest).astype(jnp.bfloat16))
            rest = rest - piece
            table[head // 2, head % 2, base + part] = 32.0 * piece
            table[head // 2, head % 2, base + 3 + part] = piece
        table[head // 2, head % 2, base + 6] = 1.0
    return table.astype(jnp.bfloat16)


def key_lanes(slots, length):
    place = jnp.arange(slots, dtype=jnp.int32)[:, None]
    lane = jnp.arange(PAIR, dtype=jnp.int32)[None, :] % HEAD_DIM
    high = (place // 32).astype(jnp.float32)
    low = (place % 32).astype(jnp.float32)
    mask = jnp.where(place < length, 0.0, masked_score)
    return jnp.where(
        lane < 3, high, jnp.where(lane < 6, low, jnp.where(lane == 6, mask, 0.0))
    ).astype(jnp.bfloat16)


def forward_kernel(
    q_ref, k_ref, v_ref, lanes_ref, rows_ref, o_ref, level_ref, key0, key1, val0, val1
):
    slots = q_ref.shape[0]
    block = QUERY_BLOCK
    low = low_lanes(slots)
    zero = jnp.zeros((slots, PAIR), jnp.bfloat16)
    one = jnp.ones((slots, PAIR), jnp.bfloat16)
    key0[...] = jnp.where(low, k_ref[...], lanes_ref[...])
    key1[...] = jnp.where(low, lanes_ref[...], k_ref[...])
    val0[:, :PAIR] = jnp.where(low, v_ref[...], zero)
    val0[:, PAIR:] = jnp.where(low, one, zero)
    val1[:, :PAIR] = jnp.where(low, zero, v_ref[...])
    val1[:, PAIR:] = jnp.where(low, zero, one)
    low_block = low_lanes(block)
    causal = lax.broadcasted_iota(jnp.int32, (block, block), 1) <= lax.broadcasted_iota(
        jnp.int32, (block, block), 0
    )
    for number in range(slots // block):
        start = number * block
        rows = q_ref[start : start + block, :] * jnp.bfloat16(0.125)
        total = None
        tops = []
        for head, (key, val) in enumerate(((key0, val0), (key1, val1))):
            extra = jnp.broadcast_to(rows_ref[0, head : head + 1, :], (block, PAIR))
            query = jnp.where(low_block, rows, extra) if head == 0 else jnp.where(
                low_block, extra, rows
            )
            own = jnp.where(causal, mm(query, key[start : start + block, :], NT), masked_score)
            highest = jnp.max(own, 1, keepdims=True)
            if start:
                past = mm(query, key[:start, :], NT)
                highest = jnp.maximum(highest, jnp.max(past, 1, keepdims=True))
                part = mm(jnp.exp(past - highest).astype(jnp.bfloat16), val[:start, :])
                total = part if total is None else total + part
            part = mm(jnp.exp(own - highest).astype(jnp.bfloat16), val[start : start + block, :])
            total = part if total is None else total + part
            tops.append(highest)
        o_ref[start : start + block, :] = (total[:, :PAIR] / total[:, PAIR:]).astype(jnp.bfloat16)
        level = (jnp.where(low_block, tops[0], tops[1]) + jnp.log(total[:, PAIR:])).T
        level_ref[0, 0:1, start : start + block] = level[0:1, :]
        level_ref[0, 1:2, start : start + block] = level[HEAD_DIM : HEAD_DIM + 1, :]


def backward_kernel(
    q_ref, k_ref, v_ref, o_ref, g_ref, level_ref, lanes_ref, rows_ref, dq_ref, dk_ref, dv_ref,
    key0, key1, val0, val1, bare0, bare1, total_k, total_v,
):
    slots = q_ref.shape[0]
    block = QUERY_BLOCK
    piece = KEY_BLOCK
    low = low_lanes(slots)
    zero = jnp.zeros((slots, PAIR), jnp.bfloat16)
    key0[...] = jnp.where(low, k_ref[...], lanes_ref[...])
    key1[...] = jnp.where(low, lanes_ref[...], k_ref[...])
    bare0[...] = jnp.where(low, k_ref[...], zero)
    bare1[...] = jnp.where(low, zero, k_ref[...])
    val0[...] = jnp.where(low, v_ref[...], zero)
    val1[...] = jnp.where(low, zero, v_ref[...])
    low_block = low_lanes(block)
    nil = jnp.zeros((block, PAIR), jnp.bfloat16)
    causal = lax.broadcasted_iota(jnp.int32, (block, block), 0) <= lax.broadcasted_iota(
        jnp.int32, (block, block), 1
    )
    for number in reversed(range(slots // block)):
        start = number * block
        stop = start + block
        rows = q_ref[start:stop, :] * jnp.bfloat16(0.125)
        grad = g_ref[start:stop, :]
        shares = (grad.astype(jnp.float32) * o_ref[start:stop, :].astype(jnp.float32)).T
        deltas = [
            jnp.sum(shares[head * HEAD_DIM : (head + 1) * HEAD_DIM, :], 0, keepdims=True)
            for head in range(2)
        ]
        levels = [level_ref[0, head : head + 1, start:stop] for head in range(2)]
        extras = [jnp.broadcast_to(rows_ref[0, h : h + 1, :], (block, PAIR)) for h in range(2)]
        queries = (
            jnp.where(low_block, rows, extras[0]),
            jnp.where(low_block, extras[1], rows),
        )
        grads = jnp.concatenate(
            [jnp.where(low_block, grad, nil), jnp.where(low_block, nil, grad)], 0
        )
        both = jnp.concatenate(
            [jnp.where(low_block, rows, nil), jnp.where(low_block, nil, rows)], 0
        )
        grad_query = None
        for begin in range(0, stop, min(piece, stop)):
            end = min(begin + piece, stop)
            probs, scores = [], []
            for head, (key, val, bare) in enumerate(((key0, val0, bare0), (key1, val1, bare1))):
                score = mm(key[begin:end, :], queries[head], NT)
                if end > start:
                    own = jnp.where(causal, score[start - begin :], masked_score)
                    score = jnp.concatenate([score[: start - begin], own], 0) if start > begin else own
                prob = jnp.exp(score - levels[head])
                grad_prob = mm(val[begin:end, :], grad, NT)
                grad_score = (prob * (grad_prob - deltas[head])).astype(jnp.bfloat16)
                probs.append(prob.astype(jnp.bfloat16))
                scores.append(grad_score)
                part = mm(grad_score, bare[begin:end, :], TN)
                grad_query = part if grad_query is None else grad_query + part
            part_v = mm(jnp.concatenate(probs, 1), grads)
            part_k = mm(jnp.concatenate(scores, 1), both)
            if stop == slots:
                total_v[begin:end, :] = part_v
                total_k[begin:end, :] = part_k
            else:
                total_v[begin:end, :] += part_v
                total_k[begin:end, :] += part_k
        dq_ref[start:stop, :] = (grad_query * 0.125).astype(jnp.bfloat16)
    dk_ref[...] = total_k[...].astype(jnp.bfloat16)
    dv_ref[...] = total_v[...].astype(jnp.bfloat16)


def pair_specs(slots):
    part = pl.BlockSpec((slots, PAIR), lambda pair: (0, pair))
    lanes = pl.BlockSpec((slots, PAIR), lambda pair: (0, 0))
    rows = pl.BlockSpec((1, 8, PAIR), lambda pair: (pair, 0, 0))
    levels = pl.BlockSpec((1, 8, slots), lambda pair: (pair, 0, 0))
    return part, lanes, rows, levels


def attention_out(query, keys, values, lanes, rows):
    slots, columns = query.shape
    part, lane_spec, row_spec, level_spec = pair_specs(slots)
    pairs = columns // PAIR
    half = slots * slots * PAIR * pairs
    return pl.pallas_call(
        forward_kernel,
        grid=(pairs,),
        out_shape=(
            jax.ShapeDtypeStruct((slots, columns), jnp.bfloat16),
            jax.ShapeDtypeStruct((pairs, 8, slots), jnp.float32),
        ),
        in_specs=[part, part, part, lane_spec, row_spec],
        out_specs=(part, level_spec),
        scratch_shapes=[pltpu.VMEM((slots, PAIR), jnp.bfloat16)] * 2
        + [pltpu.VMEM((slots, 2 * PAIR), jnp.bfloat16)] * 2,
        cost_estimate=pl.CostEstimate(
            flops=8 * half, bytes_accessed=8 * slots * columns, transcendentals=slots * slots * pairs
        ),
        name="attention_out",
    )(query, keys, values, lanes, rows)


def attention_grads(query, keys, values, mixed, levels, grad, lanes, rows):
    slots, columns = query.shape
    part, lane_spec, row_spec, level_spec = pair_specs(slots)
    pairs = columns // PAIR
    half = slots * slots * PAIR * pairs
    shape = jax.ShapeDtypeStruct((slots, columns), jnp.bfloat16)
    return pl.pallas_call(
        backward_kernel,
        grid=(pairs,),
        out_shape=(shape, shape, shape),
        in_specs=[part, part, part, part, part, level_spec, lane_spec, row_spec],
        out_specs=(part, part, part),
        scratch_shapes=[pltpu.VMEM((slots, PAIR), jnp.bfloat16)] * 6
        + [pltpu.VMEM((slots, PAIR), jnp.float32)] * 2,
        cost_estimate=pl.CostEstimate(
            flops=20 * half,
            bytes_accessed=14 * slots * columns,
            transcendentals=slots * slots * pairs,
        ),
        name="attention_grads",
    )(query, keys, values, mixed, grad, levels, lanes, rows)


ROW_BLOCK = 256


def whole_spec(array):
    zeros = (0,) * array.ndim
    return pl.BlockSpec(array.shape, lambda *_: zeros)


def row_spec(columns):
    return pl.BlockSpec((ROW_BLOCK, columns), lambda row, *_: (row, 0))


def own_spec(columns):
    return pl.BlockSpec((1, ROW_BLOCK, columns), lambda row, facts: (facts[0], row, 0))


def over_rows(kernel, slots, facts, inputs, outputs, flops):
    arrays, in_specs = zip(*inputs)
    shapes, out_specs = zip(*outputs)
    return pl.pallas_call(
        kernel,
        grid_spec=pltpu.PrefetchScalarGridSpec(
            num_scalar_prefetch=1,
            grid=(slots // ROW_BLOCK,),
            in_specs=list(in_specs),
            out_specs=list(out_specs),
        ),
        out_shape=list(shapes),
        cost_estimate=pl.CostEstimate(
            flops=flops,
            bytes_accessed=sum(array.size * array.dtype.itemsize for array in arrays),
            transcendentals=0,
        ),
    )(facts, *arrays)


def project_kernel(facts, tok_ref, gain_ref, shift_ref, w_ref, bias_ref, *refs):
    norm_ref, q_ref, k_ref, v_ref = refs[-4:]
    normal, _ = norm_parts(tok_ref[0].astype(jnp.float32))
    normed = (normal * gain_ref[...] + shift_ref[...]).astype(jnp.bfloat16)
    norm_ref[...] = normed
    q_ref[...] = (mm(normed, w_ref[0]) + bias_ref[0:1, :]).astype(jnp.bfloat16)
    k_ref[...] = mm(normed, w_ref[1]).astype(jnp.bfloat16)
    v_ref[...] = (mm(normed, w_ref[2]) + bias_ref[1:2, :]).astype(jnp.bfloat16)


def hidden_kernel(
    facts, tok_ref, a0_ref, a1_ref, w0_ref, w1_ref, bias_ref, gain_ref, shift_ref, hid_ref, norm_ref
):
    hidden = tok_ref[0].astype(jnp.float32) + bias_ref[...]
    hidden = hidden + mm(a0_ref[...], w0_ref[...]) + mm(a1_ref[...], w1_ref[...])
    hid_ref[...] = hidden
    normal, _ = norm_parts(hidden)
    norm_ref[...] = (normal * gain_ref[...] + shift_ref[...]).astype(jnp.bfloat16)


def act_kernel(norm_ref, w_ref, bias_ref, act_ref, slope_ref):
    def rows(number, carry):
        at = pl.ds(pl.multiple_of(number * ROW_BLOCK, ROW_BLOCK), ROW_BLOCK)
        value, slope = gelu_parts(mm(norm_ref[at, :], w_ref[...]) + bias_ref[...])
        act_ref[at, :] = value.astype(jnp.bfloat16)
        slope_ref[at, :] = slope.astype(jnp.bfloat16)
        return carry

    lax.fori_loop(0, norm_ref.shape[0] // ROW_BLOCK, rows, 0, unroll=True)


def activations(normed, weight, bias):
    slots, width = normed.shape
    hidden = weight.shape[1]
    columns = 512
    out = pl.BlockSpec((slots, columns), lambda col: (0, col))
    shape = jax.ShapeDtypeStruct((slots, hidden), jnp.bfloat16)
    return pl.pallas_call(
        act_kernel,
        grid=(hidden // columns,),
        in_specs=[
            whole_spec(normed),
            pl.BlockSpec((width, columns), lambda col: (0, col)),
            pl.BlockSpec((1, columns), lambda col: (0, col)),
        ],
        out_specs=(out, out),
        out_shape=(shape, shape),
        cost_estimate=pl.CostEstimate(
            flops=2 * slots * width * hidden,
            bytes_accessed=8 * slots * hidden,
            transcendentals=slots * hidden,
        ),
        name="activations",
    )(normed, weight, bias)


def output_kernel(facts, hid_ref, a0_ref, a1_ref, w0_ref, w1_ref, bias_ref, tie_ref, out_ref):
    total = hid_ref[...] + bias_ref[...] + mm(a0_ref[...], w0_ref[...])
    out_ref[...] = (total + mm(a1_ref[...], w1_ref[...])).astype(jnp.bfloat16)


def add_sums(sums_ref, rows):
    @pl.when(pl.program_id(0) == 0)
    def _():
        sums_ref[...] = jnp.zeros_like(sums_ref)

    for index, value in enumerate(rows):
        sums_ref[index : index + 1, :] += jnp.sum(value, 0, keepdims=True)


def hidden_grad_kernel(
    facts, g0_ref, g1_ref, w0_ref, w1_ref, hid_ref, gain_ref, dout_ref, grad_ref, one_ref, sums_ref
):
    grad_norm = mm(g0_ref[...], w0_ref[...], NT) + mm(g1_ref[...], w1_ref[...], NT)
    normal, inverse = norm_parts(hid_ref[...])
    place = lax.broadcasted_iota(jnp.int32, grad_norm.shape, 0) + pl.program_id(0) * ROW_BLOCK
    grad_out = jnp.where(place < facts[1], dout_ref[0].astype(jnp.float32), 0.0)
    grad = grad_out + norm_backward(grad_norm, normal, inverse, gain_ref[...])
    one = grad.astype(jnp.bfloat16)
    grad_ref[...] = grad
    one_ref[...] = one
    add_sums(sums_ref, [grad_norm * normal, grad_norm, one.astype(jnp.float32), grad_out])


def token_grad_kernel(
    facts, q0_ref, k0_ref, v0_ref, q1_ref, k1_ref, v1_ref, w0_ref, w1_ref, tok_ref, grad_ref,
    gain_ref, *refs,
):
    out_ref, sums_ref, heads_ref = refs[-3:]
    grad_norm = None
    for refs, weight in (((q0_ref, k0_ref, v0_ref), w0_ref), ((q1_ref, k1_ref, v1_ref), w1_ref)):
        for part, ref in enumerate(refs):
            more = mm(ref[...], weight[part], NT)
            grad_norm = more if grad_norm is None else grad_norm + more
    normal, inverse = norm_parts(tok_ref[0].astype(jnp.float32))
    grad = grad_ref[...] + norm_backward(grad_norm, normal, inverse, gain_ref[...])
    out_ref[...] = grad.astype(jnp.bfloat16)
    add_sums(sums_ref, [grad_norm * normal, grad_norm])
    add_sums(heads_ref, [ref[...].astype(jnp.float32) for ref in (q0_ref, q1_ref, v0_ref, v1_ref)])


RING = ((0, 0), (1, 0), (2, 0), (3, 0), (3, 1), (2, 1), (1, 1), (0, 1))


def device_of(z, y, core):
    return (z * 2 + y) * 2 + core


def to_tensor(value):
    return lax.ppermute(value, "tensor", [(0, 1), (1, 0)])


def to_core(value):
    return lax.ppermute(value, "dp", [(i, i ^ 1) for i in range(2 * len(RING))])


def rows_at(value, start, size):
    return lax.dynamic_slice_in_dim(value, start, size, value.ndim - 2)


def after(value, *earlier):
    return lax.optimization_barrier((value, *earlier))[0]


def piece(weight, index, pieces):
    size = weight.shape[-2] // pieces
    return rows_at(weight, index * size, size)


def both_cores(value, core, axis):
    beside = to_core(value)
    first = jnp.where(core == 0, value, beside)
    second = jnp.where(core == 0, beside, value)
    return jnp.concatenate([first, second], axis)


class Ring:
    def __init__(self, values, slots, sums, results, sems, cuts):
        self.values, self.slots, self.sums, self.results = values, slots, sums, results
        self.send_sems, self.recv_sems, self.swap_send_sems, self.swap_recv_sems = sems
        self.cuts = cuts
        self.count = count = len(RING)
        self.device = device = lax.axis_index("dp")
        self.core, self.y, self.z = lax.rem(device, 2), lax.rem(device // 2, 2), device // 4
        self.place = place = self.z * (1 - self.y) + (count - 1 - self.z) * self.y
        self.nexts = tuple(
            self.at_place(lax.rem(place + step, count)) for step in (1, count - 1)
        )
        self.partner = {"dp": device + 1 - 2 * self.core}
        self.streams = [
            (array, way, cut)
            for cut in range(cuts)
            for array in range(len(values))
            for way in range(2)
        ]

    def at_place(self, where):
        side = where // 4
        return {
            "dp": device_of(where * (1 - side) + (self.count - 1 - where) * side, side, self.core)
        }

    def greet(self, others=()):
        barrier = pltpu.get_barrier_semaphore()
        greeted = [*self.nexts, self.partner, *others]
        for target in greeted:
            pl.semaphore_signal(
                barrier, inc=1, device_id=target, device_id_type=pl.DeviceIdType.MESH
            )
        pl.semaphore_wait(barrier, len(greeted))

    def block(self, way, offset):
        return lax.rem(self.place - (1, -1)[way] * offset + 2 * self.count, self.count)

    def rows(self, array, cut):
        size = self.values[array].shape[2] // self.cuts
        return pl.ds(cut * size, size)

    def result(self, stream, step):
        array, way, cut = stream
        return self.results[array].at[
            self.core, way, self.block(way, step), self.rows(array, cut)
        ]

    def copy(self, stream, step):
        array, way, cut = stream
        rows = self.rows(array, cut)
        if step < self.count - 1:
            target = self.slots[array].at[way, step, rows]
            if step:
                source = self.sums[array].at[way, step - 1, rows]
            else:
                source = self.values[array].at[way, self.block(way, 0), rows]
        else:
            source = target = self.result(stream, step)
        index = self.streams.index(stream)
        return pltpu.make_async_remote_copy(
            src_ref=source,
            dst_ref=target,
            send_sem=self.send_sems.at[index, step],
            recv_sem=self.recv_sems.at[index, step],
            device_id=self.nexts[way],
            device_id_type=pl.DeviceIdType.MESH,
        )

    def swap(self, stream, step):
        index = self.streams.index(stream)
        turn = step - self.count + 1
        done = self.result(stream, step)
        return pltpu.make_async_remote_copy(
            src_ref=done,
            dst_ref=done,
            send_sem=self.swap_send_sems.at[index, turn],
            recv_sem=self.swap_recv_sems.at[index, turn],
            device_id=self.partner,
            device_id_type=pl.DeviceIdType.MESH,
        )

    def first(self):
        for stream in self.streams:
            self.copy(stream, 0).start()

    def hop(self, step):
        count = self.count
        for stream in self.streams:
            array, way, cut = stream
            rows = self.rows(array, cut)
            self.copy(stream, step - 1).wait_recv()
            if step < count:
                total = self.values[array][way, self.block(way, step), rows].astype(jnp.float32)
                total = total + self.slots[array][way, step - 1, rows].astype(jnp.float32)
                total = total.astype(jnp.bfloat16)
                if step < count - 1:
                    self.sums[array][way, step - 1, rows] = total
                else:
                    self.results[array][self.core, way, self.block(way, step), rows] = total
            self.copy(stream, step).start()
            if step >= count - 1:
                self.swap(stream, step).start()

    def last(self):
        for stream in self.streams:
            self.copy(stream, 2 * self.count - 3).wait_recv()
            self.swap(stream, 2 * self.count - 2).start()

    def drain(self):
        for stream in self.streams:
            for step in range(2 * self.count - 2):
                self.copy(stream, step).wait_send()
            for step in range(self.count - 1, 2 * self.count - 1):
                self.swap(stream, step).wait()


def ring_shape(value):
    count = len(RING)
    return value.reshape(2, count, value.shape[0] // (2 * count), value.shape[1])


def ring_scratch(shaped, cuts):
    count = len(RING)
    streams = 2 * len(shaped) * cuts
    scratch = [pltpu.VMEM((2, count - 1, *value.shape[2:]), value.dtype) for value in shaped]
    scratch += [pltpu.VMEM((2, count - 2, *value.shape[2:]), value.dtype) for value in shaped]
    scratch += [pltpu.SemaphoreType.DMA((streams, 2 * count - 2))] * 2
    return scratch + [pltpu.SemaphoreType.DMA((streams, count))] * 2


def ring_kernel(blocks, cuts, has_small, has_tie, *refs):
    values, refs = refs[:blocks], refs[blocks:]
    if has_small:
        small_ref, refs = refs[0], refs[1:]
    refs = refs[has_tie:]
    results, refs = refs[:blocks], refs[blocks:]
    if has_small:
        small_out, refs = refs[0], refs[1:]
    slots, refs = refs[:blocks], refs[blocks:]
    sums, refs = refs[:blocks], refs[blocks:]
    ring = Ring(values, slots, sums, results, refs[:4], cuts)
    if has_small:
        small_slots, small_sums, small_send_sems, small_recv_sems = refs[4:]
        device, y, z = ring.device, ring.y, ring.z
        small_targets = [
            ring.partner,
            {"tensor": 1 - lax.axis_index("tensor")},
            {"dp": device + 2 - 4 * y},
            {"dp": device + 4 - 8 * lax.rem(z, 2)},
            {"dp": device + 8 - 16 * (z // 2)},
        ]
        ring.greet(small_targets[1:])
    else:
        ring.greet()

    def exchange(turn):
        return pltpu.make_async_remote_copy(
            src_ref=small_ref if turn == 0 else small_sums.at[turn - 1],
            dst_ref=small_slots.at[turn],
            send_sem=small_send_sems.at[turn],
            recv_sem=small_recv_sems.at[turn],
            device_id=small_targets[turn],
            device_id_type=pl.DeviceIdType.MESH,
        )

    def take_exchange(turn):
        exchange(turn).wait_recv()
        total = (small_ref[...] if turn == 0 else small_sums[turn - 1]) + small_slots[turn]
        if turn == len(small_targets) - 1:
            small_out[...] = total
        else:
            small_sums[turn] = total
            exchange(turn + 1).start()

    ring.first()
    if has_small:
        exchange(0).start()
    for step in range(1, 2 * ring.count - 2):
        if has_small and step % 2 == 0 and step // 2 <= len(small_targets):
            take_exchange(step // 2 - 1)
        ring.hop(step)
    ring.last()
    ring.drain()
    if has_small:
        for turn in range(len(small_targets)):
            exchange(turn).wait_send()


def plane_sums(values, identity, small=None, tie=None, cuts=1):
    blocks = len(values)
    shaped = [ring_shape(value) for value in values]
    size = sum(value.size for value in values)
    vmem = pl.BlockSpec(memory_space=pltpu.VMEM)
    inputs, in_specs = list(shaped), [vmem] * blocks
    shapes = [jax.ShapeDtypeStruct((2, *value.shape), value.dtype) for value in shaped]
    scratch = ring_scratch(shaped, cuts)
    if small is not None:
        inputs.append(small)
        in_specs.append(vmem)
        shapes.append(jax.ShapeDtypeStruct(small.shape, small.dtype))
        scratch += [pltpu.VMEM((5, *small.shape), small.dtype)] * 2
        scratch += [pltpu.SemaphoreType.DMA((5,))] * 2
    if tie is not None:
        inputs.append(tie)
        in_specs.append(pl.BlockSpec(memory_space=pl.ANY))
    results = pl.pallas_call(
        functools.partial(ring_kernel, blocks, cuts, small is not None, int(tie is not None)),
        out_shape=shapes,
        in_specs=in_specs,
        out_specs=[vmem] * len(shapes),
        scratch_shapes=scratch,
        compiler_params=pltpu.CompilerParams(collective_id=identity, has_side_effects=True),
        cost_estimate=pl.CostEstimate(flops=size, bytes_accessed=6 * size, transcendentals=0),
        name="plane_sums",
    )(*inputs)
    sums = [
        result.reshape(2 * value.shape[0], value.shape[1]) for result, value in zip(results, values)
    ]
    return sums if small is None else (sums, results[-1])


def core_send(left, rights, core):
    half = left.shape[1] // 2
    part = lax.dynamic_slice_in_dim(left, (1 - core) * half, half, 1)
    sent = [contract_rows(part, right).astype(jnp.bfloat16) for right in rights]
    return sent, [to_core(value) for value in sent]


def core_sum(left, rights, arrived, core):
    half = left.shape[1] // 2
    kept = lax.dynamic_slice_in_dim(left, core * half, half, 1)
    return [
        contract_rows(kept, right) + part.astype(jnp.float32)
        for right, part in zip(rights, arrived)
    ]


def start_grad(left, rights, core):
    _, other = core_send(left[1], rights[1], core)
    sent, local = core_send(left[0], rights[0], core)
    summed = [part.astype(jnp.bfloat16) for part in core_sum(left[1], rights[1], other, core)]
    return local, [to_tensor(part) for part in summed], summed + sent


def pair_grad(left, rights, local, passed, core, *earlier):
    passed = [after(part, *earlier) for part in passed]
    return [
        (part + more.astype(jnp.float32)).astype(jnp.bfloat16)
        for part, more in zip(core_sum(left, rights, local, core), passed)
    ]


def trade_rows(value, own, *earlier):
    share = value.shape[0] // 2
    arrived = to_tensor(lax.dynamic_slice_in_dim(value, (1 - own) * share, share, 0))
    arrived = after(arrived, *earlier) if earlier else arrived
    kept = lax.dynamic_slice_in_dim(value, own * share, share, 0)
    return jnp.stack(
        [jnp.where(own == 0, kept, arrived), jnp.where(own == 0, arrived, kept)], 0
    )


def whole_sequence(*operands):
    return layer(*operands)


def layer(
    tokens,
    d_output,
    lengths,
    ln1_gain,
    ln1_bias,
    w_qkv,
    qv_bias,
    w_out,
    bias_out,
    ln2_gain,
    ln2_bias,
    w_up,
    b_up,
    w_down,
    b_down,
):
    own = lax.axis_index("tensor")
    device = lax.axis_index("dp")
    core = device % 2
    slots, width = tokens.shape[1:]
    local_width = w_qkv.shape[2]
    hidden_local = w_up.shape[1]
    table = jnp.asarray(slope_rows())
    pairs = local_width // PAIR
    f32 = jnp.float32

    weight_qkv = w_qkv.transpose(1, 0, 2)
    biases = jnp.concatenate([qv_bias.reshape(-1), b_up])
    other_biases = to_tensor(biases)
    piece_up, piece_qkv = piece(w_up, device, 2 * len(RING)), piece(weight_qkv, core, 2)
    far_up = to_tensor(piece_up)
    far_qkv = to_tensor(piece_qkv)
    qv = [b[: 2 * local_width].reshape(2, local_width).astype(f32) for b in (biases, other_biases)]
    ups = [b[2 * local_width :].astype(f32)[None] for b in (biases, other_biases)]
    rows = [lax.dynamic_slice_in_dim(table, index * pairs, pairs, 0) for index in (own, 1 - own)]
    gain_one, shift_one = ln1_gain.astype(f32)[None], ln1_bias.astype(f32)[None]
    gain_two, shift_two = ln2_gain.astype(f32)[None], ln2_bias.astype(f32)[None]

    length = lax.dynamic_index_in_dim(lengths, own, 0, keepdims=False)
    facts = jnp.stack([own.astype(jnp.int32), length])
    lanes = key_lanes(slots, length)
    low = jnp.bfloat16

    def run(kernel, inputs, outputs, flops):
        return over_rows(kernel, slots, facts, inputs, outputs, flops)

    def fixed(array):
        return array, whole_spec(array)

    def tied(array):
        return array, pl.BlockSpec(memory_space=pl.ANY)

    def by_row(array):
        return array, row_spec(array.shape[1])

    def rows_out(columns, dtype):
        return jax.ShapeDtypeStruct((slots, columns), dtype), row_spec(columns)

    def sums_out(columns):
        shape = jax.ShapeDtypeStruct((8, columns), f32)
        return shape, whole_spec(shape)

    square = 2 * slots * width
    tokens_in, d_output_in = (tokens, own_spec(width)), (d_output, own_spec(width))
    normed_one, *local_heads = run(
        project_kernel,
        [tokens_in, fixed(gain_one), fixed(shift_one), fixed(weight_qkv), fixed(qv[0])]
        + [tied(piece_up), tied(piece_qkv)],
        [rows_out(width, low)] + [rows_out(local_width, low)] * 3,
        3 * square * local_width,
    )
    attn, level = attention_out(*local_heads, lanes, rows[0])
    heads, mixed, levels = [tuple(local_heads)], [attn], [level]
    far_out = to_tensor(after(piece(w_out, core, 2), normed_one))
    far_down = to_tensor(after(piece(w_down, device, 2 * len(RING)), normed_one))
    up = (w_up, lax.all_gather(after(far_up, normed_one), "dp", axis=0, tiled=True))
    qkv = (weight_qkv, both_cores(after(far_qkv, attn), core, 1))
    query = (matmul(normed_one, qkv[1][0]) + qv[1][0]).astype(low)
    keys = matmul(normed_one, qkv[1][1]).astype(low)
    values = (matmul(normed_one, qkv[1][2]) + qv[1][1]).astype(low)
    heads.append((query, keys, values))
    out = (w_out, both_cores(after(far_out, keys), core, 0))
    attn, level = attention_out(query, keys, values, lanes, rows[1])
    mixed.append(attn)
    levels.append(level)
    down = (w_down, lax.all_gather(after(far_down, attn), "dp", axis=0, tiled=True))
    hidden, normed_two = run(
        hidden_kernel,
        [tokens_in, by_row(mixed[0]), by_row(mixed[1]), fixed(out[0]), fixed(out[1])]
        + [fixed(bias_out.astype(f32)[None]), fixed(gain_two), fixed(shift_two)],
        [rows_out(width, f32), rows_out(width, low)],
        2 * square * local_width,
    )
    acts = [activations(normed_two, up[0], ups[0])]
    up = (up[0], after(up[1], acts[0][0]))
    acts.append(activations(normed_two, up[1], ups[1]))

    valid = (jnp.arange(slots, dtype=jnp.int32) < length).astype(f32)[:, None]
    grad_out = lax.dynamic_index_in_dim(d_output, own, 0, keepdims=False).astype(f32) * valid
    grad_two = grad_out.astype(low)
    left_down, right_down = (acts[0][0], acts[1][0]), ([grad_two], [grad_two])
    local_down, passed_down, sent = start_grad(left_down, right_down, core)
    late_two = after(grad_two, *sent)

    bias_up = []

    def pre_grad(weight, slope):
        value = (contract_cols(late_two, weight) * slope.astype(f32)).astype(low)
        bias_up.append(jnp.sum(value.astype(f32), 0))
        return value

    grad_pre = [pre_grad(down[0], acts[0][1])]
    down = (down[0], after(down[1], grad_pre[0]))
    grad_pre.append(pre_grad(down[1], acts[1][1]))
    left_up, right_up = (normed_two, normed_two), ([grad_pre[0]], [grad_pre[1]])
    local_up, passed_up, sent = start_grad(left_up, right_up, core)
    late_pre = lax.optimization_barrier((*grad_pre, *sent))
    grad_hidden, grad_one, sums_two = run(
        hidden_grad_kernel,
        [by_row(late_pre[0]), by_row(late_pre[1]), fixed(up[0]), fixed(up[1]), by_row(hidden)]
        + [fixed(gain_two), d_output_in],
        [rows_out(width, f32), rows_out(width, low), sums_out(width)],
        2 * square * hidden_local,
    )
    left_out, right_out = (mixed[0], mixed[1]), ([grad_one], [grad_one])
    local_out, passed_out, sent = start_grad(left_out, right_out, core)
    (result,) = run(
        output_kernel,
        [by_row(hidden), by_row(acts[0][0]), by_row(acts[1][0]), fixed(down[0]), fixed(down[1])]
        + [fixed(b_down.astype(f32)[None]), tied(sent[0])],
        [rows_out(width, low)],
        2 * square * hidden_local,
    )
    late_one = after(grad_one, *sent, result)
    grads = [None, None]
    grad_attn = contract_cols(late_one, out[1]).astype(low)
    grads[1] = attention_grads(*heads[1], mixed[1], levels[1], grad_attn, lanes, rows[1])
    _, other_qkv = core_send(normed_one, grads[1], core)
    sent_qkv = [part.astype(low) for part in core_sum(normed_one, grads[1], other_qkv, core)]
    passed_qkv = [to_tensor(part) for part in sent_qkv]
    later_one = after(late_one, *sent_qkv)
    grad_attn = contract_cols(later_one, out[0]).astype(low)
    grads[0] = attention_grads(*heads[0], mixed[0], levels[0], grad_attn, lanes, rows[0])
    sent, local_qkv = core_send(normed_one, grads[0], core)
    grad_tokens, sums_one, sums_heads = run(
        token_grad_kernel,
        [by_row(part) for part in (*grads[0], *grads[1])]
        + [fixed(qkv[0]), fixed(qkv[1]), tokens_in, by_row(grad_hidden), fixed(gain_one)]
        + [tied(part) for part in sent],
        [rows_out(width, low), sums_out(width), sums_out(local_width)],
        6 * square * local_width,
    )
    done = grad_tokens
    output, grad_tokens = trade_rows(result, own, done), trade_rows(grad_tokens, own)

    def in_place(first, second):
        return jnp.concatenate(
            [jnp.where(own == 0, first, second), jnp.where(own == 0, second, first)], 0
        )

    small = jnp.concatenate(
        [
            sums_one[:2],
            sums_two[:4],
            in_place(sums_heads[0], sums_heads[1]).reshape(1, width),
            in_place(sums_heads[2], sums_heads[3]).reshape(1, width),
            in_place(*bias_up).reshape(-1, width),
        ],
        0,
    )
    small = jnp.pad(small, ((0, 16 - small.shape[0]), (0, 0)))
    mine = [
        *pair_grad(left_down[0], right_down[0], local_down, passed_down, core, done),
        *pair_grad(left_up[0], right_up[0], local_up, passed_up, core, done),
        *pair_grad(left_out[0], right_out[0], local_out, passed_out, core, done),
        *pair_grad(normed_one, grads[0], local_qkv, passed_qkv, core, done),
    ]
    (grad_wdown, grad_wup, grad_wout, *grad_wqkv), small = plane_sums(mine, 1, small)
    grad_wqkv = jnp.stack(grad_wqkv, 0).astype(f32)
    wide = [lax.dynamic_slice_in_dim(small[i], own * local_width, local_width, 0) for i in (6, 7)]
    grad_bup = lax.dynamic_slice_in_dim(
        small[8:12].reshape(-1), own * hidden_local, hidden_local, 0
    )
    return (
        output,
        grad_tokens,
        small[0],
        small[1],
        grad_wqkv.transpose(1, 0, 2),
        jnp.stack(wide, 0),
        grad_wout.astype(f32),
        small[4],
        small[2],
        small[3],
        grad_wup.astype(f32),
        grad_bup,
        grad_wdown.astype(f32),
        small[5],
    )


def on_device(
    tokens,
    d_output,
    lengths,
    ln1_gain,
    ln1_bias,
    w_qkv,
    qv_bias,
    w_out,
    bias_out,
    ln2_gain,
    ln2_bias,
    w_up,
    b_up,
    w_down,
    b_down,
):
    parts = lax.axis_size("tensor")
    place = lax.axis_index("tensor")
    batches, slots, width = tokens.shape
    share = slots // parts
    row_start = place * share
    local_width = w_qkv.shape[2]
    hidden_local = w_up.shape[1]
    heads_local = local_width // HEAD_DIM
    scale = 1.0 / math.sqrt(HEAD_DIM)
    first_head = place * heads_local
    slopes = jnp.exp2(
        -8.0
        * ((first_head + jnp.arange(heads_local, dtype=jnp.int32)).astype(jnp.float32) + 1.0)
        / HEADS
    )
    weight_qkv = w_qkv.reshape(width, 3 * local_width)
    qkv_shift = jnp.concatenate(
        [
            qv_bias[0].astype(jnp.float32),
            jnp.zeros((local_width,), jnp.float32),
            qv_bias[1].astype(jnp.float32),
        ]
    )
    gain_one = ln1_gain.astype(jnp.float32)
    shift_one = ln1_bias.astype(jnp.float32)
    gain_two = ln2_gain.astype(jnp.float32)
    shift_two = ln2_bias.astype(jnp.float32)
    out_shift = bias_out.astype(jnp.float32)
    up_shift = b_up.astype(jnp.float32)
    down_shift = b_down.astype(jnp.float32)
    grad_qkv = jnp.zeros((width, 3 * local_width), jnp.float32)
    grad_qvb = jnp.zeros((2, local_width), jnp.float32)
    grad_wout = jnp.zeros((local_width, width), jnp.float32)
    grad_wup = jnp.zeros((width, hidden_local), jnp.float32)
    grad_bup = jnp.zeros((hidden_local,), jnp.float32)
    grad_wdown = jnp.zeros((hidden_local, width), jnp.float32)
    grad_gain_one = jnp.zeros((width,), jnp.float32)
    grad_shift_one = jnp.zeros((width,), jnp.float32)
    grad_gain_two = jnp.zeros((width,), jnp.float32)
    grad_shift_two = jnp.zeros((width,), jnp.float32)
    grad_out_shift = jnp.zeros((width,), jnp.float32)
    grad_down_shift = jnp.zeros((width,), jnp.float32)
    output_rows = []
    input_rows = []
    for index in range(batches):
        tokens_f = tokens[index].astype(jnp.float32)
        length = lengths[index]
        normal_one, inverse_one = norm_parts(tokens_f)
        normed_one = (normal_one * gain_one + shift_one).astype(jnp.bfloat16)
        projected = (matmul(normed_one, weight_qkv) + qkv_shift).astype(jnp.bfloat16)
        query = projected[:, :local_width].reshape(slots, heads_local, HEAD_DIM)
        keys = projected[:, local_width : 2 * local_width].reshape(slots, heads_local, HEAD_DIM)
        values = projected[:, 2 * local_width :].reshape(slots, heads_local, HEAD_DIM)
        attn = attention_forward(query, keys, values, length, slopes, scale)
        partial_value = matmul(attn, w_out)
        summed = lax.psum(partial_value.astype(jnp.bfloat16), "tensor").astype(jnp.float32)
        hidden_full = tokens_f + summed + out_shift
        normal_full, inverse_full = norm_parts(hidden_full)
        normed_two = (normal_full * gain_two + shift_two).astype(jnp.bfloat16)
        hidden_rows = lax.dynamic_slice_in_dim(hidden_full, row_start, share, 0)
        normal_two = lax.dynamic_slice_in_dim(normal_full, row_start, share, 0)
        inverse_two = lax.dynamic_slice_in_dim(inverse_full, row_start, share, 0)
        pre = matmul(normed_two, w_up) + up_shift
        act_value, act_slope = gelu_parts(pre)
        act = act_value.astype(jnp.bfloat16)
        mlp_part = lax.psum_scatter(
            matmul(act, w_down).astype(jnp.bfloat16), "tensor", scatter_dimension=0, tiled=True
        ).astype(jnp.float32)
        output_rows.append((hidden_rows + mlp_part + down_shift).astype(jnp.bfloat16))
        valid = (jnp.arange(slots, dtype=jnp.int32) < length).astype(jnp.float32)[:, None]
        grad_out = d_output[index].astype(jnp.float32) * valid
        grad_two = grad_out.astype(jnp.bfloat16)
        grad_wdown = grad_wdown + contract_rows(act, grad_two)
        grad_pre = (contract_cols(grad_two, w_down) * act_slope).astype(jnp.bfloat16)
        grad_wup = grad_wup + contract_rows(normed_two, grad_pre)
        grad_bup = grad_bup + jnp.sum(grad_pre.astype(jnp.float32), 0)
        grad_norm_two = lax.psum_scatter(
            contract_cols(grad_pre, w_up).astype(jnp.bfloat16),
            "tensor",
            scatter_dimension=0,
            tiled=True,
        ).astype(jnp.float32)
        grad_gain_two = grad_gain_two + jnp.sum(grad_norm_two * normal_two, 0)
        grad_shift_two = grad_shift_two + jnp.sum(grad_norm_two, 0)
        grad_out_rows = lax.dynamic_slice_in_dim(grad_out, row_start, share, 0)
        grad_hidden_rows = grad_out_rows + norm_backward(
            grad_norm_two, normal_two, inverse_two, gain_two
        )
        grad_one_rows = grad_hidden_rows.astype(jnp.bfloat16)
        grad_down_shift = grad_down_shift + jnp.sum(
            lax.dynamic_slice_in_dim(grad_two, row_start, share, 0).astype(jnp.float32), 0
        )
        grad_out_shift = grad_out_shift + jnp.sum(grad_one_rows.astype(jnp.float32), 0)
        grad_one = lax.all_gather(grad_one_rows, "tensor", axis=0, tiled=True)
        grad_wout = grad_wout + contract_rows(attn, grad_one)
        grad_attn = (
            contract_cols(grad_one, w_out)
            .astype(jnp.bfloat16)
            .reshape(slots, heads_local, HEAD_DIM)
        )
        grad_query, grad_keys, grad_values = attention_backward(
            query, keys, values, grad_attn, length, slopes, scale
        )
        grad_proj = jnp.concatenate([grad_query, grad_keys, grad_values], 1)
        grad_qkv = grad_qkv + contract_rows(normed_one, grad_proj)
        grad_qvb = grad_qvb + jnp.stack(
            [
                jnp.sum(grad_query.astype(jnp.float32), 0),
                jnp.sum(grad_values.astype(jnp.float32), 0),
            ],
            0,
        )
        grad_norm_one = lax.psum_scatter(
            contract_cols(grad_proj, weight_qkv).astype(jnp.bfloat16),
            "tensor",
            scatter_dimension=0,
            tiled=True,
        ).astype(jnp.float32)
        normal_one_rows = lax.dynamic_slice_in_dim(normal_one, row_start, share, 0)
        inverse_one_rows = lax.dynamic_slice_in_dim(inverse_one, row_start, share, 0)
        grad_gain_one = grad_gain_one + jnp.sum(grad_norm_one * normal_one_rows, 0)
        grad_shift_one = grad_shift_one + jnp.sum(grad_norm_one, 0)
        input_rows.append(
            (
                grad_hidden_rows
                + norm_backward(grad_norm_one, normal_one_rows, inverse_one_rows, gain_one)
            ).astype(jnp.bfloat16)
        )
    grad_qkv, grad_qvb, grad_wout, grad_wup, grad_bup, grad_wdown = (
        lax.psum(grad_qkv.astype(jnp.bfloat16), "dp").astype(jnp.float32),
        lax.psum(grad_qvb.astype(jnp.bfloat16), "dp").astype(jnp.float32),
        lax.psum(grad_wout.astype(jnp.bfloat16), "dp").astype(jnp.float32),
        lax.psum(grad_wup.astype(jnp.bfloat16), "dp").astype(jnp.float32),
        lax.psum(grad_bup.astype(jnp.bfloat16), "dp").astype(jnp.float32),
        lax.psum(grad_wdown.astype(jnp.bfloat16), "dp").astype(jnp.float32),
    )
    (
        grad_gain_one,
        grad_shift_one,
        grad_gain_two,
        grad_shift_two,
        grad_out_shift,
        grad_down_shift,
    ) = lax.psum(
        (
            grad_gain_one,
            grad_shift_one,
            grad_gain_two,
            grad_shift_two,
            grad_out_shift,
            grad_down_shift,
        ),
        ("dp", "tensor"),
    )
    return (
        jnp.stack(output_rows, 0),
        jnp.stack(input_rows, 0),
        grad_gain_one,
        grad_shift_one,
        grad_qkv.reshape(width, 3, local_width),
        grad_qvb,
        grad_wout,
        grad_out_shift,
        grad_gain_two,
        grad_shift_two,
        grad_wup,
        grad_bup,
        grad_wdown,
        grad_down_shift,
    )


def solution(mesh):
    whole = mesh.shape["tensor"] == 2 and mesh.shape["dp"] == 2 * len(RING)
    return jax.shard_map(
        whole_sequence if whole else on_device,
        mesh=mesh,
        in_specs=(
            P("dp", None, None),
            P("dp", None, None),
            P("dp"),
            P(),
            P(),
            P(None, None, "tensor"),
            P(None, "tensor"),
            P("tensor", None),
            P(),
            P(),
            P(),
            P(None, "tensor"),
            P("tensor"),
            P("tensor", None),
            P(),
        ),
        out_specs=(
            P("dp", "tensor", None),
            P("dp", "tensor", None),
            P(),
            P(),
            P(None, None, "tensor"),
            P(None, "tensor"),
            P("tensor", None),
            P(),
            P(),
            P(),
            P(None, "tensor"),
            P("tensor"),
            P("tensor", None),
            P(),
        ),
        check_vma=False,
    )
```

```python
import functools
import math

import jax
import jax.numpy as jnp
import numpy as np
from jax import lax
from jax.experimental import pallas as pl
from jax.experimental.pallas import tpu as pltpu
from jax.sharding import PartitionSpec as P

HEADS = 16
HEAD_DIM = 64


epsilon = 1e-05
root_two_pi = math.sqrt(2.0 / math.pi)
masked_score = -1e30


def matmul(left, right):
    return jnp.dot(left, right, preferred_element_type=jnp.float32)


def contract_rows(left, right):
    return lax.dot_general(
        left, right, (((0,), (0,)), ((), ())), preferred_element_type=jnp.float32
    )


def contract_cols(left, right):
    return lax.dot_general(
        left, right, (((1,), (1,)), ((), ())), preferred_element_type=jnp.float32
    )


def norm_parts(values):
    centre = jnp.mean(values, -1, keepdims=True)
    shifted = values - centre
    inverse = lax.rsqrt(jnp.mean(shifted * shifted, -1, keepdims=True) + epsilon)
    return (shifted * inverse, inverse)


def norm_backward(grad_normed, normal, inverse, gain):
    scaled = grad_normed * gain
    return inverse * (
        scaled
        - jnp.mean(scaled, -1, keepdims=True)
        - normal * jnp.mean(scaled * normal, -1, keepdims=True)
    )


def gelu_parts(pre):
    tangent = jnp.tanh(root_two_pi * (pre + 0.044715 * pre * pre * pre))
    value = 0.5 * pre * (1.0 + tangent)
    slope = 0.5 * (1.0 + tangent) + 0.5 * pre * (1.0 - tangent * tangent) * root_two_pi * (
        1.0 + 3.0 * 0.044715 * pre * pre
    )
    return (value, slope)


def block_probs(query_rows, key_rows, start, length, slopes, scale):
    rows = query_rows.shape[0]
    cols = key_rows.shape[0]
    products = jnp.einsum("ihd,jhd->hij", query_rows, key_rows, preferred_element_type=jnp.float32)
    key_place = jnp.arange(cols, dtype=jnp.int32)
    distance = (start + jnp.arange(rows, dtype=jnp.int32))[:, None] - key_place[None, :]
    scores = products * scale - slopes[:, None, None] * distance.astype(jnp.float32)[None]
    allowed = (distance >= 0) & (key_place[None, :] < length)
    masked = jnp.where(allowed[None], scores, masked_score)
    highest = jnp.max(masked, -1, keepdims=True)
    exponent = jnp.exp(masked - highest)
    return exponent / jnp.sum(exponent, -1, keepdims=True)


def attention_forward(query, keys, values, length, slopes, scale):
    slots = query.shape[0]
    block = min(512, slots)
    outputs = []
    for number in range(slots // block):
        start = number * block
        probs = block_probs(query[start : start + block], keys, start, length, slopes, scale)
        mixed = jnp.einsum(
            "hij,jhd->ihd", probs.astype(jnp.bfloat16), values, preferred_element_type=jnp.float32
        )
        outputs.append(mixed.reshape(block, -1).astype(jnp.bfloat16))
    return jnp.concatenate(outputs, 0)


def attention_backward(query, keys, values, grad_attn, length, slopes, scale):
    slots, heads_local, head_width = query.shape
    block = min(512, slots)
    grad_keys = jnp.zeros((slots, heads_local, head_width), jnp.float32)
    grad_values = jnp.zeros((slots, heads_local, head_width), jnp.float32)
    query_parts = []
    for number in range(slots // block):
        start = number * block
        query_rows = query[start : start + block]
        grad_rows = grad_attn[start : start + block]
        probs = block_probs(query_rows, keys, start, length, slopes, scale)
        grad_probs = jnp.einsum(
            "ihd,jhd->hij", grad_rows, values, preferred_element_type=jnp.float32
        )
        delta = jnp.sum(probs * grad_probs, -1, keepdims=True)
        grad_scores = (probs * (grad_probs - delta)).astype(jnp.bfloat16)
        part_query = (
            jnp.einsum("hij,jhd->ihd", grad_scores, keys, preferred_element_type=jnp.float32)
            * scale
        )
        part_keys = (
            jnp.einsum("hij,ihd->jhd", grad_scores, query_rows, preferred_element_type=jnp.float32)
            * scale
        )
        part_values = jnp.einsum(
            "hij,ihd->jhd",
            probs.astype(jnp.bfloat16),
            grad_rows,
            preferred_element_type=jnp.float32,
        )
        part_query, part_keys, part_values = (part_query, part_keys, part_values)
        query_parts.append(part_query)
        grad_keys = grad_keys.at[:slots].add(part_keys)
        grad_values = grad_values.at[:slots].add(part_values)
    grad_query = jnp.concatenate(query_parts, 0).reshape(slots, -1).astype(jnp.bfloat16)
    return (
        grad_query,
        grad_keys.reshape(slots, -1).astype(jnp.bfloat16),
        grad_values.reshape(slots, -1).astype(jnp.bfloat16),
    )


QUERY_BLOCK = 256
KEY_BLOCK = 1024
PAIR = 128
NT = (((1,), (1,)), ((), ()))
TN = (((0,), (0,)), ((), ()))


def mm(left, right, dims=(((1,), (0,)), ((), ()))):
    return lax.dot_general(left, right, dims, preferred_element_type=jnp.float32)


def low_lanes(rows):
    return lax.broadcasted_iota(jnp.int32, (rows, PAIR), 1) < HEAD_DIM


def slope_rows():
    table = np.zeros((HEADS // 2, 8, PAIR), np.float64)
    for head in range(HEADS):
        rest = np.float64(np.float32(2.0 ** (-8.0 * (head + 1) / HEADS)))
        base = HEAD_DIM * (1 - head % 2)
        for part in range(3):
            piece = np.float64(np.asarray(rest).astype(jnp.bfloat16))
            rest = rest - piece
            table[head // 2, head % 2, base + part] = 32.0 * piece
            table[head // 2, head % 2, base + 3 + part] = piece
        table[head // 2, head % 2, base + 6] = 1.0
    return table.astype(jnp.bfloat16)


def key_lanes(slots, length):
    place = jnp.arange(slots, dtype=jnp.int32)[:, None]
    lane = jnp.arange(PAIR, dtype=jnp.int32)[None, :] % HEAD_DIM
    high = (place // 32).astype(jnp.float32)
    low = (place % 32).astype(jnp.float32)
    mask = jnp.where(place < length, 0.0, masked_score)
    return jnp.where(
        lane < 3, high, jnp.where(lane < 6, low, jnp.where(lane == 6, mask, 0.0))
    ).astype(jnp.bfloat16)


def forward_kernel(
    q_ref, k_ref, v_ref, lanes_ref, rows_ref, o_ref, level_ref, key0, key1, val0, val1
):
    slots = q_ref.shape[0]
    block = QUERY_BLOCK
    low = low_lanes(slots)
    zero = jnp.zeros((slots, PAIR), jnp.bfloat16)
    one = jnp.ones((slots, PAIR), jnp.bfloat16)
    key0[...] = jnp.where(low, k_ref[...], lanes_ref[...])
    key1[...] = jnp.where(low, lanes_ref[...], k_ref[...])
    val0[:, :PAIR] = jnp.where(low, v_ref[...], zero)
    val0[:, PAIR:] = jnp.where(low, one, zero)
    val1[:, :PAIR] = jnp.where(low, zero, v_ref[...])
    val1[:, PAIR:] = jnp.where(low, zero, one)
    low_block = low_lanes(block)
    causal = lax.broadcasted_iota(jnp.int32, (block, block), 1) <= lax.broadcasted_iota(
        jnp.int32, (block, block), 0
    )
    for number in range(slots // block):
        start = number * block
        rows = q_ref[start : start + block, :] * jnp.bfloat16(0.125)
        total = None
        tops = []
        for head, (key, val) in enumerate(((key0, val0), (key1, val1))):
            extra = jnp.broadcast_to(rows_ref[0, head : head + 1, :], (block, PAIR))
            query = jnp.where(low_block, rows, extra) if head == 0 else jnp.where(
                low_block, extra, rows
            )
            own = jnp.where(causal, mm(query, key[start : start + block, :], NT), masked_score)
            highest = jnp.max(own, 1, keepdims=True)
            if start:
                past = mm(query, key[:start, :], NT)
                highest = jnp.maximum(highest, jnp.max(past, 1, keepdims=True))
                part = mm(jnp.exp(past - highest).astype(jnp.bfloat16), val[:start, :])
                total = part if total is None else total + part
            part = mm(jnp.exp(own - highest).astype(jnp.bfloat16), val[start : start + block, :])
            total = part if total is None else total + part
            tops.append(highest)
        o_ref[start : start + block, :] = (total[:, :PAIR] / total[:, PAIR:]).astype(jnp.bfloat16)
        level = (jnp.where(low_block, tops[0], tops[1]) + jnp.log(total[:, PAIR:])).T
        level_ref[0, 0:1, start : start + block] = level[0:1, :]
        level_ref[0, 1:2, start : start + block] = level[HEAD_DIM : HEAD_DIM + 1, :]


def backward_kernel(
    q_ref, k_ref, v_ref, o_ref, g_ref, level_ref, lanes_ref, rows_ref, dq_ref, dk_ref, dv_ref,
    key0, key1, val0, val1, bare0, bare1, total_k, total_v,
):
    slots = q_ref.shape[0]
    block = QUERY_BLOCK
    piece = KEY_BLOCK
    low = low_lanes(slots)
    zero = jnp.zeros((slots, PAIR), jnp.bfloat16)
    key0[...] = jnp.where(low, k_ref[...], lanes_ref[...])
    key1[...] = jnp.where(low, lanes_ref[...], k_ref[...])
    bare0[...] = jnp.where(low, k_ref[...], zero)
    bare1[...] = jnp.where(low, zero, k_ref[...])
    val0[...] = jnp.where(low, v_ref[...], zero)
    val1[...] = jnp.where(low, zero, v_ref[...])
    low_block = low_lanes(block)
    nil = jnp.zeros((block, PAIR), jnp.bfloat16)
    causal = lax.broadcasted_iota(jnp.int32, (block, block), 0) <= lax.broadcasted_iota(
        jnp.int32, (block, block), 1
    )
    for number in reversed(range(slots // block)):
        start = number * block
        stop = start + block
        rows = q_ref[start:stop, :] * jnp.bfloat16(0.125)
        grad = g_ref[start:stop, :]
        shares = (grad.astype(jnp.float32) * o_ref[start:stop, :].astype(jnp.float32)).T
        deltas = [
            jnp.sum(shares[head * HEAD_DIM : (head + 1) * HEAD_DIM, :], 0, keepdims=True)
            for head in range(2)
        ]
        levels = [level_ref[0, head : head + 1, start:stop] for head in range(2)]
        extras = [jnp.broadcast_to(rows_ref[0, h : h + 1, :], (block, PAIR)) for h in range(2)]
        queries = (
            jnp.where(low_block, rows, extras[0]),
            jnp.where(low_block, extras[1], rows),
        )
        grads = jnp.concatenate(
            [jnp.where(low_block, grad, nil), jnp.where(low_block, nil, grad)], 0
        )
        both = jnp.concatenate(
            [jnp.where(low_block, rows, nil), jnp.where(low_block, nil, rows)], 0
        )
        grad_query = None
        for begin in range(0, stop, min(piece, stop)):
            end = min(begin + piece, stop)
            probs, scores = [], []
            for head, (key, val, bare) in enumerate(((key0, val0, bare0), (key1, val1, bare1))):
                score = mm(key[begin:end, :], queries[head], NT)
                if end > start:
                    own = jnp.where(causal, score[start - begin :], masked_score)
                    score = jnp.concatenate([score[: start - begin], own], 0) if start > begin else own
                prob = jnp.exp(score - levels[head])
                grad_prob = mm(val[begin:end, :], grad, NT)
                grad_score = (prob * (grad_prob - deltas[head])).astype(jnp.bfloat16)
                probs.append(prob.astype(jnp.bfloat16))
                scores.append(grad_score)
                part = mm(grad_score, bare[begin:end, :], TN)
                grad_query = part if grad_query is None else grad_query + part
            part_v = mm(jnp.concatenate(probs, 1), grads)
            part_k = mm(jnp.concatenate(scores, 1), both)
            if stop == slots:
                total_v[begin:end, :] = part_v
                total_k[begin:end, :] = part_k
            else:
                total_v[begin:end, :] += part_v
                total_k[begin:end, :] += part_k
        dq_ref[start:stop, :] = (grad_query * 0.125).astype(jnp.bfloat16)
    dk_ref[...] = total_k[...].astype(jnp.bfloat16)
    dv_ref[...] = total_v[...].astype(jnp.bfloat16)


def pair_specs(slots):
    part = pl.BlockSpec((slots, PAIR), lambda pair: (0, pair))
    lanes = pl.BlockSpec((slots, PAIR), lambda pair: (0, 0))
    rows = pl.BlockSpec((1, 8, PAIR), lambda pair: (pair, 0, 0))
    levels = pl.BlockSpec((1, 8, slots), lambda pair: (pair, 0, 0))
    return part, lanes, rows, levels


def attention_out(query, keys, values, lanes, rows):
    slots, columns = query.shape
    part, lane_spec, row_spec, level_spec = pair_specs(slots)
    pairs = columns // PAIR
    half = slots * slots * PAIR * pairs
    return pl.pallas_call(
        forward_kernel,
        grid=(pairs,),
        out_shape=(
            jax.ShapeDtypeStruct((slots, columns), jnp.bfloat16),
            jax.ShapeDtypeStruct((pairs, 8, slots), jnp.float32),
        ),
        in_specs=[part, part, part, lane_spec, row_spec],
        out_specs=(part, level_spec),
        scratch_shapes=[pltpu.VMEM((slots, PAIR), jnp.bfloat16)] * 2
        + [pltpu.VMEM((slots, 2 * PAIR), jnp.bfloat16)] * 2,
        cost_estimate=pl.CostEstimate(
            flops=8 * half, bytes_accessed=8 * slots * columns, transcendentals=slots * slots * pairs
        ),
        name="attention_out",
    )(query, keys, values, lanes, rows)


def attention_grads(query, keys, values, mixed, levels, grad, lanes, rows):
    slots, columns = query.shape
    part, lane_spec, row_spec, level_spec = pair_specs(slots)
    pairs = columns // PAIR
    half = slots * slots * PAIR * pairs
    shape = jax.ShapeDtypeStruct((slots, columns), jnp.bfloat16)
    return pl.pallas_call(
        backward_kernel,
        grid=(pairs,),
        out_shape=(shape, shape, shape),
        in_specs=[part, part, part, part, part, level_spec, lane_spec, row_spec],
        out_specs=(part, part, part),
        scratch_shapes=[pltpu.VMEM((slots, PAIR), jnp.bfloat16)] * 6
        + [pltpu.VMEM((slots, PAIR), jnp.float32)] * 2,
        cost_estimate=pl.CostEstimate(
            flops=20 * half,
            bytes_accessed=14 * slots * columns,
            transcendentals=slots * slots * pairs,
        ),
        name="attention_grads",
    )(query, keys, values, mixed, grad, levels, lanes, rows)


ROW_BLOCK = 512
PART = 256


def whole_spec(array):
    zeros = (0,) * array.ndim
    return pl.BlockSpec(array.shape, lambda *_: zeros)


def row_spec(columns):
    return pl.BlockSpec((ROW_BLOCK, columns), lambda row, *_: (row, 0))


def own_spec(columns):
    return pl.BlockSpec((1, ROW_BLOCK, columns), lambda row, facts: (facts[0], row, 0))


def over_rows(kernel, slots, facts, inputs, outputs, flops):
    arrays, in_specs = zip(*inputs)
    shapes, out_specs = zip(*outputs)
    return pl.pallas_call(
        kernel,
        grid_spec=pltpu.PrefetchScalarGridSpec(
            num_scalar_prefetch=1,
            grid=(slots // ROW_BLOCK,),
            in_specs=list(in_specs),
            out_specs=list(out_specs),
        ),
        out_shape=list(shapes),
        cost_estimate=pl.CostEstimate(
            flops=flops,
            bytes_accessed=sum(array.size * array.dtype.itemsize for array in arrays),
            transcendentals=0,
        ),
    )(facts, *arrays)


def parts():
    return [pl.ds(start, PART) for start in range(0, ROW_BLOCK, PART)]


def project_kernel(facts, tok_ref, gain_ref, shift_ref, w_ref, bias_ref, *refs):
    norm_ref, q_ref, k_ref, v_ref = refs[-4:]
    for at in parts():
        normal, _ = norm_parts(tok_ref[0, at, :].astype(jnp.float32))
        normed = (normal * gain_ref[...] + shift_ref[...]).astype(jnp.bfloat16)
        norm_ref[at, :] = normed
        q_ref[at, :] = (mm(normed, w_ref[0]) + bias_ref[0:1, :]).astype(jnp.bfloat16)
        k_ref[at, :] = mm(normed, w_ref[1]).astype(jnp.bfloat16)
        v_ref[at, :] = (mm(normed, w_ref[2]) + bias_ref[1:2, :]).astype(jnp.bfloat16)


def hidden_kernel(
    facts, tok_ref, a0_ref, a1_ref, w0_ref, w1_ref, bias_ref, gain_ref, shift_ref, hid_ref, norm_ref
):
    for at in parts():
        hidden = tok_ref[0, at, :].astype(jnp.float32) + bias_ref[...]
        hidden = hidden + mm(a0_ref[at, :], w0_ref[...]) + mm(a1_ref[at, :], w1_ref[...])
        hid_ref[at, :] = hidden
        normal, _ = norm_parts(hidden)
        norm_ref[at, :] = (normal * gain_ref[...] + shift_ref[...]).astype(jnp.bfloat16)


def act_parts(pre):
    square = pre * pre
    first = root_two_pi * pre * (1.0 + 0.044715 * square)
    half = 0.5 + 0.5 * jnp.tanh(first)
    value = pre * half
    steep = (2.0 * root_two_pi) + (6.0 * 0.044715 * root_two_pi) * square
    return value, half + value * (1.0 - half) * steep


def act_kernel(norm_ref, w_ref, bias_ref, act_ref, slope_ref):
    def rows(number, carry):
        at = pl.ds(pl.multiple_of(number * PART, PART), PART)
        value, slope = act_parts(mm(norm_ref[at, :], w_ref[...]) + bias_ref[...])
        act_ref[at, :] = value.astype(jnp.bfloat16)
        slope_ref[at, :] = slope.astype(jnp.bfloat16)
        return carry

    lax.fori_loop(0, norm_ref.shape[0] // PART, rows, 0, unroll=True)


def activations(normed, weight, bias):
    slots, width = normed.shape
    hidden = weight.shape[1]
    columns = 512
    out = pl.BlockSpec((slots, columns), lambda col: (0, col))
    shape = jax.ShapeDtypeStruct((slots, hidden), jnp.bfloat16)
    return pl.pallas_call(
        act_kernel,
        grid=(hidden // columns,),
        in_specs=[
            whole_spec(normed),
            pl.BlockSpec((width, columns), lambda col: (0, col)),
            pl.BlockSpec((1, columns), lambda col: (0, col)),
        ],
        out_specs=(out, out),
        out_shape=(shape, shape),
        cost_estimate=pl.CostEstimate(
            flops=2 * slots * width * hidden,
            bytes_accessed=8 * slots * hidden,
            transcendentals=slots * hidden,
        ),
        name="activations",
    )(normed, weight, bias)


def output_kernel(facts, hid_ref, a0_ref, a1_ref, w0_ref, w1_ref, bias_ref, tie_ref, out_ref):
    for at in parts():
        total = hid_ref[at, :] + bias_ref[...] + mm(a0_ref[at, :], w0_ref[...])
        out_ref[at, :] = (total + mm(a1_ref[at, :], w1_ref[...])).astype(jnp.bfloat16)


def clear_sums(*refs):
    @pl.when(pl.program_id(0) == 0)
    def _():
        for ref in refs:
            ref[...] = jnp.zeros_like(ref)


def add_sums(sums_ref, rows):
    for index, value in enumerate(rows):
        sums_ref[index : index + 1, :] += jnp.sum(value, 0, keepdims=True)


def hidden_grad_kernel(
    facts, g0_ref, g1_ref, w0_ref, w1_ref, hid_ref, gain_ref, dout_ref, grad_ref, one_ref, sums_ref
):
    clear_sums(sums_ref)
    for at in parts():
        grad_norm = mm(g0_ref[at, :], w0_ref[...], NT) + mm(g1_ref[at, :], w1_ref[...], NT)
        normal, inverse = norm_parts(hid_ref[at, :])
        first = pl.program_id(0) * ROW_BLOCK + at.start
        place = lax.broadcasted_iota(jnp.int32, grad_norm.shape, 0) + first
        grad_out = jnp.where(place < facts[1], dout_ref[0, at, :].astype(jnp.float32), 0.0)
        grad = grad_out + norm_backward(grad_norm, normal, inverse, gain_ref[...])
        one = grad.astype(jnp.bfloat16)
        grad_ref[at, :] = grad
        one_ref[at, :] = one
        add_sums(sums_ref, [grad_norm * normal, grad_norm, one.astype(jnp.float32), grad_out])


def token_grad_kernel(
    facts, q0_ref, k0_ref, v0_ref, q1_ref, k1_ref, v1_ref, w0_ref, w1_ref, tok_ref, grad_ref,
    gain_ref, *refs,
):
    out_ref, sums_ref, heads_ref = refs[-3:]
    clear_sums(sums_ref, heads_ref)
    halves = (((q0_ref, k0_ref, v0_ref), w0_ref), ((q1_ref, k1_ref, v1_ref), w1_ref))
    for at in parts():
        grad_norm = None
        for sources, weight in halves:
            for part, ref in enumerate(sources):
                more = mm(ref[at, :], weight[part], NT)
                grad_norm = more if grad_norm is None else grad_norm + more
        normal, inverse = norm_parts(tok_ref[0, at, :].astype(jnp.float32))
        grad = grad_ref[at, :] + norm_backward(grad_norm, normal, inverse, gain_ref[...])
        out_ref[at, :] = grad.astype(jnp.bfloat16)
        add_sums(sums_ref, [grad_norm * normal, grad_norm])
        heads = [ref[at, :].astype(jnp.float32) for ref in (q0_ref, q1_ref, v0_ref, v1_ref)]
        add_sums(heads_ref, heads)


RING = ((0, 0), (1, 0), (2, 0), (3, 0), (3, 1), (2, 1), (1, 1), (0, 1))


def device_of(z, y, core):
    return (z * 2 + y) * 2 + core


def to_tensor(value):
    return lax.ppermute(value, "tensor", [(0, 1), (1, 0)])


def to_core(value):
    return lax.ppermute(value, "dp", [(i, i ^ 1) for i in range(2 * len(RING))])


def rows_at(value, start, size):
    return lax.dynamic_slice_in_dim(value, start, size, value.ndim - 2)


def after(value, *earlier):
    return lax.optimization_barrier((value, *earlier))[0]


def piece(weight, index, pieces):
    size = weight.shape[-2] // pieces
    return rows_at(weight, index * size, size)


def both_cores(value, core, axis):
    beside = to_core(value)
    first = jnp.where(core == 0, value, beside)
    second = jnp.where(core == 0, beside, value)
    return jnp.concatenate([first, second], axis)


class Ring:
    def __init__(self, values, slots, sums, results, sems, cuts):
        self.values, self.slots, self.sums, self.results = values, slots, sums, results
        self.send_sems, self.recv_sems, self.swap_send_sems, self.swap_recv_sems = sems
        self.cuts = cuts
        self.count = count = len(RING)
        self.device = device = lax.axis_index("dp")
        self.core, self.y, self.z = lax.rem(device, 2), lax.rem(device // 2, 2), device // 4
        self.place = place = self.z * (1 - self.y) + (count - 1 - self.z) * self.y
        self.nexts = tuple(
            self.at_place(lax.rem(place + step, count)) for step in (1, count - 1)
        )
        self.partner = {"dp": device + 1 - 2 * self.core}
        self.streams = [
            (array, way, cut)
            for cut in range(cuts)
            for array in range(len(values))
            for way in range(2)
        ]

    def at_place(self, where):
        side = where // 4
        return {
            "dp": device_of(where * (1 - side) + (self.count - 1 - where) * side, side, self.core)
        }

    def greet(self, others=()):
        barrier = pltpu.get_barrier_semaphore()
        greeted = [*self.nexts, self.partner, *others]
        for target in greeted:
            pl.semaphore_signal(
                barrier, inc=1, device_id=target, device_id_type=pl.DeviceIdType.MESH
            )
        pl.semaphore_wait(barrier, len(greeted))

    def block(self, way, offset):
        return lax.rem(self.place - (1, -1)[way] * offset + 2 * self.count, self.count)

    def rows(self, array, cut):
        size = self.values[array].shape[2] // self.cuts
        return pl.ds(cut * size, size)

    def result(self, stream, step):
        array, way, cut = stream
        return self.results[array].at[
            self.core, way, self.block(way, step), self.rows(array, cut)
        ]

    def copy(self, stream, step):
        array, way, cut = stream
        rows = self.rows(array, cut)
        if step < self.count - 1:
            target = self.slots[array].at[way, step, rows]
            if step:
                source = self.sums[array].at[way, step - 1, rows]
            else:
                source = self.values[array].at[way, self.block(way, 0), rows]
        else:
            source = target = self.result(stream, step)
        index = self.streams.index(stream)
        return pltpu.make_async_remote_copy(
            src_ref=source,
            dst_ref=target,
            send_sem=self.send_sems.at[index, step],
            recv_sem=self.recv_sems.at[index, step],
            device_id=self.nexts[way],
            device_id_type=pl.DeviceIdType.MESH,
        )

    def swap(self, stream, step):
        index = self.streams.index(stream)
        turn = step - self.count + 1
        done = self.result(stream, step)
        return pltpu.make_async_remote_copy(
            src_ref=done,
            dst_ref=done,
            send_sem=self.swap_send_sems.at[index, turn],
            recv_sem=self.swap_recv_sems.at[index, turn],
            device_id=self.partner,
            device_id_type=pl.DeviceIdType.MESH,
        )

    def first(self):
        for stream in self.streams:
            self.copy(stream, 0).start()

    def hop(self, step):
        count = self.count
        for stream in self.streams:
            array, way, cut = stream
            rows = self.rows(array, cut)
            self.copy(stream, step - 1).wait_recv()
            if step < count:
                total = self.values[array][way, self.block(way, step), rows].astype(jnp.float32)
                total = total + self.slots[array][way, step - 1, rows].astype(jnp.float32)
                total = total.astype(jnp.bfloat16)
                if step < count - 1:
                    self.sums[array][way, step - 1, rows] = total
                else:
                    self.results[array][self.core, way, self.block(way, step), rows] = total
            self.copy(stream, step).start()
            if step >= count - 1:
                self.swap(stream, step).start()

    def last(self):
        for stream in self.streams:
            self.copy(stream, 2 * self.count - 3).wait_recv()
            self.swap(stream, 2 * self.count - 2).start()

    def drain(self):
        for stream in self.streams:
            for step in range(2 * self.count - 2):
                self.copy(stream, step).wait_send()
            for step in range(self.count - 1, 2 * self.count - 1):
                self.swap(stream, step).wait()


def ring_shape(value):
    count = len(RING)
    return value.reshape(2, count, value.shape[0] // (2 * count), value.shape[1])


def ring_scratch(shaped, cuts):
    count = len(RING)
    streams = 2 * len(shaped) * cuts
    scratch = [pltpu.VMEM((2, count - 1, *value.shape[2:]), value.dtype) for value in shaped]
    scratch += [pltpu.VMEM((2, count - 2, *value.shape[2:]), value.dtype) for value in shaped]
    scratch += [pltpu.SemaphoreType.DMA((streams, 2 * count - 2))] * 2
    return scratch + [pltpu.SemaphoreType.DMA((streams, count))] * 2


def ring_kernel(blocks, cuts, has_small, has_tie, has_swap, *refs):
    values, refs = refs[:blocks], refs[blocks:]
    if has_small:
        small_ref, refs = refs[0], refs[1:]
    refs = refs[has_tie:]
    if has_swap:
        lone_ref, refs = refs[0], refs[1:]
    results, refs = refs[:blocks], refs[blocks:]
    if has_small:
        small_out, refs = refs[0], refs[1:]
    if has_swap:
        lone_out, refs = refs[0], refs[1:]
    slots, refs = refs[:blocks], refs[blocks:]
    sums, refs = refs[:blocks], refs[blocks:]
    ring = Ring(values, slots, sums, results, refs[:4], cuts)
    refs = refs[4:]
    if has_small:
        small_slots, small_sums, small_send_sems, small_recv_sems = refs[:4]
        refs = refs[4:]
        device, y, z = ring.device, ring.y, ring.z
        small_targets = [
            ring.partner,
            {"tensor": 1 - lax.axis_index("tensor")},
            {"dp": device + 2 - 4 * y},
            {"dp": device + 4 - 8 * lax.rem(z, 2)},
            {"dp": device + 8 - 16 * (z // 2)},
        ]
        ring.greet(small_targets[1:])
    else:
        ring.greet()

    def exchange(turn):
        return pltpu.make_async_remote_copy(
            src_ref=small_ref if turn == 0 else small_sums.at[turn - 1],
            dst_ref=small_slots.at[turn],
            send_sem=small_send_sems.at[turn],
            recv_sem=small_recv_sems.at[turn],
            device_id=small_targets[turn],
            device_id_type=pl.DeviceIdType.MESH,
        )

    def take_exchange(turn):
        exchange(turn).wait_recv()
        total = (small_ref[...] if turn == 0 else small_sums[turn - 1]) + small_slots[turn]
        if turn == len(small_targets) - 1:
            small_out[...] = total
        else:
            small_sums[turn] = total
            exchange(turn + 1).start()

    ring.first()
    if has_small:
        exchange(0).start()
    if has_swap:
        lone_send_sem, lone_recv_sem = refs
        lone = pltpu.make_async_remote_copy(
            src_ref=lone_ref,
            dst_ref=lone_out.at[ring.core],
            send_sem=lone_send_sem,
            recv_sem=lone_recv_sem,
            device_id=ring.partner,
            device_id_type=pl.DeviceIdType.MESH,
        )
        lone.start()
        lone_out[ring.core] = lone_ref[...]
    for step in range(1, 2 * ring.count - 2):
        if has_small and step % 2 == 0 and step // 2 <= len(small_targets):
            take_exchange(step // 2 - 1)
        ring.hop(step)
    ring.last()
    ring.drain()
    if has_swap:
        lone.wait()
    if has_small:
        for turn in range(len(small_targets)):
            exchange(turn).wait_send()


def plane_sums(values, identity, small=None, tie=None, lone=None, cuts=1):
    blocks = len(values)
    shaped = [ring_shape(value) for value in values]
    size = sum(value.size for value in values)
    vmem = pl.BlockSpec(memory_space=pltpu.VMEM)
    inputs, in_specs = list(shaped), [vmem] * blocks
    shapes = [jax.ShapeDtypeStruct((2, *value.shape), value.dtype) for value in shaped]
    scratch = ring_scratch(shaped, cuts)
    if small is not None:
        inputs.append(small)
        in_specs.append(vmem)
        shapes.append(jax.ShapeDtypeStruct(small.shape, small.dtype))
        scratch += [pltpu.VMEM((5, *small.shape), small.dtype)] * 2
        scratch += [pltpu.SemaphoreType.DMA((5,))] * 2
    if tie is not None:
        inputs.append(tie)
        in_specs.append(pl.BlockSpec(memory_space=pl.ANY))
    if lone is not None:
        inputs.append(lone)
        in_specs.append(vmem)
        shapes.append(jax.ShapeDtypeStruct((2, *lone.shape), lone.dtype))
        scratch += [pltpu.SemaphoreType.DMA] * 2
    flags = (small is not None, int(tie is not None), lone is not None)
    results = pl.pallas_call(
        functools.partial(ring_kernel, blocks, cuts, *flags),
        out_shape=shapes,
        in_specs=in_specs,
        out_specs=[vmem] * len(shapes),
        scratch_shapes=scratch,
        compiler_params=pltpu.CompilerParams(collective_id=identity, has_side_effects=True),
        cost_estimate=pl.CostEstimate(flops=size, bytes_accessed=6 * size, transcendentals=0),
        name="plane_sums",
    )(*inputs)
    sums = [
        result.reshape(2 * value.shape[0], value.shape[1]) for result, value in zip(results, values)
    ]
    return [*sums, *results[blocks:]]


def core_send(left, rights, core):
    half = left.shape[1] // 2
    part = lax.dynamic_slice_in_dim(left, (1 - core) * half, half, 1)
    sent = [contract_rows(part, right).astype(jnp.bfloat16) for right in rights]
    return sent, [to_core(value) for value in sent]


def core_sum(left, rights, arrived, core):
    half = left.shape[1] // 2
    kept = lax.dynamic_slice_in_dim(left, core * half, half, 1)
    return [
        contract_rows(kept, right) + part.astype(jnp.float32)
        for right, part in zip(rights, arrived)
    ]


def start_grad(left, rights, core):
    _, other = core_send(left[1], rights[1], core)
    sent, local = core_send(left[0], rights[0], core)
    summed = [part.astype(jnp.bfloat16) for part in core_sum(left[1], rights[1], other, core)]
    return local, [to_tensor(part) for part in summed], summed + sent


def pair_grad(left, rights, local, passed, core, *earlier):
    passed = [after(part, *earlier) for part in passed]
    return [
        (part + more.astype(jnp.float32)).astype(jnp.bfloat16)
        for part, more in zip(core_sum(left, rights, local, core), passed)
    ]


def trade_rows(value, own, *earlier):
    share = value.shape[0] // 2
    arrived = to_tensor(lax.dynamic_slice_in_dim(value, (1 - own) * share, share, 0))
    arrived = after(arrived, *earlier) if earlier else arrived
    kept = lax.dynamic_slice_in_dim(value, own * share, share, 0)
    return jnp.stack(
        [jnp.where(own == 0, kept, arrived), jnp.where(own == 0, arrived, kept)], 0
    )


def whole_sequence(*operands):
    return layer(*operands)


def layer(
    tokens,
    d_output,
    lengths,
    ln1_gain,
    ln1_bias,
    w_qkv,
    qv_bias,
    w_out,
    bias_out,
    ln2_gain,
    ln2_bias,
    w_up,
    b_up,
    w_down,
    b_down,
):
    own = lax.axis_index("tensor")
    device = lax.axis_index("dp")
    core = device % 2
    slots, width = tokens.shape[1:]
    local_width = w_qkv.shape[2]
    hidden_local = w_up.shape[1]
    table = jnp.asarray(slope_rows())
    pairs = local_width // PAIR
    f32 = jnp.float32

    weight_qkv = w_qkv.transpose(1, 0, 2)
    biases = jnp.concatenate([qv_bias.reshape(-1), b_up])
    other_biases = to_tensor(biases)
    piece_up, piece_qkv = piece(w_up, device, 2 * len(RING)), piece(weight_qkv, core, 2)
    far_up = to_tensor(piece_up)
    far_qkv = to_tensor(piece_qkv)
    qv = [b[: 2 * local_width].reshape(2, local_width).astype(f32) for b in (biases, other_biases)]
    ups = [b[2 * local_width :].astype(f32)[None] for b in (biases, other_biases)]
    rows = [lax.dynamic_slice_in_dim(table, index * pairs, pairs, 0) for index in (own, 1 - own)]
    gain_one, shift_one = ln1_gain.astype(f32)[None], ln1_bias.astype(f32)[None]
    gain_two, shift_two = ln2_gain.astype(f32)[None], ln2_bias.astype(f32)[None]

    length = lax.dynamic_index_in_dim(lengths, own, 0, keepdims=False)
    facts = jnp.stack([own.astype(jnp.int32), length])
    lanes = key_lanes(slots, length)
    low = jnp.bfloat16

    def run(kernel, inputs, outputs, flops):
        return over_rows(kernel, slots, facts, inputs, outputs, flops)

    def fixed(array):
        return array, whole_spec(array)

    def tied(array):
        return array, pl.BlockSpec(memory_space=pl.ANY)

    def by_row(array):
        return array, row_spec(array.shape[1])

    def rows_out(columns, dtype):
        return jax.ShapeDtypeStruct((slots, columns), dtype), row_spec(columns)

    def sums_out(columns):
        shape = jax.ShapeDtypeStruct((8, columns), f32)
        return shape, whole_spec(shape)

    square = 2 * slots * width
    tokens_in, d_output_in = (tokens, own_spec(width)), (d_output, own_spec(width))
    normed_one, *local_heads = run(
        project_kernel,
        [tokens_in, fixed(gain_one), fixed(shift_one), fixed(weight_qkv), fixed(qv[0])]
        + [tied(piece_up), tied(piece_qkv)],
        [rows_out(width, low)] + [rows_out(local_width, low)] * 3,
        3 * square * local_width,
    )
    attn, level = attention_out(*local_heads, lanes, rows[0])
    heads, mixed, levels = [tuple(local_heads)], [attn], [level]
    far_out = to_tensor(after(piece(w_out, core, 2), normed_one))
    far_down = to_tensor(after(piece(w_down, device, 2 * len(RING)), normed_one))
    up = (w_up, lax.all_gather(after(far_up, normed_one), "dp", axis=0, tiled=True))
    qkv = (weight_qkv, both_cores(after(far_qkv, attn), core, 1))
    query = (matmul(normed_one, qkv[1][0]) + qv[1][0]).astype(low)
    keys = matmul(normed_one, qkv[1][1]).astype(low)
    values = (matmul(normed_one, qkv[1][2]) + qv[1][1]).astype(low)
    heads.append((query, keys, values))
    out = (w_out, both_cores(after(far_out, keys), core, 0))
    attn, level = attention_out(query, keys, values, lanes, rows[1])
    mixed.append(attn)
    levels.append(level)
    down = (w_down, lax.all_gather(after(far_down, attn), "dp", axis=0, tiled=True))
    hidden, normed_two = run(
        hidden_kernel,
        [tokens_in, by_row(mixed[0]), by_row(mixed[1]), fixed(out[0]), fixed(out[1])]
        + [fixed(bias_out.astype(f32)[None]), fixed(gain_two), fixed(shift_two)],
        [rows_out(width, f32), rows_out(width, low)],
        2 * square * local_width,
    )
    acts = [activations(normed_two, up[0], ups[0])]
    up = (up[0], after(up[1], acts[0][0]))
    acts.append(activations(normed_two, up[1], ups[1]))

    valid = (jnp.arange(slots, dtype=jnp.int32) < length).astype(f32)[:, None]
    grad_out = lax.dynamic_index_in_dim(d_output, own, 0, keepdims=False).astype(f32) * valid
    grad_two = grad_out.astype(low)
    left_down, right_down = (acts[0][0], acts[1][0]), ([grad_two], [grad_two])
    local_down, passed_down, sent = start_grad(left_down, right_down, core)
    late_two = after(grad_two, *sent)

    bias_up = []

    def pre_grad(weight, slope):
        value = (contract_cols(late_two, weight) * slope.astype(f32)).astype(low)
        bias_up.append(jnp.sum(value.astype(f32), 0))
        return value

    grad_pre = [pre_grad(down[0], acts[0][1])]
    down = (down[0], after(down[1], grad_pre[0]))
    grad_pre.append(pre_grad(down[1], acts[1][1]))
    left_up, right_up = (normed_two, normed_two), ([grad_pre[0]], [grad_pre[1]])
    local_up, passed_up, sent = start_grad(left_up, right_up, core)
    late_pre = lax.optimization_barrier((*grad_pre, *sent))
    (mine_down,) = pair_grad(
        left_down[0], right_down[0], local_down, passed_down, core, *sent
    )
    planes = [list(range(core_at, 2 * len(RING), 2)) for core_at in range(2)]
    sum_down = lax.psum(mine_down, "dp", axis_index_groups=planes)
    grad_hidden, grad_one, sums_two = run(
        hidden_grad_kernel,
        [by_row(late_pre[0]), by_row(late_pre[1]), fixed(up[0]), fixed(up[1]), by_row(hidden)]
        + [fixed(gain_two), d_output_in],
        [rows_out(width, f32), rows_out(width, low), sums_out(width)],
        2 * square * hidden_local,
    )
    left_out, right_out = (mixed[0], mixed[1]), ([grad_one], [grad_one])
    local_out, passed_out, sent = start_grad(left_out, right_out, core)
    (result,) = run(
        output_kernel,
        [by_row(hidden), by_row(acts[0][0]), by_row(acts[1][0]), fixed(down[0]), fixed(down[1])]
        + [fixed(b_down.astype(f32)[None]), tied(sent[0])],
        [rows_out(width, low)],
        2 * square * hidden_local,
    )
    late_one = after(grad_one, *sent, result)
    grads = [None, None]
    grad_attn = contract_cols(late_one, out[1]).astype(low)
    grads[1] = attention_grads(*heads[1], mixed[1], levels[1], grad_attn, lanes, rows[1])
    _, other_qkv = core_send(normed_one, grads[1], core)
    sent_qkv = [part.astype(low) for part in core_sum(normed_one, grads[1], other_qkv, core)]
    passed_qkv = [to_tensor(part) for part in sent_qkv]
    later_one = after(late_one, *sent_qkv)
    grad_attn = contract_cols(later_one, out[0]).astype(low)
    grads[0] = attention_grads(*heads[0], mixed[0], levels[0], grad_attn, lanes, rows[0])
    sent, local_qkv = core_send(normed_one, grads[0], core)
    grad_tokens, sums_one, sums_heads = run(
        token_grad_kernel,
        [by_row(part) for part in (*grads[0], *grads[1])]
        + [fixed(qkv[0]), fixed(qkv[1]), tokens_in, by_row(grad_hidden), fixed(gain_one)]
        + [tied(part) for part in sent],
        [rows_out(width, low), sums_out(width), sums_out(local_width)],
        6 * square * local_width,
    )
    done = grad_tokens
    output, grad_tokens = trade_rows(result, own, done), trade_rows(grad_tokens, own)

    def in_place(first, second):
        return jnp.concatenate(
            [jnp.where(own == 0, first, second), jnp.where(own == 0, second, first)], 0
        )

    small = jnp.concatenate(
        [
            sums_one[:2],
            sums_two[:4],
            in_place(sums_heads[0], sums_heads[1]).reshape(1, width),
            in_place(sums_heads[2], sums_heads[3]).reshape(1, width),
            in_place(*bias_up).reshape(-1, width),
        ],
        0,
    )
    small = jnp.pad(small, ((0, 16 - small.shape[0]), (0, 0)))
    mine = [
        *pair_grad(left_up[0], right_up[0], local_up, passed_up, core, done),
        *pair_grad(left_out[0], right_out[0], local_out, passed_out, core, done),
        *pair_grad(normed_one, grads[0], local_qkv, passed_qkv, core, done),
    ]
    grad_wup, grad_wout, *grad_wqkv, small, grad_wdown = plane_sums(mine, 1, small, lone=sum_down)
    grad_wdown = grad_wdown.reshape(2 * grad_wdown.shape[1], width)
    grad_wqkv = jnp.stack(grad_wqkv, 0).astype(f32)
    wide = [lax.dynamic_slice_in_dim(small[i], own * local_width, local_width, 0) for i in (6, 7)]
    grad_bup = lax.dynamic_slice_in_dim(
        small[8:12].reshape(-1), own * hidden_local, hidden_local, 0
    )
    return (
        output,
        grad_tokens,
        small[0],
        small[1],
        grad_wqkv.transpose(1, 0, 2),
        jnp.stack(wide, 0),
        grad_wout.astype(f32),
        small[4],
        small[2],
        small[3],
        grad_wup.astype(f32),
        grad_bup,
        grad_wdown.astype(f32),
        small[5],
    )


def on_device(
    tokens,
    d_output,
    lengths,
    ln1_gain,
    ln1_bias,
    w_qkv,
    qv_bias,
    w_out,
    bias_out,
    ln2_gain,
    ln2_bias,
    w_up,
    b_up,
    w_down,
    b_down,
):
    parts = lax.axis_size("tensor")
    place = lax.axis_index("tensor")
    batches, slots, width = tokens.shape
    share = slots // parts
    row_start = place * share
    local_width = w_qkv.shape[2]
    hidden_local = w_up.shape[1]
    heads_local = local_width // HEAD_DIM
    scale = 1.0 / math.sqrt(HEAD_DIM)
    first_head = place * heads_local
    slopes = jnp.exp2(
        -8.0
        * ((first_head + jnp.arange(heads_local, dtype=jnp.int32)).astype(jnp.float32) + 1.0)
        / HEADS
    )
    weight_qkv = w_qkv.reshape(width, 3 * local_width)
    qkv_shift = jnp.concatenate(
        [
            qv_bias[0].astype(jnp.float32),
            jnp.zeros((local_width,), jnp.float32),
            qv_bias[1].astype(jnp.float32),
        ]
    )
    gain_one = ln1_gain.astype(jnp.float32)
    shift_one = ln1_bias.astype(jnp.float32)
    gain_two = ln2_gain.astype(jnp.float32)
    shift_two = ln2_bias.astype(jnp.float32)
    out_shift = bias_out.astype(jnp.float32)
    up_shift = b_up.astype(jnp.float32)
    down_shift = b_down.astype(jnp.float32)
    grad_qkv = jnp.zeros((width, 3 * local_width), jnp.float32)
    grad_qvb = jnp.zeros((2, local_width), jnp.float32)
    grad_wout = jnp.zeros((local_width, width), jnp.float32)
    grad_wup = jnp.zeros((width, hidden_local), jnp.float32)
    grad_bup = jnp.zeros((hidden_local,), jnp.float32)
    grad_wdown = jnp.zeros((hidden_local, width), jnp.float32)
    grad_gain_one = jnp.zeros((width,), jnp.float32)
    grad_shift_one = jnp.zeros((width,), jnp.float32)
    grad_gain_two = jnp.zeros((width,), jnp.float32)
    grad_shift_two = jnp.zeros((width,), jnp.float32)
    grad_out_shift = jnp.zeros((width,), jnp.float32)
    grad_down_shift = jnp.zeros((width,), jnp.float32)
    output_rows = []
    input_rows = []
    for index in range(batches):
        tokens_f = tokens[index].astype(jnp.float32)
        length = lengths[index]
        normal_one, inverse_one = norm_parts(tokens_f)
        normed_one = (normal_one * gain_one + shift_one).astype(jnp.bfloat16)
        projected = (matmul(normed_one, weight_qkv) + qkv_shift).astype(jnp.bfloat16)
        query = projected[:, :local_width].reshape(slots, heads_local, HEAD_DIM)
        keys = projected[:, local_width : 2 * local_width].reshape(slots, heads_local, HEAD_DIM)
        values = projected[:, 2 * local_width :].reshape(slots, heads_local, HEAD_DIM)
        attn = attention_forward(query, keys, values, length, slopes, scale)
        partial_value = matmul(attn, w_out)
        summed = lax.psum(partial_value.astype(jnp.bfloat16), "tensor").astype(jnp.float32)
        hidden_full = tokens_f + summed + out_shift
        normal_full, inverse_full = norm_parts(hidden_full)
        normed_two = (normal_full * gain_two + shift_two).astype(jnp.bfloat16)
        hidden_rows = lax.dynamic_slice_in_dim(hidden_full, row_start, share, 0)
        normal_two = lax.dynamic_slice_in_dim(normal_full, row_start, share, 0)
        inverse_two = lax.dynamic_slice_in_dim(inverse_full, row_start, share, 0)
        pre = matmul(normed_two, w_up) + up_shift
        act_value, act_slope = gelu_parts(pre)
        act = act_value.astype(jnp.bfloat16)
        mlp_part = lax.psum_scatter(
            matmul(act, w_down).astype(jnp.bfloat16), "tensor", scatter_dimension=0, tiled=True
        ).astype(jnp.float32)
        output_rows.append((hidden_rows + mlp_part + down_shift).astype(jnp.bfloat16))
        valid = (jnp.arange(slots, dtype=jnp.int32) < length).astype(jnp.float32)[:, None]
        grad_out = d_output[index].astype(jnp.float32) * valid
        grad_two = grad_out.astype(jnp.bfloat16)
        grad_wdown = grad_wdown + contract_rows(act, grad_two)
        grad_pre = (contract_cols(grad_two, w_down) * act_slope).astype(jnp.bfloat16)
        grad_wup = grad_wup + contract_rows(normed_two, grad_pre)
        grad_bup = grad_bup + jnp.sum(grad_pre.astype(jnp.float32), 0)
        grad_norm_two = lax.psum_scatter(
            contract_cols(grad_pre, w_up).astype(jnp.bfloat16),
            "tensor",
            scatter_dimension=0,
            tiled=True,
        ).astype(jnp.float32)
        grad_gain_two = grad_gain_two + jnp.sum(grad_norm_two * normal_two, 0)
        grad_shift_two = grad_shift_two + jnp.sum(grad_norm_two, 0)
        grad_out_rows = lax.dynamic_slice_in_dim(grad_out, row_start, share, 0)
        grad_hidden_rows = grad_out_rows + norm_backward(
            grad_norm_two, normal_two, inverse_two, gain_two
        )
        grad_one_rows = grad_hidden_rows.astype(jnp.bfloat16)
        grad_down_shift = grad_down_shift + jnp.sum(
            lax.dynamic_slice_in_dim(grad_two, row_start, share, 0).astype(jnp.float32), 0
        )
        grad_out_shift = grad_out_shift + jnp.sum(grad_one_rows.astype(jnp.float32), 0)
        grad_one = lax.all_gather(grad_one_rows, "tensor", axis=0, tiled=True)
        grad_wout = grad_wout + contract_rows(attn, grad_one)
        grad_attn = (
            contract_cols(grad_one, w_out)
            .astype(jnp.bfloat16)
            .reshape(slots, heads_local, HEAD_DIM)
        )
        grad_query, grad_keys, grad_values = attention_backward(
            query, keys, values, grad_attn, length, slopes, scale
        )
        grad_proj = jnp.concatenate([grad_query, grad_keys, grad_values], 1)
        grad_qkv = grad_qkv + contract_rows(normed_one, grad_proj)
        grad_qvb = grad_qvb + jnp.stack(
            [
                jnp.sum(grad_query.astype(jnp.float32), 0),
                jnp.sum(grad_values.astype(jnp.float32), 0),
            ],
            0,
        )
        grad_norm_one = lax.psum_scatter(
            contract_cols(grad_proj, weight_qkv).astype(jnp.bfloat16),
            "tensor",
            scatter_dimension=0,
            tiled=True,
        ).astype(jnp.float32)
        normal_one_rows = lax.dynamic_slice_in_dim(normal_one, row_start, share, 0)
        inverse_one_rows = lax.dynamic_slice_in_dim(inverse_one, row_start, share, 0)
        grad_gain_one = grad_gain_one + jnp.sum(grad_norm_one * normal_one_rows, 0)
        grad_shift_one = grad_shift_one + jnp.sum(grad_norm_one, 0)
        input_rows.append(
            (
                grad_hidden_rows
                + norm_backward(grad_norm_one, normal_one_rows, inverse_one_rows, gain_one)
            ).astype(jnp.bfloat16)
        )
    grad_qkv, grad_qvb, grad_wout, grad_wup, grad_bup, grad_wdown = (
        lax.psum(grad_qkv.astype(jnp.bfloat16), "dp").astype(jnp.float32),
        lax.psum(grad_qvb.astype(jnp.bfloat16), "dp").astype(jnp.float32),
        lax.psum(grad_wout.astype(jnp.bfloat16), "dp").astype(jnp.float32),
        lax.psum(grad_wup.astype(jnp.bfloat16), "dp").astype(jnp.float32),
        lax.psum(grad_bup.astype(jnp.bfloat16), "dp").astype(jnp.float32),
        lax.psum(grad_wdown.astype(jnp.bfloat16), "dp").astype(jnp.float32),
    )
    (
        grad_gain_one,
        grad_shift_one,
        grad_gain_two,
        grad_shift_two,
        grad_out_shift,
        grad_down_shift,
    ) = lax.psum(
        (
            grad_gain_one,
            grad_shift_one,
            grad_gain_two,
            grad_shift_two,
            grad_out_shift,
            grad_down_shift,
        ),
        ("dp", "tensor"),
    )
    return (
        jnp.stack(output_rows, 0),
        jnp.stack(input_rows, 0),
        grad_gain_one,
        grad_shift_one,
        grad_qkv.reshape(width, 3, local_width),
        grad_qvb,
        grad_wout,
        grad_out_shift,
        grad_gain_two,
        grad_shift_two,
        grad_wup,
        grad_bup,
        grad_wdown,
        grad_down_shift,
    )


def solution(mesh):
    whole = mesh.shape["tensor"] == 2 and mesh.shape["dp"] == 2 * len(RING)
    return jax.shard_map(
        whole_sequence if whole else on_device,
        mesh=mesh,
        in_specs=(
            P("dp", None, None),
            P("dp", None, None),
            P("dp"),
            P(),
            P(),
            P(None, None, "tensor"),
            P(None, "tensor"),
            P("tensor", None),
            P(),
            P(),
            P(),
            P(None, "tensor"),
            P("tensor"),
            P("tensor", None),
            P(),
        ),
        out_specs=(
            P("dp", "tensor", None),
            P("dp", "tensor", None),
            P(),
            P(),
            P(None, None, "tensor"),
            P(None, "tensor"),
            P("tensor", None),
            P(),
            P(),
            P(),
            P(None, "tensor"),
            P("tensor"),
            P("tensor", None),
            P(),
        ),
        check_vma=False,
    )
```
